32 devices in a mesh: row: 2 (over y), col: 4 (over z), layer: 4 (over x, core).
Axes of the slice: x: 2, y: 2, z: 4, core: 2. Of those that a mesh axis runs over, the one named last changes fastest.
Arguments:
- integrals: bfloat16 [64, 1024, 768], P('layer', 'col', 'row'), may hold values from -0.0234375 to 0.0234375
- amplitudes: bfloat16 [64, 1024, 512], P('layer', 'row', 'col'), may hold values from -6 to 6
- coulomb: bfloat16 [768, 512], P(('row', 'layer'), 'col'), may hold values from -6 to 6
- row_gap: float32 [768], P(('row', 'layer')), may hold values from 0.5 to 4
- col_gap: float32 [512], P('col'), may hold values from 0.5 to 4
Outputs:
- residual: float32 [768, 512], P(('row', 'layer'), 'col')
The draws below stay inside these ranges and needn't reach their ends.
All inputs are finite; a program needn't handle non-finite values.
Results may differ from the reference program's by a relative error of at most 0.0003.
Values may be sent and summed in bfloat16 or wider, within the bound.
A program may use at most 64 MiB of HBM per device.

```python
import math
import jax
import jax.numpy as jnp

OCC = 64
VIR = 1024
NROW = 768
NCOL = 512


def levels(own_key, shape, split, low, top_value):
    def one(dim, blocks):
        heights = jax.random.uniform(jax.random.fold_in(jax.random.fold_in(own_key, 6), dim), (blocks,), jnp.float32, low / len(split), top_value / len(split))
        return jnp.repeat(jnp.exp(heights), shape[dim] // blocks).reshape((-1,) + (1,) * (len(shape) - dim - 1))

    gain = one(*split[0])
    for cut in split[1:]:
        gain = gain * one(*cut)
    return gain


def scatter_about(key, dims, deviation, bound, cuts=(), dtype=jnp.bfloat16):
    factor_of = levels(key, dims, cuts, -0.22, 0.18) if cuts else 1.0
    entries = jax.random.normal(key, dims, jnp.float32) * deviation * factor_of
    return jnp.minimum(jnp.maximum(entries, -bound), bound).astype(dtype)


def setup_inputs(seed: int = 0) -> dict:
    key_of = jax.random.split(jax.random.key(seed), 6)
    return {
        "integrals": scatter_about(key_of[0], (OCC, VIR, NROW), (OCC * VIR) ** -0.5, 0.0234375, ((0, 4), (1, 4), (2, 2))),
        "amplitudes": scatter_about(key_of[1], (OCC, VIR, NCOL), 1.0, 6.0, ((0, 4), (1, 2), (2, 4))),
        "coulomb": scatter_about(key_of[2], (NROW, NCOL), 1.0, 6.0, ((0, 8), (1, 4))),
        "row_gap": jnp.clip(jnp.exp(math.log(4.0) - 2.0794415 * jax.random.uniform(key_of[3], (NROW,), jnp.float32) ** levels(key_of[3], (NROW,), ((0, 8),), -0.2, 0.2)), 0.5, 4.0),
        "col_gap": jnp.clip(jnp.exp(math.log(4.0) - 2.0794415 * jax.random.uniform(key_of[4], (NCOL,), jnp.float32) ** levels(key_of[4], (NCOL,), ((0, 4),), -0.2, 0.2)), 0.5, 4.0),
    }


def reference(integrals, amplitudes, coulomb, row_gap, col_gap):
    left_matrix = integrals.reshape(OCC * VIR, NROW)
    right_matrix = amplitudes.reshape(OCC * VIR, NCOL)
    product = jnp.dot(left_matrix.T, right_matrix, preferred_element_type=jnp.float32)
    gap_sum = row_gap[:, None] + col_gap[None, :]
    return (coulomb.astype(jnp.float32) + product) / gap_sum
```

```python
import functools

import jax
import jax.numpy as jnp
from jax import lax
from jax.experimental import pallas as pl
from jax.experimental.pallas import tpu as pltpu
from jax.sharding import PartitionSpec as P

MESH = pl.DeviceIdType.MESH


def hi_order(n):
    if n == 1:
        return [0]
    below = hi_order(n // 2)
    return [2 * x + 1 for x in below] + [2 * x for x in below]


def kernel(R, C, L, Q, i_ref, a_ref, o_ref,
           a_all, az, i_all, i_t, acc, lay_buf, row_buf, col_buf,
           asend, arecv, xsend, xrecv, zsend, zrecv,
           osend, orecv, lsend, lrecv, rsend, rrecv, csend, crecv):
    r, c, l = lax.axis_index("row"), lax.axis_index("col"), lax.axis_index("layer")
    K, V_row, N = a_ref.shape
    V, M = i_ref.shape[1:]
    Kr = K // R
    kc = Kr // Q
    m = C // R
    w = kc * V
    rows = M // L
    stages = L.bit_length() - 1
    late = M // 2 // 128 * 128 if stages == 2 and M % 128 == 0 else 0
    early = M - late
    top = l >> (stages - 1)

    def remote(src, dst, ss, rs, **to):
        where = {"row": r, "col": c, "layer": l}
        where.update(to)
        return pltpu.make_async_remote_copy(src_ref=src, dst_ref=dst, send_sem=ss, recv_sem=rs,
                                            device_id=where, device_id_type=MESH)

    def ks(q):
        return pl.ds(q * kc, kc)

    def far_row(d):
        return lax.rem(r + d, R)

    def near(dc):
        return lax.rem(c + dc + C, C)

    order = sorted(range(1, C), key=lambda d: -min(d, C - d))

    def slice_for(d, q):
        return pl.ds(far_row(d) * Kr + q * kc, kc)

    def own_a(q):
        return pltpu.make_async_copy(a_ref.at[slice_for(0, q)], a_all.at[0, ks(q)], arecv.at[0, q])

    def own_i(q):
        return pltpu.make_async_copy(i_ref.at[slice_for(0, q)], i_all.at[0, ks(q)], xrecv.at[0, q])

    for q in range(Q):
        own_a(q).start()
        own_i(q).start()

    barrier = pltpu.get_barrier_semaphore()
    partners = [{"row": far_row(d), "col": near(dc)} for d in range(R) for dc in range(C) if d or dc]
    partners += [{"layer": l ^ (1 << t)} for t in range(stages)]
    for p in partners:
        where = {"row": r, "col": c, "layer": l}
        where.update(p)
        pl.semaphore_signal(barrier, inc=1, device_id=where, device_id_type=MESH)
    pl.semaphore_wait(barrier, len(partners))

    def row_a(d, q):
        return remote(a_ref.at[slice_for(d, q)], a_all.at[R - d, ks(q)], asend.at[d, q], arecv.at[R - d, q], row=far_row(d))

    parts = [(0, early, (1 - top) * late)] + ([(early, late, top * early)] if late else [])

    def row_i(d, q, p):
        at, size, start = parts[p]
        src = i_ref.at[slice_for(d, q), :, pl.ds(pl.multiple_of(start, 128), size)] if late else i_ref.at[slice_for(d, q)]
        return remote(src, i_all.at[R - d, ks(q), :, pl.ds(at, size)], xsend.at[p * R + d, q], xrecv.at[p * R + R - d, q],
                      row=far_row(d))

    def col_a(d, j, q):
        b = far_row(d) * m + j
        at = pl.ds(j * V, V)
        src = a_all.at[d, ks(q), at] if d else a_ref.at[slice_for(0, q), at]
        return b, remote(src, az.at[c, ks(q)], zsend.at[d, j, q], zrecv.at[c, q], col=b)

    def col_start(d, q):
        for j in range(m):
            b, cp = col_a(d, j, q)

            @pl.when(b != c)
            def _():
                cp.start()

    for q in range(Q):
        for d in range(1, R):
            row_a(d, q).start()
        col_start(0, q)
    for p in range(len(parts)):
        for q in range(Q):
            for d in range(1, R):
                row_i(d, q, p).start()

    whole = (0, M, 0)

    def turn(d, q, part):
        first, size = part[:2]
        for k in range(kc):
            at = (q * kc + k) * V
            i_t[d, first:first + size, at:at + V] = i_all[d, q * kc + k, :, first:first + size].T

    def add(d, block, x, q, part):
        first, size, start = part
        piece = lax.dot_general(i_t[d, first:first + size, q * w:(q + 1) * w], x, (((1,), (0,)), ((), ())),
                                preferred_element_type=jnp.float32)
        to = pl.ds(start if isinstance(start, int) else pl.multiple_of(start, 128), size)
        if q == 0:
            acc[d, block, to] = piece
        else:
            acc[d, block, to] += piece

    own_row = lax.rem(lax.div(c, m) - r + R, R)
    own_at = pl.ds(pl.multiple_of(lax.rem(c, m) * V, V), V)

    def own_block(d, q, part):
        add(d, c, a_all[own_row, ks(q), own_at].reshape(w, N), q, part)

    for q in range(Q):
        own_a(q).wait()
        for d in range(1, R):
            row_a(R - d, q).wait_recv()
            col_start(d, q)
        own_i(q).wait()
        turn(0, q, whole)
        own_block(0, q, whole)

    for q in range(Q):
        for dc in order[::-1]:
            s = near(dc)
            here = az.at[s, ks(q)]
            remote(here, here, zsend.at[0, 0, q], zrecv.at[s, q], col=s).wait_recv()
            add(0, s, az[s, ks(q)].reshape(w, N), q, whole)

    def block(t, hi, bit):
        return (hi << (t + 1)) | (bit << t) | (l & ((1 << t) - 1))

    def halving(d, t, i, col):
        n = L >> (t + 1)
        hi = (l >> (t + 1)) ^ hi_order(n)[i]
        bit = (l >> t) & 1
        slot = n - 1 + hi
        give, keep = block(t, hi, 1 - bit), block(t, hi, bit)
        give, keep = (pl.ds(pl.multiple_of(b * rows, 8), rows) for b in (give, keep))
        if d == 0:
            cp = remote(acc.at[0, :, give], lay_buf.at[0, slot], osend.at[slot], orecv.at[slot], layer=l ^ (1 << t))
        else:
            cp = remote(acc.at[d, col, give], lay_buf.at[d, slot, col], lsend.at[d, slot, col], lrecv.at[d, slot, col],
                        layer=l ^ (1 << t))
        return cp, keep, slot

    def own_stage(t):
        for i in range(L >> (t + 1)):
            cp, keep, slot = halving(0, t, i, None)
            cp.wait_recv()
            acc[0, :, keep] += lay_buf[0, slot]
            if t + 1 < stages and i < L >> (t + 2):
                halving(0, t + 1, i, None)[0].start()

    for i in range(L >> 1):
        halving(0, 0, i, None)[0].start()

    c_order = [near(dc) for dc in order] + [c]
    mine = pl.ds(pl.multiple_of(l * rows, 8), rows)

    def first_stage_start(i):
        for d in range(1, R):
            for col in c_order:
                halving(d, 0, i, col)[0].start()

    def stage_end(t, i):
        for d in range(1, R):
            for col in c_order:
                cp, keep, slot = halving(d, t, i, col)
                cp.wait_recv()
                acc[d, col, keep] += lay_buf[d, slot, col]
                if t + 1 == stages:
                    row_sum(d, col).start()
                elif i < L >> (t + 2):
                    halving(d, t + 1, i, col)[0].start()

    for p, part in enumerate(parts):
        for q in range(Q):
            for d in range(1, R):
                row_i(R - d, q, p).wait_recv()
                turn(d, q, part)
                own_block(d, q, part)
                for dc in order:
                    s = near(dc)
                    add(d, s, az[s, ks(q)].reshape(w, N), q, part)
            if p == 0 and q == 0:
                own_stage(0)
            if p == 1 and q == min(1, Q - 1):
                stage_end(0, 0)
        if late:
            first_stage_start(p)

    def row_sum(d, col):
        return remote(acc.at[d, col, mine], row_buf.at[R - d, c], rsend.at[d, col], rrecv.at[R - d, c],
                      row=far_row(d), col=col)

    def col_sum(dc):
        return remote(acc.at[0, near(dc), mine], col_buf.at[c], csend.at[dc], crecv.at[c], col=near(dc))

    if not late:
        for i in range(L >> 1):
            first_stage_start(i)
    for t in range(1, stages):
        own_stage(t)
    for dc in order:
        col_sum(dc).start()
    for t in range(stages):
        for i in range(L >> (t + 1)):
            if not (late and t == 0 and i == 0):
                stage_end(t, i)
    total = acc[0, c, mine]
    for dc in order[::-1]:
        s = near(dc)
        remote(col_buf.at[s], col_buf.at[s], csend.at[dc], crecv.at[s], col=s).wait_recv()
        total += col_buf[s]
    for col in c_order[::-1]:
        for d in range(1, R):
            here = row_buf.at[d, col]
            remote(here, here, rsend.at[d, col], rrecv.at[d, col], row=far_row(d), col=col).wait_recv()
            total += row_buf[d, col]
    o_ref[...] = total

    for q in range(Q):
        for d in range(R):
            if d:
                row_a(d, q).wait_send()
                for p in range(len(parts)):
                    row_i(d, q, p).wait_send()
            for j in range(m):
                b, cp = col_a(d, j, q)

                @pl.when(b != c)
                def _():
                    cp.wait_send()
    for t in range(stages):
        for i in range(L >> (t + 1)):
            halving(0, t, i, None)[0].wait_send()
            for d in range(1, R):
                for col in c_order:
                    halving(d, t, i, col)[0].wait_send()
    for col in c_order:
        for d in range(1, R):
            row_sum(d, col).wait_send()
    for dc in order:
        col_sum(dc).wait_send()


def general_call(R, C, L, integrals, amplitudes):
    K, V, M = integrals.shape
    V_row, N = amplitudes.shape[1:]
    rows = M // L
    Kr = K // R
    Q = Kr
    m = C // R
    slots = L - 1
    dma = pltpu.SemaphoreType.DMA
    vmem = pl.BlockSpec(memory_space=pltpu.VMEM)
    anyspace = pl.BlockSpec(memory_space=pl.ANY)
    return pl.pallas_call(
        functools.partial(kernel, R, C, L, Q),
        out_shape=jax.ShapeDtypeStruct((rows, N), jnp.float32),
        in_specs=[anyspace, anyspace],
        out_specs=vmem,
        scratch_shapes=[
            pltpu.VMEM((R, Kr, V_row, N), jnp.bfloat16),
            pltpu.VMEM((C, Kr, V, N), jnp.bfloat16),
            pltpu.VMEM((R, Kr, V, M), jnp.bfloat16),
            pltpu.VMEM((R, M, Kr * V), jnp.bfloat16),
            pltpu.VMEM((R, C, M, N), jnp.float32),
            pltpu.VMEM((R, slots, C, rows, N), jnp.float32),
            pltpu.VMEM((R, C, rows, N), jnp.float32),
            pltpu.VMEM((C, rows, N), jnp.float32),
            dma((R, Q)), dma((R, Q)),
            dma((2 * R, Q)), dma((2 * R, Q)),
            dma((R, m, Q)), dma((C, Q)),
            dma((slots,)), dma((slots,)),
            dma((R, slots, C)), dma((R, slots, C)),
            dma((R, C)), dma((R, C)),
            dma((C,)), dma((C,)),
        ],
        compiler_params=pltpu.CompilerParams(collective_id=0, has_side_effects=True),
    )(integrals, amplitudes)


def swift(R, C, L, T, i_ref, a_ref, o_ref,
          a_x, az, i_in, i_s, i_t, acc, last, core_buf, x_buf, z_buf, y_out, y_buf, last_buf,
          own, iown, asend, arecv, isend, irecv, zsend, zrecv,
          csend, crecv, xsend, xrecv, wsend, wrecv, ysend, yrecv, lsend, lrecv, there):
    r, c, l = lax.axis_index("row"), lax.axis_index("col"), lax.axis_index("layer")
    K, V, M = i_ref.shape
    N = a_ref.shape[2]
    Kr = K // R
    W = Kr * V
    m = C // R
    rows = M // L
    half_rows = 2 * rows
    body = rows - T
    o = 1 - r
    x, core = lax.div(l, 2), lax.rem(l, 2)
    home = lax.div(c, m) == r

    def remote(src, dst, ss, rs, **to):
        where = {"row": r, "col": c, "layer": l}
        where.update(to)
        return pltpu.make_async_remote_copy(src_ref=src, dst_ref=dst, send_sem=ss, recv_sem=rs,
                                            device_id=where, device_id_type=MESH)

    def signal(sem, **to):
        where = {"row": r, "col": c, "layer": l}
        where.update(to)
        pl.semaphore_signal(sem, inc=1, device_id=where, device_id_type=MESH)

    def at(start, size, unit):
        return pl.ds(pl.multiple_of(start, unit), size)

    sib, opp = l ^ 1, l ^ 2

    def local_a(q):
        return pltpu.make_async_copy(a_ref.at[r * Kr + q, at(lax.rem(c, m) * V, V, V)], az.at[c, q], own.at[q])

    def cross_a(q):
        return pltpu.make_async_copy(a_x.at[q, at(lax.rem(c, m) * V, V, V)], az.at[c, q], own.at[q])

    def local_i(k):
        return pltpu.make_async_copy(i_ref.at[k], i_in.at[k], iown.at[k])

    barrier = pltpu.get_barrier_semaphore()
    signal(barrier, row=o)
    signal(barrier, layer=sib)
    signal(barrier, layer=opp)

    @pl.when(c > 0)
    def _():
        signal(barrier, col=c - 1)

    @pl.when(c < C - 1)
    def _():
        signal(barrier, col=c + 1)

    for k in range(Kr):
        local_i(o * Kr + k).start()
    for k in range(Kr):
        local_i(r * Kr + k).start()

    @pl.when(home)
    def _():
        for q in range(Kr):
            local_a(q).start()

    pl.semaphore_wait(barrier, 3 + (c > 0).astype(jnp.int32) + (c < C - 1).astype(jnp.int32))

    def row_a(q):
        return remote(a_ref.at[o * Kr + q], a_x.at[q], asend.at[q], arecv.at[q], row=o)

    for q in range(Kr):
        row_a(q).start()

    for t in range(2, C):
        @pl.when((c >= 1) & (c + t - 1 < C))
        def _():
            signal(there.at[0, t], col=c - 1)

        @pl.when((c + 1 < C) & (c - t + 1 >= 0))
        def _():
            signal(there.at[1, t], col=c + 1)

        @pl.when(c + t < C)
        def _():
            pl.semaphore_wait(there.at[0, t], 1)

        @pl.when(c - t >= 0)
        def _():
            pl.semaphore_wait(there.at[1, t], 1)

    def col_a(d, j, q):
        b = (o if d else r) * m + j
        span = pl.ds(j * V, V)
        src = a_x.at[q, span] if d else a_ref.at[r * Kr + q, span]
        return b, remote(src, az.at[c, q], zsend.at[d, j, q], zrecv.at[c, q], col=b)

    def col_start(d, q):
        for j in range(m):
            b, cp = col_a(d, j, q)

            @pl.when(b != c)
            def _():
                cp.start()

    ahead = 2
    for q in range(ahead):
        col_start(0, q)

    def turn(dst, k, kk):
        dst[:, kk * V:(kk + 1) * V] = i_in[k].T

    other = (1 - x) * half_rows
    mine = x * half_rows
    groups = [(other, rows), (other + rows, rows), (mine, body), (mine + rows, body),
              (mine + body, T), (mine + rows + body, T)]

    def row_i(g):
        start, size = groups[g]
        span = at(start, size, 16)
        return remote(i_s.at[span], i_t.at[1, span], isend.at[g], irecv.at[g], row=o)

    per = 2 * Kr // Kr
    for q in range(Kr):
        row_a(q).wait_recv()
        col_start(1, q)

        @pl.when(jnp.logical_not(home))
        def _():
            cross_a(q).start()

        if q + ahead < Kr:
            col_start(0, q + ahead)
        for kk in range(per * q, per * q + per):
            if kk < Kr:
                local_i(o * Kr + kk).wait()
                turn(i_s, o * Kr + kk, kk)
                if kk == Kr - 1:
                    for g in range(len(groups)):
                        row_i(g).start()
            else:
                local_i(r * Kr + kk - Kr).wait()
                turn(i_t.at[0], r * Kr + kk - Kr, kk - Kr)

    near, far = lax.div(c, m) * m, (1 - lax.div(c, m)) * m
    first = [near, far]

    def wait_piece(s):
        for q in range(Kr):
            @pl.when(s == c)
            def _():
                local_a(q).wait()

            @pl.when(s != c)
            def _():
                here = az.at[s, q]
                remote(here, here, zsend.at[0, 0, q], zrecv.at[s, q], col=s).wait_recv()

    def wide(h):
        return jnp.concatenate([az[first[h] + j].reshape(W, N) for j in range(m)], axis=1)

    def product(d, start, size, right):
        return lax.dot_general(i_t[d, at(start, size, 16)], right, (((1,), (0,)), ((), ())),
                               preferred_element_type=jnp.float32)

    def fill(d, h, start, size, right):
        piece = product(d, start, size, right)
        for j in range(m):
            acc[d, first[h] + j, at(start, size, 16)] = piece[:, j * N:(j + 1) * N]

    def pair(h):
        return pl.ds(first[h], m)

    def block(b, size=rows):
        return at(b * rows, size, 16)

    def core_copy(d, h, keep):
        xx = x if keep else 1 - x
        size = body if d and keep else rows
        give = block(2 * xx + 1 - core, size)
        return remote(acc.at[d, pair(h), give], core_buf.at[d, h, keep, :, pl.ds(0, size)],
                      csend.at[d, h, keep], crecv.at[d, h, keep], layer=sib)

    def core_end(d, h, keep):
        xx = x if keep else 1 - x
        size = body if d and keep else rows
        core_copy(d, h, keep).wait_recv()
        acc[d, pair(h), block(2 * xx + core, size)] += core_buf[d, h, keep, :, :size]

    def x_copy(d, h):
        return remote(acc.at[d, pair(h), block(2 * (1 - x) + core)], x_buf.at[d, h], xsend.at[d, h], xrecv.at[d, h], layer=opp)

    def x_end(d, h):
        x_copy(d, h).wait_recv()
        if d:
            acc[d, pair(h), block(l, body)] += x_buf[d, h, :, :body]
            acc[d, pair(h), at(l * rows + body, T, 16)] = x_buf[d, h, :, body:]
        else:
            acc[d, pair(h), block(l)] += x_buf[d, h]

    def z_copy(d, h, j):
        s = first[h] + j
        return s, remote(acc.at[d, s, block(l)], z_buf.at[d, c], wsend.at[d, h, j], wrecv.at[d, c], col=s)

    def z_start(d, h):
        for j in range(m):
            s, cp = z_copy(d, h, j)

            @pl.when(s != c)
            def _():
                cp.start()

    def z_end(d):
        total = acc[d, c, block(l)]
        for dc in range(1, C):
            s = lax.rem(c + dc, C)
            here = z_buf.at[d, s]
            remote(here, here, wsend.at[d, 0, 0], wrecv.at[d, s], col=s).wait_recv()
            total += z_buf[d, s]
        return total

    for j in range(m):
        wait_piece(near + j)
    right = wide(0)
    fill(0, 0, 0, M, right)
    core_copy(0, 0, 0).start()
    core_copy(0, 0, 1).start()
    core_end(0, 0, 0)
    x_copy(0, 0).start()
    core_end(0, 0, 1)

    for g in range(2):
        row_i(g).wait_recv()
    fill(1, 0, other, half_rows, right)
    core_copy(1, 0, 0).start()
    x_end(0, 0)
    z_start(0, 0)
    core_end(1, 0, 0)
    x_copy(1, 0).start()

    for j in range(m):
        wait_piece(far + j)
    right = wide(1)
    fill(0, 1, 0, M, right)
    core_copy(0, 1, 0).start()
    core_copy(0, 1, 1).start()
    fill(1, 1, other, half_rows, right)
    core_copy(1, 1, 0).start()
    core_end(0, 1, 0)
    x_copy(0, 1).start()
    core_end(1, 1, 0)
    x_copy(1, 1).start()
    core_end(0, 1, 1)

    for g in range(2, 4):
        row_i(g).wait_recv()
    for h in range(2):
        right = wide(h)
        for i in range(2):
            fill(1, h, mine + i * rows, body, right)
        core_copy(1, h, 1).start()
    x_end(0, 1)
    z_start(0, 1)
    for h in range(2):
        core_end(1, h, 1)

    def last_copy(i, s):
        return remote(last.at[i, s], last_buf.at[core, c], lsend.at[i, s], lrecv.at[core, c],
                      row=o, col=s, layer=2 * x + i)

    for g in range(4, 6):
        row_i(g).wait_recv()
    for h in range(2):
        right = wide(h)
        for i in range(2):
            piece = product(1, mine + i * rows + body, T, right)
            for j in range(m):
                last[i, first[h] + j] = piece[:, j * N:(j + 1) * N]
    for dc in range(C):
        for i in range(2):
            last_copy(i, c ^ (C - 1 - dc)).start()

    for h in range(2):
        x_end(1, h)
        z_start(1, h)
    total = z_end(0)
    y_out[...] = z_end(1)

    def y_copy():
        return remote(y_out, y_buf, ysend, yrecv, row=o)

    y_copy().start()
    tail = jnp.zeros((T, N), jnp.float32)
    for i in range(2):
        for dc in range(C):
            s = c ^ dc
            here = last_buf.at[i, s]
            remote(here, here, lsend.at[0, 0], lrecv.at[i, s], row=o, col=s, layer=2 * x + i).wait_recv()
            tail += last_buf[i, s]
    y_copy().wait_recv()
    total += y_buf[...]
    o_ref[:body] = total[:body]
    o_ref[body:] = total[body:] + tail

    for q in range(Kr):
        row_a(q).wait_send()
        for d in range(2):
            for j in range(m):
                b, cp = col_a(d, j, q)

                @pl.when(b != c)
                def _():
                    cp.wait_send()
    for g in range(len(groups)):
        row_i(g).wait_send()
    for d in range(2):
        for h in range(2):
            for keep in range(2):
                core_copy(d, h, keep).wait_send()
            x_copy(d, h).wait_send()
            for j in range(m):
                s, cp = z_copy(d, h, j)

                @pl.when(s != c)
                def _():
                    cp.wait_send()
    for s in range(C):
        for i in range(2):
            last_copy(i, s).wait_send()
    y_copy().wait_send()


def swift_call(R, C, L, integrals, amplitudes):
    K, V, M = integrals.shape
    V_row, N = amplitudes.shape[1:]
    rows = M // L
    Kr = K // R
    m = C // R
    T = 16
    dma = pltpu.SemaphoreType.DMA
    f32, bf16 = jnp.float32, jnp.bfloat16
    anyspace = pl.BlockSpec(memory_space=pl.ANY)
    return pl.pallas_call(
        functools.partial(swift, R, C, L, T),
        out_shape=jax.ShapeDtypeStruct((rows, N), f32),
        in_specs=[anyspace, anyspace],
        out_specs=pl.BlockSpec(memory_space=pltpu.VMEM),
        scratch_shapes=[
            pltpu.VMEM((Kr, V_row, N), bf16),
            pltpu.VMEM((C, Kr, V, N), bf16),
            pltpu.VMEM((K, V, M), bf16),
            pltpu.VMEM((M, Kr * V), bf16),
            pltpu.VMEM((2, M, Kr * V), bf16),
            pltpu.VMEM((2, C, M, N), f32),
            pltpu.VMEM((2, C, T, N), f32),
            pltpu.VMEM((2, 2, 2, m, rows, N), f32),
            pltpu.VMEM((2, 2, m, rows, N), f32),
            pltpu.VMEM((2, C, rows, N), f32),
            pltpu.VMEM((rows, N), f32),
            pltpu.VMEM((rows, N), f32),
            pltpu.VMEM((2, C, T, N), f32),
            dma((Kr,)), dma((K,)),
            dma((Kr,)), dma((Kr,)),
            dma((6,)), dma((6,)),
            dma((2, m, Kr)), dma((C, Kr)),
            dma((2, 2, 2)), dma((2, 2, 2)),
            dma((2, 2)), dma((2, 2)),
            dma((2, 2, m)), dma((2, C)),
            dma, dma,
            dma((2, C)), dma((2, C)),
            pltpu.SemaphoreType.REGULAR((2, C)),
        ],
        compiler_params=pltpu.CompilerParams(collective_id=0, has_side_effects=True),
    )(integrals, amplitudes)


def local(R, C, L, integrals, amplitudes, coulomb, row_gap, col_gap):
    swift_fits = R == 2 and C == 4 and L == 4 and integrals.shape[2] % (16 * L) == 0
    call = swift_call if swift_fits else general_call
    own_rows = call(R, C, L, integrals, amplitudes)
    gap_sum = row_gap[:, None] + col_gap[None, :]
    return (coulomb.astype(jnp.float32) + own_rows) / gap_sum


def solution(mesh):
    R, C, L = (mesh.shape[a] for a in ("row", "col", "layer"))
    placed = (
        P("layer", "col", "row"),
        P("layer", "row", "col"),
        P(("row", "layer"), "col"),
        P(("row", "layer")),
        P("col"),
    )
    return jax.shard_map(
        functools.partial(local, R, C, L), mesh=mesh, in_specs=placed, out_specs=P(("row", "layer"), "col"),
        check_vma=False,
    )
```

```python
import functools

import jax
import jax.numpy as jnp
from jax import lax
from jax.experimental import pallas as pl
from jax.experimental.pallas import tpu as pltpu
from jax.sharding import PartitionSpec as P

MESH = pl.DeviceIdType.MESH


def hi_order(n):
    if n == 1:
        return [0]
    below = hi_order(n // 2)
    return [2 * x + 1 for x in below] + [2 * x for x in below]


def kernel(R, C, L, Q, i_ref, a_ref, o_ref,
           a_all, az, i_all, i_t, acc, lay_buf, row_buf, col_buf,
           asend, arecv, xsend, xrecv, zsend, zrecv,
           osend, orecv, lsend, lrecv, rsend, rrecv, csend, crecv):
    r, c, l = lax.axis_index("row"), lax.axis_index("col"), lax.axis_index("layer")
    K, V_row, N = a_ref.shape
    V, M = i_ref.shape[1:]
    Kr = K // R
    kc = Kr // Q
    m = C // R
    w = kc * V
    rows = M // L
    stages = L.bit_length() - 1
    late = M // 2 // 128 * 128 if stages == 2 and M % 128 == 0 else 0
    early = M - late
    top = l >> (stages - 1)

    def remote(src, dst, ss, rs, **to):
        where = {"row": r, "col": c, "layer": l}
        where.update(to)
        return pltpu.make_async_remote_copy(src_ref=src, dst_ref=dst, send_sem=ss, recv_sem=rs,
                                            device_id=where, device_id_type=MESH)

    def ks(q):
        return pl.ds(q * kc, kc)

    def far_row(d):
        return lax.rem(r + d, R)

    def near(dc):
        return lax.rem(c + dc + C, C)

    order = sorted(range(1, C), key=lambda d: -min(d, C - d))

    def slice_for(d, q):
        return pl.ds(far_row(d) * Kr + q * kc, kc)

    def own_a(q):
        return pltpu.make_async_copy(a_ref.at[slice_for(0, q)], a_all.at[0, ks(q)], arecv.at[0, q])

    def own_i(q):
        return pltpu.make_async_copy(i_ref.at[slice_for(0, q)], i_all.at[0, ks(q)], xrecv.at[0, q])

    for q in range(Q):
        own_a(q).start()
        own_i(q).start()

    barrier = pltpu.get_barrier_semaphore()
    partners = [{"row": far_row(d), "col": near(dc)} for d in range(R) for dc in range(C) if d or dc]
    partners += [{"layer": l ^ (1 << t)} for t in range(stages)]
    for p in partners:
        where = {"row": r, "col": c, "layer": l}
        where.update(p)
        pl.semaphore_signal(barrier, inc=1, device_id=where, device_id_type=MESH)
    pl.semaphore_wait(barrier, len(partners))

    def row_a(d, q):
        return remote(a_ref.at[slice_for(d, q)], a_all.at[R - d, ks(q)], asend.at[d, q], arecv.at[R - d, q], row=far_row(d))

    parts = [(0, early, (1 - top) * late)] + ([(early, late, top * early)] if late else [])

    def row_i(d, q, p):
        at, size, start = parts[p]
        src = i_ref.at[slice_for(d, q), :, pl.ds(pl.multiple_of(start, 128), size)] if late else i_ref.at[slice_for(d, q)]
        return remote(src, i_all.at[R - d, ks(q), :, pl.ds(at, size)], xsend.at[p * R + d, q], xrecv.at[p * R + R - d, q],
                      row=far_row(d))

    def col_a(d, j, q):
        b = far_row(d) * m + j
        at = pl.ds(j * V, V)
        src = a_all.at[d, ks(q), at] if d else a_ref.at[slice_for(0, q), at]
        return b, remote(src, az.at[c, ks(q)], zsend.at[d, j, q], zrecv.at[c, q], col=b)

    def col_start(d, q):
        for j in range(m):
            b, cp = col_a(d, j, q)

            @pl.when(b != c)
            def _():
                cp.start()

    for q in range(Q):
        for d in range(1, R):
            row_a(d, q).start()
        col_start(0, q)
    for p in range(len(parts)):
        for q in range(Q):
            for d in range(1, R):
                row_i(d, q, p).start()

    whole = (0, M, 0)

    def turn(d, q, part):
        first, size = part[:2]
        for k in range(kc):
            at = (q * kc + k) * V
            i_t[d, first:first + size, at:at + V] = i_all[d, q * kc + k, :, first:first + size].T

    def add(d, block, x, q, part):
        first, size, start = part
        piece = lax.dot_general(i_t[d, first:first + size, q * w:(q + 1) * w], x, (((1,), (0,)), ((), ())),
                                preferred_element_type=jnp.float32)
        to = pl.ds(start if isinstance(start, int) else pl.multiple_of(start, 128), size)
        if q == 0:
            acc[d, block, to] = piece
        else:
            acc[d, block, to] += piece

    own_row = lax.rem(lax.div(c, m) - r + R, R)
    own_at = pl.ds(pl.multiple_of(lax.rem(c, m) * V, V), V)

    def own_block(d, q, part):
        add(d, c, a_all[own_row, ks(q), own_at].reshape(w, N), q, part)

    for q in range(Q):
        own_a(q).wait()
        for d in range(1, R):
            row_a(R - d, q).wait_recv()
            col_start(d, q)
        own_i(q).wait()
        turn(0, q, whole)
        own_block(0, q, whole)

    for q in range(Q):
        for dc in order[::-1]:
            s = near(dc)
            here = az.at[s, ks(q)]
            remote(here, here, zsend.at[0, 0, q], zrecv.at[s, q], col=s).wait_recv()
            add(0, s, az[s, ks(q)].reshape(w, N), q, whole)

    def block(t, hi, bit):
        return (hi << (t + 1)) | (bit << t) | (l & ((1 << t) - 1))

    def halving(d, t, i, col):
        n = L >> (t + 1)
        hi = (l >> (t + 1)) ^ hi_order(n)[i]
        bit = (l >> t) & 1
        slot = n - 1 + hi
        give, keep = block(t, hi, 1 - bit), block(t, hi, bit)
        give, keep = (pl.ds(pl.multiple_of(b * rows, 8), rows) for b in (give, keep))
        if d == 0:
            cp = remote(acc.at[0, :, give], lay_buf.at[0, slot], osend.at[slot], orecv.at[slot], layer=l ^ (1 << t))
        else:
            cp = remote(acc.at[d, col, give], lay_buf.at[d, slot, col], lsend.at[d, slot, col], lrecv.at[d, slot, col],
                        layer=l ^ (1 << t))
        return cp, keep, slot

    def own_stage(t):
        for i in range(L >> (t + 1)):
            cp, keep, slot = halving(0, t, i, None)
            cp.wait_recv()
            acc[0, :, keep] += lay_buf[0, slot]
            if t + 1 < stages and i < L >> (t + 2):
                halving(0, t + 1, i, None)[0].start()

    for i in range(L >> 1):
        halving(0, 0, i, None)[0].start()

    c_order = [near(dc) for dc in order] + [c]
    mine = pl.ds(pl.multiple_of(l * rows, 8), rows)

    def first_stage_start(i):
        for d in range(1, R):
            for col in c_order:
                halving(d, 0, i, col)[0].start()

    def stage_end(t, i):
        for d in range(1, R):
            for col in c_order:
                cp, keep, slot = halving(d, t, i, col)
                cp.wait_recv()
                acc[d, col, keep] += lay_buf[d, slot, col]
                if t + 1 == stages:
                    row_sum(d, col).start()
                elif i < L >> (t + 2):
                    halving(d, t + 1, i, col)[0].start()

    for p, part in enumerate(parts):
        for q in range(Q):
            for d in range(1, R):
                row_i(R - d, q, p).wait_recv()
                turn(d, q, part)
                own_block(d, q, part)
                for dc in order:
                    s = near(dc)
                    add(d, s, az[s, ks(q)].reshape(w, N), q, part)
            if p == 0 and q == 0:
                own_stage(0)
            if p == 1 and q == min(1, Q - 1):
                stage_end(0, 0)
        if late:
            first_stage_start(p)

    def row_sum(d, col):
        return remote(acc.at[d, col, mine], row_buf.at[R - d, c], rsend.at[d, col], rrecv.at[R - d, c],
                      row=far_row(d), col=col)

    def col_sum(dc):
        return remote(acc.at[0, near(dc), mine], col_buf.at[c], csend.at[dc], crecv.at[c], col=near(dc))

    if not late:
        for i in range(L >> 1):
            first_stage_start(i)
    for t in range(1, stages):
        own_stage(t)
    for dc in order:
        col_sum(dc).start()
    for t in range(stages):
        for i in range(L >> (t + 1)):
            if not (late and t == 0 and i == 0):
                stage_end(t, i)
    total = acc[0, c, mine]
    for dc in order[::-1]:
        s = near(dc)
        remote(col_buf.at[s], col_buf.at[s], csend.at[dc], crecv.at[s], col=s).wait_recv()
        total += col_buf[s]
    for col in c_order[::-1]:
        for d in range(1, R):
            here = row_buf.at[d, col]
            remote(here, here, rsend.at[d, col], rrecv.at[d, col], row=far_row(d), col=col).wait_recv()
            total += row_buf[d, col]
    o_ref[...] = total

    for q in range(Q):
        for d in range(R):
            if d:
                row_a(d, q).wait_send()
                for p in range(len(parts)):
                    row_i(d, q, p).wait_send()
            for j in range(m):
                b, cp = col_a(d, j, q)

                @pl.when(b != c)
                def _():
                    cp.wait_send()
    for t in range(stages):
        for i in range(L >> (t + 1)):
            halving(0, t, i, None)[0].wait_send()
            for d in range(1, R):
                for col in c_order:
                    halving(d, t, i, col)[0].wait_send()
    for col in c_order:
        for d in range(1, R):
            row_sum(d, col).wait_send()
    for dc in order:
        col_sum(dc).wait_send()


def general_call(R, C, L, integrals, amplitudes):
    K, V, M = integrals.shape
    V_row, N = amplitudes.shape[1:]
    rows = M // L
    Kr = K // R
    Q = Kr
    m = C // R
    slots = L - 1
    dma = pltpu.SemaphoreType.DMA
    vmem = pl.BlockSpec(memory_space=pltpu.VMEM)
    anyspace = pl.BlockSpec(memory_space=pl.ANY)
    return pl.pallas_call(
        functools.partial(kernel, R, C, L, Q),
        out_shape=jax.ShapeDtypeStruct((rows, N), jnp.float32),
        in_specs=[anyspace, anyspace],
        out_specs=vmem,
        scratch_shapes=[
            pltpu.VMEM((R, Kr, V_row, N), jnp.bfloat16),
            pltpu.VMEM((C, Kr, V, N), jnp.bfloat16),
            pltpu.VMEM((R, Kr, V, M), jnp.bfloat16),
            pltpu.VMEM((R, M, Kr * V), jnp.bfloat16),
            pltpu.VMEM((R, C, M, N), jnp.float32),
            pltpu.VMEM((R, slots, C, rows, N), jnp.float32),
            pltpu.VMEM((R, C, rows, N), jnp.float32),
            pltpu.VMEM((C, rows, N), jnp.float32),
            dma((R, Q)), dma((R, Q)),
            dma((2 * R, Q)), dma((2 * R, Q)),
            dma((R, m, Q)), dma((C, Q)),
            dma((slots,)), dma((slots,)),
            dma((R, slots, C)), dma((R, slots, C)),
            dma((R, C)), dma((R, C)),
            dma((C,)), dma((C,)),
        ],
        compiler_params=pltpu.CompilerParams(collective_id=0, has_side_effects=True),
    )(integrals, amplitudes)


def swift(R, C, L, T, i_ref, a_ref, o_ref,
          a_x, az, i_in, i_s, i_t, acc, last, core_buf, x_buf, z_buf, y_out, y_buf, last_buf, hi_buf, lo_buf,
          own, iown, asend, arecv, isend, irecv, zsend, zrecv,
          csend, crecv, xsend, xrecv, wsend, wrecv, ysend, yrecv, lsend, lrecv, hsend, hrecv, there):
    r, c, l = lax.axis_index("row"), lax.axis_index("col"), lax.axis_index("layer")
    K, V, M = i_ref.shape
    N = a_ref.shape[2]
    Kr = K // R
    W = Kr * V
    m = C // R
    rows = M // L
    half_rows = 2 * rows
    body = rows - T
    low = rows // 2 // 16 * 16
    o = 1 - r
    x, core = lax.div(l, 2), lax.rem(l, 2)
    home = lax.div(c, m) == r
    away = jnp.logical_not(home)
    outer = (c == 0) | (c == C - 1)
    inner = jnp.logical_not(outer)

    def remote(src, dst, ss, rs, **to):
        where = {"row": r, "col": c, "layer": l}
        where.update(to)
        return pltpu.make_async_remote_copy(src_ref=src, dst_ref=dst, send_sem=ss, recv_sem=rs,
                                            device_id=where, device_id_type=MESH)

    def signal(sem, **to):
        where = {"row": r, "col": c, "layer": l}
        where.update(to)
        pl.semaphore_signal(sem, inc=1, device_id=where, device_id_type=MESH)

    def at(start, size, unit):
        return pl.ds(pl.multiple_of(start, unit), size)

    sib, opp = l ^ 1, l ^ 2

    def local_a(q):
        return pltpu.make_async_copy(a_ref.at[r * Kr + q, at(lax.rem(c, m) * V, V, V)], az.at[c, q], own.at[q])

    def cross_a(q):
        return pltpu.make_async_copy(a_x.at[q, at(lax.rem(c, m) * V, V, V)], az.at[c, q], own.at[q])

    def local_i(k):
        return pltpu.make_async_copy(i_ref.at[k], i_in.at[k], iown.at[k])

    barrier = pltpu.get_barrier_semaphore()
    signal(barrier, row=o)
    signal(barrier, layer=sib)
    signal(barrier, layer=opp)

    @pl.when(c > 0)
    def _():
        signal(barrier, col=c - 1)

    @pl.when(c < C - 1)
    def _():
        signal(barrier, col=c + 1)

    pl.semaphore_wait(barrier, 3 + (c > 0).astype(jnp.int32) + (c < C - 1).astype(jnp.int32))

    def row_a(q, j):
        span = pl.ds(j * V, V)
        return remote(a_ref.at[o * Kr + q, span], a_x.at[q, span], asend.at[q, j], arecv.at[q, j], row=o)

    for q in range(Kr):
        for j in range(m):
            row_a(q, j).start()

    def col_a(d, j, q):
        b = (o if d else r) * m + j
        span = pl.ds(j * V, V)
        src = a_x.at[q, span] if d else a_ref.at[r * Kr + q, span]
        return b, remote(src, az.at[c, q], zsend.at[d, j, q], zrecv.at[c, q], col=b)

    def col_start(d, *qs, js=range(m)):
        for q in qs:
            for j in js:
                b, cp = col_a(d, j, q)

                @pl.when(b != c)
                def _():
                    cp.start()

    ahead, turnover = 3, Kr - 2

    @pl.when(home)
    def _():
        col_start(0, *range(ahead))

    @pl.when(home & inner)
    def _():
        col_start(0, *range(ahead, Kr))

    for t in range(2, C):
        @pl.when((c >= 1) & (c + t - 1 < C))
        def _():
            signal(there.at[0, t], col=c - 1)

        @pl.when((c + 1 < C) & (c - t + 1 >= 0))
        def _():
            signal(there.at[1, t], col=c + 1)

        @pl.when(c + t < C)
        def _():
            pl.semaphore_wait(there.at[0, t], 1)

        @pl.when(c - t >= 0)
        def _():
            pl.semaphore_wait(there.at[1, t], 1)

    @pl.when(away & outer)
    def _():
        col_start(0, *range(Kr))

    for k in range(Kr):
        local_i(o * Kr + k).start()
    for k in range(Kr):
        local_i(r * Kr + k).start()

    @pl.when(home)
    def _():
        for q in range(Kr):
            local_a(q).start()

    def turn(dst, k, kk):
        dst[:, kk * V:(kk + 1) * V] = i_in[k].T

    other = (1 - x) * half_rows
    mine = x * half_rows
    groups = [(other, rows), (other + rows, rows), (mine, low), (mine + rows, low),
              (mine + low, body - low), (mine + rows + low, body - low), (mine + body, T), (mine + rows + body, T)]

    def row_i(g):
        start, size = groups[g]
        span = at(start, size, 16)
        return remote(i_s.at[span], i_t.at[1, span], isend.at[g], irecv.at[g], row=o)

    per = 2 * Kr // Kr
    for q in range(Kr):
        for j in range(m):
            row_a(q, j).wait_recv()
            if q < turnover:
                @pl.when(outer | away)
                def _():
                    col_start(1, q, js=[j])
            else:
                col_start(1, q, js=[j])

        @pl.when(away)
        def _():
            cross_a(q).start()

        if q == turnover:
            @pl.when(inner & home)
            def _():
                col_start(1, *range(turnover))

            @pl.when(inner & away)
            def _():
                col_start(0, *range(Kr))

            @pl.when(outer & home)
            def _():
                col_start(0, *range(ahead, Kr))

        for kk in range(per * q, per * q + per):
            if kk < Kr:
                local_i(o * Kr + kk).wait()
                turn(i_s, o * Kr + kk, kk)
                if kk == Kr - 1:
                    for g in range(len(groups)):
                        row_i(g).start()
            else:
                local_i(r * Kr + kk - Kr).wait()
                turn(i_t.at[0], r * Kr + kk - Kr, kk - Kr)

    side = lax.div(c, m)
    units = [(side * m, m), ((1 - side) * (C - 1), 1), (1 + (1 - side), 1)]

    def wait_piece(s):
        for q in range(Kr):
            @pl.when(s == c)
            def _():
                local_a(q).wait()

            @pl.when(s != c)
            def _():
                here = az.at[s, q]
                remote(here, here, zsend.at[0, 0, q], zrecv.at[s, q], col=s).wait_recv()

    def columns(us):
        return [units[u][0] + j for u in us for j in range(units[u][1])]

    def wide(us):
        return jnp.concatenate([az[s].reshape(W, N) for s in columns(us)], axis=1)

    def product(d, start, size, right):
        return lax.dot_general(i_t[d, at(start, size, 16)], right, (((1,), (0,)), ((), ())),
                               preferred_element_type=jnp.float32)

    def fill(d, us, start, size, right):
        piece = product(d, start, size, right)
        for j, s in enumerate(columns(us)):
            acc[d, s, at(start, size, 16)] = piece[:, j * N:(j + 1) * N]

    def pair(u):
        return pl.ds(*units[u])

    def block(b, size=rows):
        return at(b * rows, size, 16)

    def core_span(d, keep):
        if d and keep:
            return (0, low) if keep == 1 else (low, body - low)
        return (0, rows)

    def core_copy(d, u, keep):
        start, size = core_span(d, keep)
        give = 2 * (x if keep else 1 - x) + 1 - core
        return remote(acc.at[d, pair(u), at(give * rows + start, size, 16)],
                      core_buf.at[d, u, min(keep, 1), pl.ds(0, units[u][1]), pl.ds(start, size)],
                      csend.at[d, u, keep], crecv.at[d, u, keep], layer=sib)

    def core_end(d, u, keep):
        start, size = core_span(d, keep)
        have = 2 * (x if keep else 1 - x) + core
        core_copy(d, u, keep).wait_recv()
        acc[d, pair(u), at(have * rows + start, size, 16)] += core_buf[d, u, min(keep, 1), :units[u][1], start:start + size]

    def x_copy(d, u):
        return remote(acc.at[d, pair(u), block(2 * (1 - x) + core)], x_buf.at[d, u, pl.ds(0, units[u][1])],
                      xsend.at[d, u], xrecv.at[d, u], layer=opp)

    def x_add(d, u, start, size):
        acc[d, pair(u), at(l * rows + start, size, 16)] += x_buf[d, u, :units[u][1], start:start + size]

    def z_size(d):
        return low if d else rows

    def z_copy(d, u, j):
        s = units[u][0] + j
        return s, remote(acc.at[d, s, block(l, z_size(d))], z_buf.at[d, c, pl.ds(0, z_size(d))],
                         wsend.at[d, u, j], wrecv.at[d, c], col=s)

    def z_start(d, u):
        for j in range(units[u][1]):
            s, cp = z_copy(d, u, j)

            @pl.when(s != c)
            def _():
                cp.start()

    def z_wait(d, s):
        here = z_buf.at[d, s, pl.ds(0, z_size(d))]
        remote(here, here, wsend.at[d, 0, 0], wrecv.at[d, s], col=s).wait_recv()

    def hi_copy(s):
        return remote(acc.at[1, s, at(l * rows + low, rows - low, 16)], hi_buf.at[c], hsend.at[0, s], hrecv.at[0, c], row=o, col=s)

    def lo_copy():
        s = units[2][0]
        return remote(acc.at[1, s, block(l, low)], lo_buf.at[lax.rem(c, m)], hsend.at[1, 0], hrecv.at[1, lax.rem(c, m)], row=o, col=s)

    for s in columns([0, 1]):
        wait_piece(s)
    for u in (0, 1):
        fill(0, [u], 0, M, wide([u]))
        core_copy(0, u, 0).start()
        core_copy(0, u, 1).start()
    for u in (0, 1):
        core_end(0, u, 0)
        x_copy(0, u).start()
    for u in (0, 1):
        core_end(0, u, 1)

    for g in range(2):
        row_i(g).wait_recv()
    for u in (0, 1):
        fill(1, [u], other, half_rows, wide([u]))
        core_copy(1, u, 0).start()
    for u in (0, 1):
        x_copy(0, u).wait_recv()
        x_add(0, u, 0, rows)
        z_start(0, u)
    for u in (0, 1):
        core_end(1, u, 0)
        x_copy(1, u).start()

    for g in range(2, 4):
        row_i(g).wait_recv()
    for u in (0, 1):
        right = wide([u])
        for i in range(2):
            fill(1, [u], mine + i * rows, low, right)
        core_copy(1, u, 1).start()
    for u in (0, 1):
        core_end(1, u, 1)
        x_copy(1, u).wait_recv()
        x_add(1, u, 0, low)
        z_start(1, u)

    for s in columns([2]):
        wait_piece(s)
    right = wide([2])
    fill(0, [2], 0, M, right)
    core_copy(0, 2, 0).start()
    core_copy(0, 2, 1).start()
    fill(1, [2], other, half_rows, right)
    core_copy(1, 2, 0).start()
    core_end(0, 2, 0)
    x_copy(0, 2).start()
    for i in range(2):
        fill(1, [2], mine + i * rows, low, right)
    core_copy(1, 2, 1).start()
    core_end(1, 2, 0)
    x_copy(1, 2).start()
    core_end(0, 2, 1)
    core_end(1, 2, 1)

    for g in range(4, 6):
        row_i(g).wait_recv()
    for us in ([0], [1, 2]):
        right = wide(us)
        for i in range(2):
            fill(1, us, mine + i * rows + low, body - low, right)
        for u in us:
            core_copy(1, u, 2).start()
    x_copy(0, 2).wait_recv()
    x_add(0, 2, 0, rows)
    z_start(0, 2)

    def high_start(u):
        x_add(1, u, low, body - low)
        acc[1, pair(u), at(l * rows + body, T, 16)] = x_buf[1, u, :units[u][1], body:]
        for s in columns([u]):
            hi_copy(s).start()

    for u in (0, 1):
        core_end(1, u, 2)
        high_start(u)

    def last_copy(i, s):
        return remote(last.at[i, s], last_buf.at[core, c], lsend.at[i, s], lrecv.at[core, c],
                      row=o, col=s, layer=2 * x + i)

    for g in range(6, 8):
        row_i(g).wait_recv()
    for us in ([0], [1, 2]):
        right = wide(us)
        for i in range(2):
            piece = product(1, mine + i * rows + body, T, right)
            for j, s in enumerate(columns(us)):
                last[i, s] = piece[:, j * N:(j + 1) * N]
    for dc in range(C):
        for i in range(2):
            last_copy(i, c ^ (C - 1 - dc)).start()

    core_end(1, 2, 2)
    x_copy(1, 2).wait_recv()
    x_add(1, 2, 0, low)
    lo_copy().start()
    high_start(2)

    def y_copy():
        return remote(y_out, y_buf, ysend, yrecv, row=o)

    beside = c ^ 1
    z_wait(1, beside)
    y_out[...] = acc[1, c, block(l, low)] + z_buf[1, beside, :low]
    across = [(1 - side) * m + j for j in range(m)]

    @pl.when(outer)
    def _():
        for s in across:
            z_wait(1, s)
            y_out[...] += z_buf[1, s, :low]

    y_copy().start()

    for q in range(Kr):
        for j in range(m):
            row_a(q, j).wait_send()
        for d in range(2):
            for j in range(m):
                b, cp = col_a(d, j, q)

                @pl.when(b != c)
                def _():
                    cp.wait_send()
    for g in range(len(groups)):
        row_i(g).wait_send()
    for d in range(2):
        for u in range(3):
            for keep in range(2 + d):
                core_copy(d, u, keep).wait_send()
            x_copy(d, u).wait_send()

    total = acc[0, c, block(l)]
    for s in [beside] + across:
        z_wait(0, s)
        total += z_buf[0, s]
    y_copy().wait_recv()
    o_ref[:low] = total[:low] + y_buf[...]

    @pl.when(inner)
    def _():
        for j in range(m):
            here = lo_buf.at[j]
            remote(here, here, hsend.at[1, 0], hrecv.at[1, j], row=o, col=across[j]).wait_recv()
            o_ref[:low] += lo_buf[j]

    high = total[low:]
    for s in range(C):
        here = hi_buf.at[s]
        remote(here, here, hsend.at[0, 0], hrecv.at[0, s], row=o, col=s).wait_recv()
        high += hi_buf[s]
    tail = jnp.zeros((T, N), jnp.float32)
    for i in range(2):
        for s in range(C):
            here = last_buf.at[i, s]
            remote(here, here, lsend.at[0, 0], lrecv.at[i, s], row=o, col=s, layer=2 * x + i).wait_recv()
            tail += last_buf[i, s]
    o_ref[low:body] = high[:body - low]
    o_ref[body:] = high[body - low:] + tail

    for d in range(2):
        for u in range(3 - d):
            for j in range(units[u][1]):
                s, cp = z_copy(d, u, j)

                @pl.when(s != c)
                def _():
                    cp.wait_send()
    for s in range(C):
        hi_copy(s).wait_send()
        for i in range(2):
            last_copy(i, s).wait_send()
    lo_copy().wait_send()
    y_copy().wait_send()


def swift_call(R, C, L, integrals, amplitudes):
    K, V, M = integrals.shape
    V_row, N = amplitudes.shape[1:]
    rows = M // L
    Kr = K // R
    m = C // R
    T = 16
    low = rows // 2 // 16 * 16
    dma = pltpu.SemaphoreType.DMA
    f32, bf16 = jnp.float32, jnp.bfloat16
    anyspace = pl.BlockSpec(memory_space=pl.ANY)
    return pl.pallas_call(
        functools.partial(swift, R, C, L, T),
        out_shape=jax.ShapeDtypeStruct((rows, N), f32),
        in_specs=[anyspace, anyspace],
        out_specs=pl.BlockSpec(memory_space=pltpu.VMEM),
        scratch_shapes=[
            pltpu.VMEM((Kr, V_row, N), bf16),
            pltpu.VMEM((C, Kr, V, N), bf16),
            pltpu.VMEM((K, V, M), bf16),
            pltpu.VMEM((M, Kr * V), bf16),
            pltpu.VMEM((2, M, Kr * V), bf16),
            pltpu.VMEM((2, C, M, N), f32),
            pltpu.VMEM((2, C, T, N), f32),
            pltpu.VMEM((2, 3, 2, m, rows, N), f32),
            pltpu.VMEM((2, 3, m, rows, N), f32),
            pltpu.VMEM((2, C, rows, N), f32),
            pltpu.VMEM((low, N), f32),
            pltpu.VMEM((low, N), f32),
            pltpu.VMEM((2, C, T, N), f32),
            pltpu.VMEM((C, rows - low, N), f32),
            pltpu.VMEM((m, low, N), f32),
            dma((Kr,)), dma((K,)),
            dma((Kr, m)), dma((Kr, m)),
            dma((8,)), dma((8,)),
            dma((2, m, Kr)), dma((C, Kr)),
            dma((2, 3, 3)), dma((2, 3, 3)),
            dma((2, 3)), dma((2, 3)),
            dma((2, 3, m)), dma((2, C)),
            dma, dma,
            dma((2, C)), dma((2, C)),
            dma((2, C)), dma((2, C)),
            pltpu.SemaphoreType.REGULAR((2, C)),
        ],
        compiler_params=pltpu.CompilerParams(collective_id=0, has_side_effects=True),
    )(integrals, amplitudes)


def local(R, C, L, integrals, amplitudes, coulomb, row_gap, col_gap):
    swift_fits = R == 2 and C == 4 and L == 4 and integrals.shape[2] % (16 * L) == 0
    call = swift_call if swift_fits else general_call
    own_rows = call(R, C, L, integrals, amplitudes)
    gap_sum = row_gap[:, None] + col_gap[None, :]
    return (coulomb.astype(jnp.float32) + own_rows) / gap_sum


def solution(mesh):
    R, C, L = (mesh.shape[a] for a in ("row", "col", "layer"))
    placed = (
        P("layer", "col", "row"),
        P("layer", "row", "col"),
        P(("row", "layer"), "col"),
        P(("row", "layer")),
        P("col"),
    )
    return jax.shard_map(
        functools.partial(local, R, C, L), mesh=mesh, in_specs=placed, out_specs=P(("row", "layer"), "col"),
        check_vma=False,
    )
```

```python
import functools

import jax
import jax.numpy as jnp
from jax import lax
from jax.experimental import pallas as pl
from jax.experimental.pallas import tpu as pltpu
from jax.sharding import PartitionSpec as P

MESH = pl.DeviceIdType.MESH


def hi_order(n):
    if n == 1:
        return [0]
    below = hi_order(n // 2)
    return [2 * x + 1 for x in below] + [2 * x for x in below]


def kernel(R, C, L, Q, i_ref, a_ref, o_ref,
           a_all, az, i_all, i_t, acc, lay_buf, row_buf, col_buf,
           asend, arecv, xsend, xrecv, zsend, zrecv,
           osend, orecv, lsend, lrecv, rsend, rrecv, csend, crecv):
    r, c, l = lax.axis_index("row"), lax.axis_index("col"), lax.axis_index("layer")
    K, V_row, N = a_ref.shape
    V, M = i_ref.shape[1:]
    Kr = K // R
    kc = Kr // Q
    m = C // R
    w = kc * V
    rows = M // L
    stages = L.bit_length() - 1
    late = M // 2 // 128 * 128 if stages == 2 and M % 128 == 0 else 0
    early = M - late
    top = l >> (stages - 1)

    def remote(src, dst, ss, rs, **to):
        where = {"row": r, "col": c, "layer": l}
        where.update(to)
        return pltpu.make_async_remote_copy(src_ref=src, dst_ref=dst, send_sem=ss, recv_sem=rs,
                                            device_id=where, device_id_type=MESH)

    def ks(q):
        return pl.ds(q * kc, kc)

    def far_row(d):
        return lax.rem(r + d, R)

    def near(dc):
        return lax.rem(c + dc + C, C)

    order = sorted(range(1, C), key=lambda d: -min(d, C - d))

    def slice_for(d, q):
        return pl.ds(far_row(d) * Kr + q * kc, kc)

    def own_a(q):
        return pltpu.make_async_copy(a_ref.at[slice_for(0, q)], a_all.at[0, ks(q)], arecv.at[0, q])

    def own_i(q):
        return pltpu.make_async_copy(i_ref.at[slice_for(0, q)], i_all.at[0, ks(q)], xrecv.at[0, q])

    for q in range(Q):
        own_a(q).start()
        own_i(q).start()

    barrier = pltpu.get_barrier_semaphore()
    partners = [{"row": far_row(d), "col": near(dc)} for d in range(R) for dc in range(C) if d or dc]
    partners += [{"layer": l ^ (1 << t)} for t in range(stages)]
    for p in partners:
        where = {"row": r, "col": c, "layer": l}
        where.update(p)
        pl.semaphore_signal(barrier, inc=1, device_id=where, device_id_type=MESH)
    pl.semaphore_wait(barrier, len(partners))

    def row_a(d, q):
        return remote(a_ref.at[slice_for(d, q)], a_all.at[R - d, ks(q)], asend.at[d, q], arecv.at[R - d, q], row=far_row(d))

    parts = [(0, early, (1 - top) * late)] + ([(early, late, top * early)] if late else [])

    def row_i(d, q, p):
        at, size, start = parts[p]
        src = i_ref.at[slice_for(d, q), :, pl.ds(pl.multiple_of(start, 128), size)] if late else i_ref.at[slice_for(d, q)]
        return remote(src, i_all.at[R - d, ks(q), :, pl.ds(at, size)], xsend.at[p * R + d, q], xrecv.at[p * R + R - d, q],
                      row=far_row(d))

    def col_a(d, j, q):
        b = far_row(d) * m + j
        at = pl.ds(j * V, V)
        src = a_all.at[d, ks(q), at] if d else a_ref.at[slice_for(0, q), at]
        return b, remote(src, az.at[c, ks(q)], zsend.at[d, j, q], zrecv.at[c, q], col=b)

    def col_start(d, q):
        for j in range(m):
            b, cp = col_a(d, j, q)

            @pl.when(b != c)
            def _():
                cp.start()

    for q in range(Q):
        for d in range(1, R):
            row_a(d, q).start()
        col_start(0, q)
    for p in range(len(parts)):
        for q in range(Q):
            for d in range(1, R):
                row_i(d, q, p).start()

    whole = (0, M, 0)

    def turn(d, q, part):
        first, size = part[:2]
        for k in range(kc):
            at = (q * kc + k) * V
            i_t[d, first:first + size, at:at + V] = i_all[d, q * kc + k, :, first:first + size].T

    def add(d, block, x, q, part):
        first, size, start = part
        piece = lax.dot_general(i_t[d, first:first + size, q * w:(q + 1) * w], x, (((1,), (0,)), ((), ())),
                                preferred_element_type=jnp.float32)
        to = pl.ds(start if isinstance(start, int) else pl.multiple_of(start, 128), size)
        if q == 0:
            acc[d, block, to] = piece
        else:
            acc[d, block, to] += piece

    own_row = lax.rem(lax.div(c, m) - r + R, R)
    own_at = pl.ds(pl.multiple_of(lax.rem(c, m) * V, V), V)

    def own_block(d, q, part):
        add(d, c, a_all[own_row, ks(q), own_at].reshape(w, N), q, part)

    for q in range(Q):
        own_a(q).wait()
        for d in range(1, R):
            row_a(R - d, q).wait_recv()
            col_start(d, q)
        own_i(q).wait()
        turn(0, q, whole)
        own_block(0, q, whole)

    for q in range(Q):
        for dc in order[::-1]:
            s = near(dc)
            here = az.at[s, ks(q)]
            remote(here, here, zsend.at[0, 0, q], zrecv.at[s, q], col=s).wait_recv()
            add(0, s, az[s, ks(q)].reshape(w, N), q, whole)

    def block(t, hi, bit):
        return (hi << (t + 1)) | (bit << t) | (l & ((1 << t) - 1))

    def halving(d, t, i, col):
        n = L >> (t + 1)
        hi = (l >> (t + 1)) ^ hi_order(n)[i]
        bit = (l >> t) & 1
        slot = n - 1 + hi
        give, keep = block(t, hi, 1 - bit), block(t, hi, bit)
        give, keep = (pl.ds(pl.multiple_of(b * rows, 8), rows) for b in (give, keep))
        if d == 0:
            cp = remote(acc.at[0, :, give], lay_buf.at[0, slot], osend.at[slot], orecv.at[slot], layer=l ^ (1 << t))
        else:
            cp = remote(acc.at[d, col, give], lay_buf.at[d, slot, col], lsend.at[d, slot, col], lrecv.at[d, slot, col],
                        layer=l ^ (1 << t))
        return cp, keep, slot

    def own_stage(t):
        for i in range(L >> (t + 1)):
            cp, keep, slot = halving(0, t, i, None)
            cp.wait_recv()
            acc[0, :, keep] += lay_buf[0, slot]
            if t + 1 < stages and i < L >> (t + 2):
                halving(0, t + 1, i, None)[0].start()

    for i in range(L >> 1):
        halving(0, 0, i, None)[0].start()

    c_order = [near(dc) for dc in order] + [c]
    mine = pl.ds(pl.multiple_of(l * rows, 8), rows)

    def first_stage_start(i):
        for d in range(1, R):
            for col in c_order:
                halving(d, 0, i, col)[0].start()

    def stage_end(t, i):
        for d in range(1, R):
            for col in c_order:
                cp, keep, slot = halving(d, t, i, col)
                cp.wait_recv()
                acc[d, col, keep] += lay_buf[d, slot, col]
                if t + 1 == stages:
                    row_sum(d, col).start()
                elif i < L >> (t + 2):
                    halving(d, t + 1, i, col)[0].start()

    for p, part in enumerate(parts):
        for q in range(Q):
            for d in range(1, R):
                row_i(R - d, q, p).wait_recv()
                turn(d, q, part)
                own_block(d, q, part)
                for dc in order:
                    s = near(dc)
                    add(d, s, az[s, ks(q)].reshape(w, N), q, part)
            if p == 0 and q == 0:
                own_stage(0)
            if p == 1 and q == min(1, Q - 1):
                stage_end(0, 0)
        if late:
            first_stage_start(p)

    def row_sum(d, col):
        return remote(acc.at[d, col, mine], row_buf.at[R - d, c], rsend.at[d, col], rrecv.at[R - d, c],
                      row=far_row(d), col=col)

    def col_sum(dc):
        return remote(acc.at[0, near(dc), mine], col_buf.at[c], csend.at[dc], crecv.at[c], col=near(dc))

    if not late:
        for i in range(L >> 1):
            first_stage_start(i)
    for t in range(1, stages):
        own_stage(t)
    for dc in order:
        col_sum(dc).start()
    for t in range(stages):
        for i in range(L >> (t + 1)):
            if not (late and t == 0 and i == 0):
                stage_end(t, i)
    total = acc[0, c, mine]
    for dc in order[::-1]:
        s = near(dc)
        remote(col_buf.at[s], col_buf.at[s], csend.at[dc], crecv.at[s], col=s).wait_recv()
        total += col_buf[s]
    for col in c_order[::-1]:
        for d in range(1, R):
            here = row_buf.at[d, col]
            remote(here, here, rsend.at[d, col], rrecv.at[d, col], row=far_row(d), col=col).wait_recv()
            total += row_buf[d, col]
    o_ref[...] = total

    for q in range(Q):
        for d in range(R):
            if d:
                row_a(d, q).wait_send()
                for p in range(len(parts)):
                    row_i(d, q, p).wait_send()
            for j in range(m):
                b, cp = col_a(d, j, q)

                @pl.when(b != c)
                def _():
                    cp.wait_send()
    for t in range(stages):
        for i in range(L >> (t + 1)):
            halving(0, t, i, None)[0].wait_send()
            for d in range(1, R):
                for col in c_order:
                    halving(d, t, i, col)[0].wait_send()
    for col in c_order:
        for d in range(1, R):
            row_sum(d, col).wait_send()
    for dc in order:
        col_sum(dc).wait_send()


def general_call(R, C, L, integrals, amplitudes):
    K, V, M = integrals.shape
    V_row, N = amplitudes.shape[1:]
    rows = M // L
    Kr = K // R
    Q = Kr
    m = C // R
    slots = L - 1
    dma = pltpu.SemaphoreType.DMA
    vmem = pl.BlockSpec(memory_space=pltpu.VMEM)
    anyspace = pl.BlockSpec(memory_space=pl.ANY)
    return pl.pallas_call(
        functools.partial(kernel, R, C, L, Q),
        out_shape=jax.ShapeDtypeStruct((rows, N), jnp.float32),
        in_specs=[anyspace, anyspace],
        out_specs=vmem,
        scratch_shapes=[
            pltpu.VMEM((R, Kr, V_row, N), jnp.bfloat16),
            pltpu.VMEM((C, Kr, V, N), jnp.bfloat16),
            pltpu.VMEM((R, Kr, V, M), jnp.bfloat16),
            pltpu.VMEM((R, M, Kr * V), jnp.bfloat16),
            pltpu.VMEM((R, C, M, N), jnp.float32),
            pltpu.VMEM((R, slots, C, rows, N), jnp.float32),
            pltpu.VMEM((R, C, rows, N), jnp.float32),
            pltpu.VMEM((C, rows, N), jnp.float32),
            dma((R, Q)), dma((R, Q)),
            dma((2 * R, Q)), dma((2 * R, Q)),
            dma((R, m, Q)), dma((C, Q)),
            dma((slots,)), dma((slots,)),
            dma((R, slots, C)), dma((R, slots, C)),
            dma((R, C)), dma((R, C)),
            dma((C,)), dma((C,)),
        ],
        compiler_params=pltpu.CompilerParams(collective_id=0, has_side_effects=True),
    )(integrals, amplitudes)


def swift(R, C, L, T, lo, i_ref, a_ref, o_ref,
          a_x, az, i_in, i_s, i_t, acc, last, core_buf, x_buf, z_buf, y_out, y_buf, last_buf, hi_buf, lo_buf,
          own, iown, asend, arecv, isend, irecv, zsend, zrecv,
          csend, crecv, xsend, xrecv, wsend, wrecv, ysend, yrecv, lsend, lrecv, hsend, hrecv, there):
    r, c, l = lax.axis_index("row"), lax.axis_index("col"), lax.axis_index("layer")
    K, V, M = i_ref.shape
    N = a_ref.shape[2]
    Kr = K // R
    W = Kr * V
    m = C // R
    rows = M // L
    half_rows = 2 * rows
    o = 1 - r
    x, core = lax.div(l, 2), lax.rem(l, 2)
    side = lax.div(c, m)
    home = side == r
    away = jnp.logical_not(home)
    outer = (c == 0) | (c == C - 1)
    inner = jnp.logical_not(outer)

    def remote(src, dst, ss, rs, **to):
        where = {"row": r, "col": c, "layer": l}
        where.update(to)
        return pltpu.make_async_remote_copy(src_ref=src, dst_ref=dst, send_sem=ss, recv_sem=rs,
                                            device_id=where, device_id_type=MESH)

    def landed(ref, sem):
        pltpu.make_async_copy(ref, ref, sem).wait()

    def signal(sem, **to):
        where = {"row": r, "col": c, "layer": l}
        where.update(to)
        pl.semaphore_signal(sem, inc=1, device_id=where, device_id_type=MESH)

    def at(start, size, unit=16):
        return pl.ds(pl.multiple_of(start, unit), size)

    sib, opp = l ^ 1, l ^ 2

    barrier = pltpu.get_barrier_semaphore()
    signal(barrier, row=o)
    signal(barrier, layer=sib)
    signal(barrier, layer=opp)

    @pl.when(c > 0)
    def _():
        signal(barrier, col=c - 1)

    @pl.when(c < C - 1)
    def _():
        signal(barrier, col=c + 1)

    pl.semaphore_wait(barrier, 3 + (c > 0).astype(jnp.int32) + (c < C - 1).astype(jnp.int32))

    def row_a(q, j):
        span = pl.ds(j * V, V)
        return remote(a_ref.at[o * Kr + q, span], a_x.at[q, span], asend, arecv.at[q, j], row=o)

    for q in range(Kr):
        for j in range(m):
            row_a(q, j).start()

    def col_start(d, *qs, js=range(m)):
        for q in qs:
            for j in js:
                b = (o if d else r) * m + j
                span = pl.ds(j * V, V)
                src = a_x.at[q, span] if d else a_ref.at[r * Kr + q, span]

                @pl.when(b != c)
                def _():
                    remote(src, az.at[c, q], zsend, zrecv.at[c], col=b).start()

    ahead, turnover = 3, Kr - 2

    @pl.when(home)
    def _():
        col_start(0, *range(ahead))

    @pl.when(home & inner)
    def _():
        col_start(0, *range(ahead, Kr))

    for t in range(2, C):
        @pl.when((c >= 1) & (c + t - 1 < C))
        def _():
            signal(there.at[0, t - 2], col=c - 1)

        @pl.when((c + 1 < C) & (c - t + 1 >= 0))
        def _():
            signal(there.at[1, t - 2], col=c + 1)

        @pl.when(c + t < C)
        def _():
            pl.semaphore_wait(there.at[0, t - 2], 1)

        @pl.when(c - t >= 0)
        def _():
            pl.semaphore_wait(there.at[1, t - 2], 1)

    @pl.when(away & outer)
    def _():
        col_start(0, *range(Kr))

    here_v = at(lax.rem(c, m) * V, V, V)

    def own_a(q, src):
        pltpu.make_async_copy(src.at[q, here_v], az.at[c, q], own).start()

    per = 2

    def own_k(n):
        return (r if n * per >= Kr else o) * Kr + n * per % Kr

    for n in range(K // per):
        pltpu.make_async_copy(i_ref.at[pl.ds(own_k(n), per)], i_in.at[pl.ds(n * per, per)], iown.at[n]).start()

    @pl.when(home)
    def _():
        for q in range(Kr):
            pltpu.make_async_copy(a_ref.at[r * Kr + q, here_v], az.at[c, q], own).start()

    other = (1 - x) * half_rows
    mine = x * half_rows
    first, middle, final = (T, lo - T), (lo, rows - lo), (0, T)

    def both(part):
        start, size = part
        return [(mine + start, size), (mine + rows + start, size)]

    groups = [(other, half_rows)] + both(first) + both(middle) + both(final)

    def row_i(g):
        start, size = groups[g]
        span = at(start, size)
        return remote(i_s.at[span], i_t.at[1, span], isend, irecv.at[(g + 1) // 2], row=o)

    def slab_wait(n):
        size = groups[2 * n - 1][1] * 2 if n else half_rows
        landed(i_t.at[1, pl.ds(0, size)], irecv.at[n])

    for q in range(Kr):
        for j in range(m):
            row_a(q, j).wait_recv()
            if q < turnover:
                @pl.when(outer | away)
                def _():
                    col_start(1, q, js=[j])
            else:
                col_start(1, q, js=[j])

        @pl.when(away)
        def _():
            own_a(q, a_x)

        if q == turnover:
            @pl.when(inner & home)
            def _():
                col_start(1, *range(turnover))

            @pl.when(inner & away)
            def _():
                col_start(0, *range(Kr))

            @pl.when(outer & home)
            def _():
                col_start(0, *range(ahead, Kr))

        if q < K // per:
            landed(i_in.at[pl.ds(q * per, per)], iown.at[q])
            for k in range(q * per, q * per + per):
                if k < Kr:
                    i_s[:, k * V:(k + 1) * V] = i_in[k].T
                else:
                    i_t[0, :, (k - Kr) * V:(k - Kr + 1) * V] = i_in[k].T
            if (q + 1) * per == Kr:
                for g in range(len(groups)):
                    row_i(g).start()

    cols = [side * m, side * m + 1, (1 - side) * (C - 1), 2 - side]
    near, wide, late = (0, 2), (2, 1), (3, 1)
    early = (0, 3)

    def pick(u):
        return cols[u[0]:u[0] + u[1]]

    def wait_piece(s):
        @pl.when(s == c)
        def _():
            landed(az.at[c], own)

        @pl.when(s != c)
        def _():
            landed(az.at[s], zrecv.at[s])

    def fill(d, u, spans, keep=None):
        left = [i_t[d, at(start, size)] for start, size in spans]
        left = left[0] if len(left) == 1 else jnp.concatenate(left, axis=0)
        right = [az[s].reshape(W, N) for s in pick(u)]
        right = right[0] if len(right) == 1 else jnp.concatenate(right, axis=1)
        piece = lax.dot_general(left, right, (((1,), (0,)), ((), ())), preferred_element_type=jnp.float32)
        for j, s in enumerate(pick(u)):
            done = 0
            for i, (start, size) in enumerate(spans):
                part = piece[done:done + size, j * N:(j + 1) * N]
                if keep is None:
                    acc[d, s, at(start, size)] = part
                else:
                    keep[i, s] = part
                done += size

    def from_to(u):
        return pl.ds(cols[u[0]], u[1]), pl.ds(u[0], u[1])

    def core_span(d, keep):
        return first if d and keep == 1 else middle if keep == 2 else (0, rows)

    def core_start(d, us, keep):
        start, size = core_span(d, keep)
        give = 2 * (x if keep else 1 - x) + 1 - core
        for u in us:
            src, dst = from_to(u)
            remote(acc.at[d, src, at(give * rows + start, size)], core_buf.at[d, min(keep, 1), dst, pl.ds(start, size)],
                   csend, crecv.at[d, us[0][0] // 3, keep], layer=sib).start()

    def core_end(d, us, keep):
        start, size = core_span(d, keep)
        have = 2 * (x if keep else 1 - x) + core
        slots = pl.ds(us[0][0], sum(u[1] for u in us))
        landed(core_buf.at[d, min(keep, 1), slots, pl.ds(start, size)], crecv.at[d, us[0][0] // 3, keep])
        for u in us:
            src, dst = from_to(u)
            acc[d, src, at(have * rows + start, size)] += core_buf[d, min(keep, 1), dst, start:start + size]

    def x_start(d, us):
        for u in us:
            src, dst = from_to(u)
            remote(acc.at[d, src, at((2 * (1 - x) + core) * rows, rows)], x_buf.at[d, dst],
                   xsend, xrecv.at[d, us[0][0] // 3], layer=opp).start()

    def x_wait(d, us):
        landed(x_buf.at[d, pl.ds(us[0][0], sum(u[1] for u in us))], xrecv.at[d, us[0][0] // 3])

    def x_add(d, us, start, size, add=True):
        for u in us:
            src, dst = from_to(u)
            where = at(l * rows + start, size)
            if add:
                acc[d, src, where] += x_buf[d, dst, start:start + size]
            else:
                acc[d, src, where] = x_buf[d, dst, start:start + size]

    def z_start(d, u):
        size = lo if d else rows
        for s in pick(u):
            slot = (c ^ s) - 1
            sem = wrecv.at[jnp.where(slot == 0, 1, 2)] if d else wrecv.at[0]

            @pl.when(s != c)
            def _():
                remote(acc.at[d, s, at(l * rows, size)], z_buf.at[d, slot, pl.ds(0, size)], wsend, sem, col=s).start()

    def hi_start(us):
        for u in us:
            for s in pick(u):
                remote(acc.at[1, s, at(l * rows + lo, rows - lo)], hi_buf.at[c], hsend, hrecv.at[0], row=o, col=s).start()

    def lo_start():
        s = cols[3]
        remote(acc.at[1, s, at(l * rows, lo)], lo_buf.at[lax.rem(c, m)], hsend, hrecv.at[1], row=o, col=s).start()

    most = (near, wide)
    for i in range(3):
        wait_piece(cols[i])
    for u in most:
        fill(0, u, [(0, M)])
    core_start(0, most, 0)
    core_start(0, most, 1)
    core_end(0, most, 0)
    x_start(0, most)
    core_end(0, most, 1)

    slab_wait(0)
    for u in most:
        fill(1, u, [(other, half_rows)])
    core_start(1, most, 0)
    x_wait(0, most)
    x_add(0, most, 0, rows)
    z_start(0, near)
    core_end(1, most, 0)
    x_start(1, most)

    wait_piece(cols[3])
    fill(0, late, [(other, half_rows)])
    core_start(0, [late], 0)
    fill(1, late, [(other, half_rows)])
    core_start(1, [late], 0)
    z_start(0, wide)
    core_end(0, [late], 0)
    x_start(0, [late])
    core_end(1, [late], 0)
    x_start(1, [late])
    fill(0, late, [(mine, half_rows)])
    core_start(0, [late], 1)

    slab_wait(1)
    for u in (near, (2, 2)):
        fill(1, u, both(first))
    core_start(1, most, 1)
    core_start(1, [late], 1)
    x_wait(1, most)
    core_end(0, [late], 1)
    core_end(1, most, 1)
    x_add(1, most, 0, T, add=False)
    x_add(1, most, T, lo - T)
    z_start(1, near)
    z_start(1, wide)
    core_end(1, [late], 1)
    x_wait(0, [late])
    x_add(0, [late], 0, rows)
    z_start(0, late)

    slab_wait(2)
    for u in (near, (2, 2)):
        fill(1, u, both(middle))
    core_start(1, most, 2)
    core_start(1, [late], 2)
    x_wait(1, [late])
    x_add(1, [late], 0, T, add=False)
    x_add(1, [late], T, lo - T)
    lo_start()
    core_end(1, most, 2)
    x_add(1, most, lo, rows - lo)
    hi_start(most)
    core_end(1, [late], 2)
    x_add(1, [late], lo, rows - lo)
    hi_start([late])

    slab_wait(3)
    for u in (near, (2, 2)):
        fill(1, u, both(final), keep=last)
    for dc in range(C):
        s = c ^ (C - 1 - dc)
        for i in range(2):
            remote(last.at[i, s], last_buf.at[core, c], lsend, lrecv, row=o, col=s, layer=2 * x + i).start()

    landed(z_buf.at[1, 0, pl.ds(0, lo)], wrecv.at[1])
    y_out[...] = acc[1, c, at(l * rows, lo)] + z_buf[1, 0, :lo]

    @pl.when(outer)
    def _():
        landed(z_buf.at[1, pl.ds(1, 2), pl.ds(0, lo)], wrecv.at[2])
        y_out[...] += z_buf[1, 1, :lo] + z_buf[1, 2, :lo]

    remote(y_out, y_buf, ysend, yrecv, row=o).start()

    landed(a_x, asend)
    landed(az.at[pl.ds(0, m + 1)], zsend)
    landed(i_s, isend)
    landed(acc.at[0, :, pl.ds(0, M - T)], csend)
    landed(acc.at[0, :, pl.ds(0, half_rows)], xsend)

    landed(z_buf.at[0], wrecv.at[0])
    total = acc[0, c, at(l * rows, rows)]
    for i in range(C - 1):
        total += z_buf[0, i]
    landed(y_buf, yrecv)
    o_ref[:lo] = total[:lo] + y_buf[...]

    @pl.when(inner)
    def _():
        landed(lo_buf, hrecv.at[1])
        o_ref[:lo] += lo_buf[0] + lo_buf[1]

    landed(hi_buf, hrecv.at[0])
    high = total[lo:]
    for s in range(C):
        high += hi_buf[s]
    o_ref[lo:] = high
    landed(last_buf, lrecv)
    tail = o_ref[:T]
    for i in range(2):
        for s in range(C):
            tail += last_buf[i, s]
    o_ref[:T] = tail

    landed(acc.at[0, 0, pl.ds(0, 3 * rows + 2 * lo)] if 3 * rows + 2 * lo <= M else acc.at[0, pl.ds(0, 2), pl.ds(0, (3 * rows + 2 * lo) // 2)],
           wsend)
    landed(acc.at[0, 0, pl.ds(0, C * (rows - lo) + lo)], hsend)
    landed(last, lsend)
    landed(y_out, ysend)


def swift_call(R, C, L, integrals, amplitudes):
    K, V, M = integrals.shape
    V_row, N = amplitudes.shape[1:]
    rows = M // L
    Kr = K // R
    m = C // R
    T = 16
    lo = rows * 5 // 6 // 16 * 16
    dma = pltpu.SemaphoreType.DMA
    f32, bf16 = jnp.float32, jnp.bfloat16
    anyspace = pl.BlockSpec(memory_space=pl.ANY)
    return pl.pallas_call(
        functools.partial(swift, R, C, L, T, lo),
        out_shape=jax.ShapeDtypeStruct((rows, N), f32),
        in_specs=[anyspace, anyspace],
        out_specs=pl.BlockSpec(memory_space=pltpu.VMEM),
        scratch_shapes=[
            pltpu.VMEM((Kr, V_row, N), bf16),
            pltpu.VMEM((C, Kr, V, N), bf16),
            pltpu.VMEM((K, V, M), bf16),
            pltpu.VMEM((M, Kr * V), bf16),
            pltpu.VMEM((2, M, Kr * V), bf16),
            pltpu.VMEM((2, C, M, N), f32),
            pltpu.VMEM((2, C, T, N), f32),
            pltpu.VMEM((2, 2, C, rows, N), f32),
            pltpu.VMEM((2, C, rows, N), f32),
            pltpu.VMEM((2, C - 1, rows, N), f32),
            pltpu.VMEM((lo, N), f32),
            pltpu.VMEM((lo, N), f32),
            pltpu.VMEM((2, C, T, N), f32),
            pltpu.VMEM((C, rows - lo, N), f32),
            pltpu.VMEM((m, lo, N), f32),
            dma, dma((Kr,)),
            dma, dma((Kr, m)),
            dma, dma((4,)),
            dma, dma((C,)),
            dma, dma((2, 2, 3)),
            dma, dma((2, 2)),
            dma, dma((3,)),
            dma, dma,
            dma, dma,
            dma, dma((2,)),
            pltpu.SemaphoreType.REGULAR((2, C - 2)),
        ],
        compiler_params=pltpu.CompilerParams(collective_id=0, has_side_effects=True),
    )(integrals, amplitudes)


def local(R, C, L, integrals, amplitudes, coulomb, row_gap, col_gap):
    swift_fits = R == 2 and C == 4 and L == 4 and integrals.shape[2] % (16 * L) == 0
    call = swift_call if swift_fits else general_call
    own_rows = call(R, C, L, integrals, amplitudes)
    gap_sum = row_gap[:, None] + col_gap[None, :]
    return (coulomb.astype(jnp.float32) + own_rows) / gap_sum


def solution(mesh):
    R, C, L = (mesh.shape[a] for a in ("row", "col", "layer"))
    placed = (
        P("layer", "col", "row"),
        P("layer", "row", "col"),
        P(("row", "layer"), "col"),
        P(("row", "layer")),
        P("col"),
    )
    return jax.shard_map(
        functools.partial(local, R, C, L), mesh=mesh, in_specs=placed, out_specs=P(("row", "layer"), "col"),
        check_vma=False,
    )
```

```python
import functools

import jax
import jax.numpy as jnp
from jax import lax
from jax.experimental import pallas as pl
from jax.experimental.pallas import tpu as pltpu
from jax.sharding import PartitionSpec as P

MESH = pl.DeviceIdType.MESH


def hi_order(n):
    if n == 1:
        return [0]
    below = hi_order(n // 2)
    return [2 * x + 1 for x in below] + [2 * x for x in below]


def kernel(R, C, L, Q, i_ref, a_ref, o_ref,
           a_all, az, i_all, i_t, acc, lay_buf, row_buf, col_buf,
           asend, arecv, xsend, xrecv, zsend, zrecv,
           osend, orecv, lsend, lrecv, rsend, rrecv, csend, crecv):
    r, c, l = lax.axis_index("row"), lax.axis_index("col"), lax.axis_index("layer")
    K, V_row, N = a_ref.shape
    V, M = i_ref.shape[1:]
    Kr = K // R
    kc = Kr // Q
    m = C // R
    w = kc * V
    rows = M // L
    stages = L.bit_length() - 1
    late = M // 2 // 128 * 128 if stages == 2 and M % 128 == 0 else 0
    early = M - late
    top = l >> (stages - 1)

    def remote(src, dst, ss, rs, **to):
        where = {"row": r, "col": c, "layer": l}
        where.update(to)
        return pltpu.make_async_remote_copy(src_ref=src, dst_ref=dst, send_sem=ss, recv_sem=rs,
                                            device_id=where, device_id_type=MESH)

    def ks(q):
        return pl.ds(q * kc, kc)

    def far_row(d):
        return lax.rem(r + d, R)

    def near(dc):
        return lax.rem(c + dc + C, C)

    order = sorted(range(1, C), key=lambda d: -min(d, C - d))

    def slice_for(d, q):
        return pl.ds(far_row(d) * Kr + q * kc, kc)

    def own_a(q):
        return pltpu.make_async_copy(a_ref.at[slice_for(0, q)], a_all.at[0, ks(q)], arecv.at[0, q])

    def own_i(q):
        return pltpu.make_async_copy(i_ref.at[slice_for(0, q)], i_all.at[0, ks(q)], xrecv.at[0, q])

    for q in range(Q):
        own_a(q).start()
        own_i(q).start()

    barrier = pltpu.get_barrier_semaphore()
    partners = [{"row": far_row(d), "col": near(dc)} for d in range(R) for dc in range(C) if d or dc]
    partners += [{"layer": l ^ (1 << t)} for t in range(stages)]
    for p in partners:
        where = {"row": r, "col": c, "layer": l}
        where.update(p)
        pl.semaphore_signal(barrier, inc=1, device_id=where, device_id_type=MESH)
    pl.semaphore_wait(barrier, len(partners))

    def row_a(d, q):
        return remote(a_ref.at[slice_for(d, q)], a_all.at[R - d, ks(q)], asend.at[d, q], arecv.at[R - d, q], row=far_row(d))

    parts = [(0, early, (1 - top) * late)] + ([(early, late, top * early)] if late else [])

    def row_i(d, q, p):
        at, size, start = parts[p]
        src = i_ref.at[slice_for(d, q), :, pl.ds(pl.multiple_of(start, 128), size)] if late else i_ref.at[slice_for(d, q)]
        return remote(src, i_all.at[R - d, ks(q), :, pl.ds(at, size)], xsend.at[p * R + d, q], xrecv.at[p * R + R - d, q],
                      row=far_row(d))

    def col_a(d, j, q):
        b = far_row(d) * m + j
        at = pl.ds(j * V, V)
        src = a_all.at[d, ks(q), at] if d else a_ref.at[slice_for(0, q), at]
        return b, remote(src, az.at[c, ks(q)], zsend.at[d, j, q], zrecv.at[c, q], col=b)

    def col_start(d, q):
        for j in range(m):
            b, cp = col_a(d, j, q)

            @pl.when(b != c)
            def _():
                cp.start()

    for q in range(Q):
        for d in range(1, R):
            row_a(d, q).start()
        col_start(0, q)
    for p in range(len(parts)):
        for q in range(Q):
            for d in range(1, R):
                row_i(d, q, p).start()

    whole = (0, M, 0)

    def turn(d, q, part):
        first, size = part[:2]
        for k in range(kc):
            at = (q * kc + k) * V
            i_t[d, first:first + size, at:at + V] = i_all[d, q * kc + k, :, first:first + size].T

    def add(d, block, x, q, part):
        first, size, start = part
        piece = lax.dot_general(i_t[d, first:first + size, q * w:(q + 1) * w], x, (((1,), (0,)), ((), ())),
                                preferred_element_type=jnp.float32)
        to = pl.ds(start if isinstance(start, int) else pl.multiple_of(start, 128), size)
        if q == 0:
            acc[d, block, to] = piece
        else:
            acc[d, block, to] += piece

    own_row = lax.rem(lax.div(c, m) - r + R, R)
    own_at = pl.ds(pl.multiple_of(lax.rem(c, m) * V, V), V)

    def own_block(d, q, part):
        add(d, c, a_all[own_row, ks(q), own_at].reshape(w, N), q, part)

    for q in range(Q):
        own_a(q).wait()
        for d in range(1, R):
            row_a(R - d, q).wait_recv()
            col_start(d, q)
        own_i(q).wait()
        turn(0, q, whole)
        own_block(0, q, whole)

    for q in range(Q):
        for dc in order[::-1]:
            s = near(dc)
            here = az.at[s, ks(q)]
            remote(here, here, zsend.at[0, 0, q], zrecv.at[s, q], col=s).wait_recv()
            add(0, s, az[s, ks(q)].reshape(w, N), q, whole)

    def block(t, hi, bit):
        return (hi << (t + 1)) | (bit << t) | (l & ((1 << t) - 1))

    def halving(d, t, i, col):
        n = L >> (t + 1)
        hi = (l >> (t + 1)) ^ hi_order(n)[i]
        bit = (l >> t) & 1
        slot = n - 1 + hi
        give, keep = block(t, hi, 1 - bit), block(t, hi, bit)
        give, keep = (pl.ds(pl.multiple_of(b * rows, 8), rows) for b in (give, keep))
        if d == 0:
            cp = remote(acc.at[0, :, give], lay_buf.at[0, slot], osend.at[slot], orecv.at[slot], layer=l ^ (1 << t))
        else:
            cp = remote(acc.at[d, col, give], lay_buf.at[d, slot, col], lsend.at[d, slot, col], lrecv.at[d, slot, col],
                        layer=l ^ (1 << t))
        return cp, keep, slot

    def own_stage(t):
        for i in range(L >> (t + 1)):
            cp, keep, slot = halving(0, t, i, None)
            cp.wait_recv()
            acc[0, :, keep] += lay_buf[0, slot]
            if t + 1 < stages and i < L >> (t + 2):
                halving(0, t + 1, i, None)[0].start()

    for i in range(L >> 1):
        halving(0, 0, i, None)[0].start()

    c_order = [near(dc) for dc in order] + [c]
    mine = pl.ds(pl.multiple_of(l * rows, 8), rows)

    def first_stage_start(i):
        for d in range(1, R):
            for col in c_order:
                halving(d, 0, i, col)[0].start()

    def stage_end(t, i):
        for d in range(1, R):
            for col in c_order:
                cp, keep, slot = halving(d, t, i, col)
                cp.wait_recv()
                acc[d, col, keep] += lay_buf[d, slot, col]
                if t + 1 == stages:
                    row_sum(d, col).start()
                elif i < L >> (t + 2):
                    halving(d, t + 1, i, col)[0].start()

    for p, part in enumerate(parts):
        for q in range(Q):
            for d in range(1, R):
                row_i(R - d, q, p).wait_recv()
                turn(d, q, part)
                own_block(d, q, part)
                for dc in order:
                    s = near(dc)
                    add(d, s, az[s, ks(q)].reshape(w, N), q, part)
            if p == 0 and q == 0:
                own_stage(0)
            if p == 1 and q == min(1, Q - 1):
                stage_end(0, 0)
        if late:
            first_stage_start(p)

    def row_sum(d, col):
        return remote(acc.at[d, col, mine], row_buf.at[R - d, c], rsend.at[d, col], rrecv.at[R - d, c],
                      row=far_row(d), col=col)

    def col_sum(dc):
        return remote(acc.at[0, near(dc), mine], col_buf.at[c], csend.at[dc], crecv.at[c], col=near(dc))

    if not late:
        for i in range(L >> 1):
            first_stage_start(i)
    for t in range(1, stages):
        own_stage(t)
    for dc in order:
        col_sum(dc).start()
    for t in range(stages):
        for i in range(L >> (t + 1)):
            if not (late and t == 0 and i == 0):
                stage_end(t, i)
    total = acc[0, c, mine]
    for dc in order[::-1]:
        s = near(dc)
        remote(col_buf.at[s], col_buf.at[s], csend.at[dc], crecv.at[s], col=s).wait_recv()
        total += col_buf[s]
    for col in c_order[::-1]:
        for d in range(1, R):
            here = row_buf.at[d, col]
            remote(here, here, rsend.at[d, col], rrecv.at[d, col], row=far_row(d), col=col).wait_recv()
            total += row_buf[d, col]
    o_ref[...] = total

    for q in range(Q):
        for d in range(R):
            if d:
                row_a(d, q).wait_send()
                for p in range(len(parts)):
                    row_i(d, q, p).wait_send()
            for j in range(m):
                b, cp = col_a(d, j, q)

                @pl.when(b != c)
                def _():
                    cp.wait_send()
    for t in range(stages):
        for i in range(L >> (t + 1)):
            halving(0, t, i, None)[0].wait_send()
            for d in range(1, R):
                for col in c_order:
                    halving(d, t, i, col)[0].wait_send()
    for col in c_order:
        for d in range(1, R):
            row_sum(d, col).wait_send()
    for dc in order:
        col_sum(dc).wait_send()


def general_call(R, C, L, integrals, amplitudes):
    K, V, M = integrals.shape
    V_row, N = amplitudes.shape[1:]
    rows = M // L
    Kr = K // R
    Q = Kr
    m = C // R
    slots = L - 1
    dma = pltpu.SemaphoreType.DMA
    vmem = pl.BlockSpec(memory_space=pltpu.VMEM)
    anyspace = pl.BlockSpec(memory_space=pl.ANY)
    return pl.pallas_call(
        functools.partial(kernel, R, C, L, Q),
        out_shape=jax.ShapeDtypeStruct((rows, N), jnp.float32),
        in_specs=[anyspace, anyspace],
        out_specs=vmem,
        scratch_shapes=[
            pltpu.VMEM((R, Kr, V_row, N), jnp.bfloat16),
            pltpu.VMEM((C, Kr, V, N), jnp.bfloat16),
            pltpu.VMEM((R, Kr, V, M), jnp.bfloat16),
            pltpu.VMEM((R, M, Kr * V), jnp.bfloat16),
            pltpu.VMEM((R, C, M, N), jnp.float32),
            pltpu.VMEM((R, slots, C, rows, N), jnp.float32),
            pltpu.VMEM((R, C, rows, N), jnp.float32),
            pltpu.VMEM((C, rows, N), jnp.float32),
            dma((R, Q)), dma((R, Q)),
            dma((2 * R, Q)), dma((2 * R, Q)),
            dma((R, m, Q)), dma((C, Q)),
            dma((slots,)), dma((slots,)),
            dma((R, slots, C)), dma((R, slots, C)),
            dma((R, C)), dma((R, C)),
            dma((C,)), dma((C,)),
        ],
        compiler_params=pltpu.CompilerParams(collective_id=0, has_side_effects=True),
    )(integrals, amplitudes)


def swift(R, C, L, T, lo, i_ref, a_ref, o_ref,
          a_x, az, i_in, i_s, i_t, acc, last, core_buf, x_buf, p_buf, z_buf, y_out, y_buf, last_buf, hi_buf, lo_buf,
          own, iown, asend, arecv, isend, irecv, zsend, zrecv,
          csend, crecv, xsend, xrecv, wsend, precv, wrecv, ysend, yrecv, lsend, lrecv, hsend, hrecv, there):
    r, c, l = lax.axis_index("row"), lax.axis_index("col"), lax.axis_index("layer")
    K, V, M = i_ref.shape
    N = a_ref.shape[2]
    Kr = K // R
    W = Kr * V
    m = C // R
    rows = M // L
    half_rows = 2 * rows
    o = 1 - r
    x, core = lax.div(l, 2), lax.rem(l, 2)
    side = lax.div(c, m)
    home = side == r
    away = jnp.logical_not(home)
    outer = (c == 0) | (c == C - 1)
    inner = jnp.logical_not(outer)

    def remote(src, dst, ss, rs, **to):
        where = {"row": r, "col": c, "layer": l}
        where.update(to)
        return pltpu.make_async_remote_copy(src_ref=src, dst_ref=dst, send_sem=ss, recv_sem=rs,
                                            device_id=where, device_id_type=MESH)

    def landed(ref, sem):
        pltpu.make_async_copy(ref, ref, sem).wait()

    def signal(sem, **to):
        where = {"row": r, "col": c, "layer": l}
        where.update(to)
        pl.semaphore_signal(sem, inc=1, device_id=where, device_id_type=MESH)

    def at(start, size, unit=16):
        return pl.ds(pl.multiple_of(start, unit), size)

    sib, opp = l ^ 1, l ^ 2

    barrier = pltpu.get_barrier_semaphore()
    signal(barrier, row=o)
    signal(barrier, layer=sib)
    signal(barrier, layer=opp)

    @pl.when(c > 0)
    def _():
        signal(barrier, col=c - 1)

    @pl.when(c < C - 1)
    def _():
        signal(barrier, col=c + 1)

    pl.semaphore_wait(barrier, 3 + (c > 0).astype(jnp.int32) + (c < C - 1).astype(jnp.int32))

    def row_a(q, j):
        span = pl.ds(j * V, V)
        return remote(a_ref.at[o * Kr + q, span], a_x.at[q, span], asend, arecv.at[q, j], row=o)

    for q in range(Kr):
        for j in range(m):
            row_a(q, j).start()

    def col_start(d, *qs, js=range(m)):
        for q in qs:
            for j in js:
                b = (o if d else r) * m + j
                span = pl.ds(j * V, V)
                src = a_x.at[q, span] if d else a_ref.at[r * Kr + q, span]

                @pl.when(b != c)
                def _():
                    remote(src, az.at[c, q], zsend, zrecv.at[c], col=b).start()

    ahead, hold, turnover = 3, 2, Kr - 2

    @pl.when(home)
    def _():
        col_start(0, *range(ahead))

    @pl.when(home & inner)
    def _():
        col_start(0, *range(ahead, Kr))

    for t in range(2, C):
        @pl.when((c >= 1) & (c + t - 1 < C))
        def _():
            signal(there.at[0, t - 2], col=c - 1)

        @pl.when((c + 1 < C) & (c - t + 1 >= 0))
        def _():
            signal(there.at[1, t - 2], col=c + 1)

        @pl.when(c + t < C)
        def _():
            pl.semaphore_wait(there.at[0, t - 2], 1)

        @pl.when(c - t >= 0)
        def _():
            pl.semaphore_wait(there.at[1, t - 2], 1)

    @pl.when(away)
    def _():
        col_start(0, *range(hold))

    @pl.when(away & outer)
    def _():
        col_start(0, *range(hold, Kr))

    here_v = at(lax.rem(c, m) * V, V, V)

    def own_a(q, src):
        pltpu.make_async_copy(src.at[q, here_v], az.at[c, q], own).start()

    per = 2

    def own_k(n):
        return (r if n * per >= Kr else o) * Kr + n * per % Kr

    for n in range(K // per):
        pltpu.make_async_copy(i_ref.at[pl.ds(own_k(n), per)], i_in.at[pl.ds(n * per, per)], iown.at[n]).start()

    @pl.when(home)
    def _():
        for q in range(Kr):
            pltpu.make_async_copy(a_ref.at[r * Kr + q, here_v], az.at[c, q], own).start()

    other = (1 - x) * half_rows
    mine = x * half_rows
    first, middle, final = (T, lo - T), (lo, rows - lo), (0, T)

    def both(part):
        start, size = part
        return [(mine + start, size), (mine + rows + start, size)]

    groups = [(other, half_rows)] + both(first) + both(middle) + both(final)

    def row_i(g):
        start, size = groups[g]
        span = at(start, size)
        return remote(i_s.at[span], i_t.at[1, span], isend, irecv.at[(g + 1) // 2], row=o)

    def slab_wait(n):
        size = groups[2 * n - 1][1] * 2 if n else half_rows
        landed(i_t.at[1, pl.ds(0, size)], irecv.at[n])

    for q in range(Kr):
        for j in range(m):
            row_a(q, j).wait_recv()
            if hold <= q < turnover:
                @pl.when(outer | away)
                def _():
                    col_start(1, q, js=[j])
            else:
                col_start(1, q, js=[j])

        @pl.when(away)
        def _():
            own_a(q, a_x)

        if q == turnover:
            @pl.when(inner & home)
            def _():
                col_start(1, *range(hold, turnover))

            @pl.when(inner & away)
            def _():
                col_start(0, *range(hold, Kr))

            @pl.when(outer & home)
            def _():
                col_start(0, *range(ahead, Kr))

        if q < K // per:
            landed(i_in.at[pl.ds(q * per, per)], iown.at[q])
            for k in range(q * per, q * per + per):
                if k < Kr:
                    i_s[:, k * V:(k + 1) * V] = i_in[k].T
                else:
                    i_t[0, :, (k - Kr) * V:(k - Kr + 1) * V] = i_in[k].T
            if (q + 1) * per == Kr:
                for g in range(len(groups)):
                    row_i(g).start()

    cols = [side * m, side * m + 1, (1 - side) * (C - 1), 2 - side]
    near, wide, late = (0, 2), (2, 1), (3, 1)
    early = (0, 3)

    def pick(u):
        return cols[u[0]:u[0] + u[1]]

    def wait_piece(s):
        @pl.when(s == c)
        def _():
            landed(az.at[c], own)

        @pl.when(s != c)
        def _():
            landed(az.at[s], zrecv.at[s])

    def fill(d, u, spans, keep=None):
        left = [i_t[d, at(start, size)] for start, size in spans]
        left = left[0] if len(left) == 1 else jnp.concatenate(left, axis=0)
        right = [az[s].reshape(W, N) for s in pick(u)]
        right = right[0] if len(right) == 1 else jnp.concatenate(right, axis=1)
        piece = lax.dot_general(left, right, (((1,), (0,)), ((), ())), preferred_element_type=jnp.float32)
        for j, s in enumerate(pick(u)):
            done = 0
            for i, (start, size) in enumerate(spans):
                part = piece[done:done + size, j * N:(j + 1) * N]
                if keep is None:
                    acc[d, s, at(start, size)] = part
                else:
                    keep[i, s] = part
                done += size

    def from_to(u):
        return pl.ds(cols[u[0]], u[1]), pl.ds(u[0], u[1])

    def core_span(d, keep):
        return first if d and keep == 1 else middle if keep == 2 else (0, rows)

    def core_start(d, us, keep):
        start, size = core_span(d, keep)
        give = 2 * (x if keep else 1 - x) + 1 - core
        for u in us:
            src, dst = from_to(u)
            remote(acc.at[d, src, at(give * rows + start, size)], core_buf.at[d, min(keep, 1), dst, pl.ds(start, size)],
                   csend, crecv.at[d, us[0][0] // 3, keep], layer=sib).start()

    def core_end(d, us, keep):
        start, size = core_span(d, keep)
        have = 2 * (x if keep else 1 - x) + core
        slots = pl.ds(us[0][0], sum(u[1] for u in us))
        landed(core_buf.at[d, min(keep, 1), slots, pl.ds(start, size)], crecv.at[d, us[0][0] // 3, keep])
        for u in us:
            src, dst = from_to(u)
            acc[d, src, at(have * rows + start, size)] += core_buf[d, min(keep, 1), dst, start:start + size]

    def x_start(d, us):
        for u in us:
            src, dst = from_to(u)
            remote(acc.at[d, src, at((2 * (1 - x) + core) * rows, rows)], x_buf.at[d, dst],
                   xsend, xrecv.at[d, us[0][0] // 3], layer=opp).start()

    def x_wait(d, us):
        landed(x_buf.at[d, pl.ds(us[0][0], sum(u[1] for u in us))], xrecv.at[d, us[0][0] // 3])

    def x_add(d, us, start, size, add=True):
        for u in us:
            src, dst = from_to(u)
            where = at(l * rows + start, size)
            if add:
                acc[d, src, where] += x_buf[d, dst, start:start + size]
            else:
                acc[d, src, where] = x_buf[d, dst, start:start + size]

    def z_start(d, s):
        size, slot = lo if d else rows, (c ^ s) - 1
        sem = wrecv.at[d, jnp.where(slot == 0, 0, 1)]
        remote(acc.at[d, s, at(l * rows, size)], z_buf.at[d, slot, pl.ds(0, size)], wsend, sem, col=s).start()

    def lean(d, s):
        @pl.when(outer)
        def _():
            remote(acc.at[d, s, at(l * rows, rows)], p_buf, wsend, precv, col=c ^ 1).start()

    def across(d, s):
        @pl.when(inner)
        def _():
            landed(p_buf, precv)
            acc[d, s, at(l * rows, rows)] += p_buf[...]
            z_start(d, s)

    def hi_start(us):
        for u in us:
            for s in pick(u):
                remote(acc.at[1, s, at(l * rows + lo, rows - lo)], hi_buf.at[c], hsend, hrecv.at[0], row=o, col=s).start()

    def lo_start():
        s = cols[3]
        remote(acc.at[1, s, at(l * rows, lo)], lo_buf.at[lax.rem(c, m)], hsend, hrecv.at[1], row=o, col=s).start()

    most = (near, wide)
    for i in range(3):
        wait_piece(cols[i])
    for u in most:
        fill(0, u, [(0, M)])
    core_start(0, most, 0)
    core_start(0, most, 1)
    core_end(0, most, 0)
    x_start(0, most)
    core_end(0, most, 1)

    slab_wait(0)
    for u in most:
        fill(1, u, [(other, half_rows)])
    core_start(1, most, 0)
    x_wait(0, most)
    x_add(0, most, 0, rows)
    z_start(0, c ^ 1)
    lean(0, cols[2])
    core_end(1, most, 0)
    x_start(1, most)

    wait_piece(cols[3])
    fill(0, late, [(other, half_rows)])
    core_start(0, [late], 0)
    fill(1, late, [(other, half_rows)])
    core_start(1, [late], 0)
    across(0, cols[2])
    core_end(0, [late], 0)
    x_start(0, [late])
    core_end(1, [late], 0)
    x_start(1, [late])
    fill(0, late, [(mine, half_rows)])
    core_start(0, [late], 1)

    slab_wait(1)
    for u in (near, (2, 2)):
        fill(1, u, both(first))
    core_start(1, most, 1)
    core_start(1, [late], 1)
    core_end(0, [late], 1)
    x_wait(0, [late])
    x_add(0, [late], 0, rows)
    z_start(0, cols[3])
    x_wait(1, most)
    core_end(1, most, 1)
    x_add(1, most, 0, T, add=False)
    x_add(1, most, T, lo - T)
    z_start(1, cols[2])
    z_start(1, c ^ 1)
    core_end(1, [late], 1)
    x_wait(1, [late])
    x_add(1, [late], 0, T, add=False)
    x_add(1, [late], T, lo - T)
    lo_start()

    slab_wait(2)
    for u in (near, (2, 2)):
        fill(1, u, both(middle))
    core_start(1, most, 2)
    core_start(1, [late], 2)
    core_end(1, most, 2)
    x_add(1, most, lo, rows - lo)
    hi_start(most)
    core_end(1, [late], 2)
    x_add(1, [late], lo, rows - lo)
    hi_start([late])

    slab_wait(3)
    for u in (near, (2, 2)):
        fill(1, u, both(final), keep=last)
    for dc in range(C):
        s = c ^ (C - 1 - dc)
        for i in range(2):
            remote(last.at[i, s], last_buf.at[core, c], lsend, lrecv, row=o, col=s, layer=2 * x + i).start()

    landed(z_buf.at[1, 0, pl.ds(0, lo)], wrecv.at[1, 0])
    y_out[...] = acc[1, c, at(l * rows, lo)] + z_buf[1, 0, :lo]

    @pl.when(outer)
    def _():
        landed(z_buf.at[1, pl.ds(1, 2), pl.ds(0, lo)], wrecv.at[1, 1])
        y_out[...] += z_buf[1, 1, :lo] + z_buf[1, 2, :lo]

    remote(y_out, y_buf, ysend, yrecv, row=o).start()

    landed(a_x, asend)
    landed(az.at[pl.ds(0, m + 1)], zsend)
    landed(i_s, isend)
    landed(acc.at[0, :, pl.ds(0, M - T)], csend)
    landed(acc.at[0, :, pl.ds(0, half_rows)], xsend)

    landed(z_buf.at[0, 0], wrecv.at[0, 0])
    o_ref[...] = acc[0, c, at(l * rows, rows)] + z_buf[0, 0]

    @pl.when(outer)
    def _():
        landed(z_buf.at[0, 0], wrecv.at[0, 1])
        o_ref[...] += z_buf[0, 1]

    @pl.when(inner)
    def _():
        landed(z_buf.at[0, pl.ds(1, 2)], wrecv.at[0, 1])
        o_ref[...] += z_buf[0, 1] + z_buf[0, 2]
        landed(lo_buf, hrecv.at[1])
        o_ref[:lo] += lo_buf[0] + lo_buf[1]

    landed(hi_buf, hrecv.at[0])
    high = o_ref[lo:]
    for s in range(C):
        high += hi_buf[s]
    o_ref[lo:] = high
    landed(last_buf, lrecv)
    tail = o_ref[:T]
    for i in range(2):
        for s in range(C):
            tail += last_buf[i, s]
    o_ref[:T] = tail
    landed(y_buf, yrecv)
    o_ref[:lo] += y_buf[...]

    landed(acc.at[0, 0, pl.ds(0, 3 * rows + 2 * lo)] if 3 * rows + 2 * lo <= M else acc.at[0, pl.ds(0, 2), pl.ds(0, (3 * rows + 2 * lo) // 2)],
           wsend)
    landed(acc.at[0, 0, pl.ds(0, C * (rows - lo) + lo)], hsend)
    landed(last, lsend)
    landed(y_out, ysend)


def swift_call(R, C, L, integrals, amplitudes):
    K, V, M = integrals.shape
    V_row, N = amplitudes.shape[1:]
    rows = M // L
    Kr = K // R
    m = C // R
    T = 16
    lo = rows * 5 // 6 // 16 * 16
    dma = pltpu.SemaphoreType.DMA
    f32, bf16 = jnp.float32, jnp.bfloat16
    anyspace = pl.BlockSpec(memory_space=pl.ANY)
    return pl.pallas_call(
        functools.partial(swift, R, C, L, T, lo),
        out_shape=pltpu.VMEM((rows, N), f32),
        in_specs=[anyspace, anyspace],
        out_specs=pl.BlockSpec(memory_space=pltpu.VMEM),
        scratch_shapes=[
            pltpu.VMEM((Kr, V_row, N), bf16),
            pltpu.VMEM((C, Kr, V, N), bf16),
            pltpu.VMEM((K, V, M), bf16),
            pltpu.VMEM((M, Kr * V), bf16),
            pltpu.VMEM((2, M, Kr * V), bf16),
            pltpu.VMEM((2, C, M, N), f32),
            pltpu.VMEM((2, C, T, N), f32),
            pltpu.VMEM((2, 2, C, rows, N), f32),
            pltpu.VMEM((2, C, rows, N), f32),
            pltpu.VMEM((rows, N), f32),
            pltpu.VMEM((2, C - 1, rows, N), f32),
            pltpu.VMEM((lo, N), f32),
            pltpu.VMEM((lo, N), f32),
            pltpu.VMEM((2, C, T, N), f32),
            pltpu.VMEM((C, rows - lo, N), f32),
            pltpu.VMEM((m, lo, N), f32),
            dma, dma((Kr,)),
            dma, dma((Kr, m)),
            dma, dma((4,)),
            dma, dma((C,)),
            dma, dma((2, 2, 3)),
            dma, dma((2, 2)),
            dma, dma, dma((2, 2)),
            dma, dma,
            dma, dma,
            dma, dma((2,)),
            pltpu.SemaphoreType.REGULAR((2, C - 2)),
        ],
        compiler_params=pltpu.CompilerParams(collective_id=0, has_side_effects=True),
    )(integrals, amplitudes)


def local(R, C, L, integrals, amplitudes, coulomb, row_gap, col_gap):
    swift_fits = R == 2 and C == 4 and L == 4 and integrals.shape[2] % (16 * L) == 0
    call = swift_call if swift_fits else general_call
    own_rows = call(R, C, L, integrals, amplitudes)
    gap_sum = row_gap[:, None] + col_gap[None, :]
    return (coulomb.astype(jnp.float32) + own_rows) / gap_sum


def solution(mesh):
    R, C, L = (mesh.shape[a] for a in ("row", "col", "layer"))
    placed = (
        P("layer", "col", "row"),
        P("layer", "row", "col"),
        P(("row", "layer"), "col"),
        P(("row", "layer")),
        P("col"),
    )
    return jax.shard_map(
        functools.partial(local, R, C, L), mesh=mesh, in_specs=placed, out_specs=P(("row", "layer"), "col"),
        check_vma=False,
    )
```

```python
import functools

import jax
import jax.numpy as jnp
from jax import lax
from jax.experimental import pallas as pl
from jax.experimental.pallas import tpu as pltpu
from jax.sharding import PartitionSpec as P

MESH = pl.DeviceIdType.MESH


def hi_order(n):
    if n == 1:
        return [0]
    below = hi_order(n // 2)
    return [2 * x + 1 for x in below] + [2 * x for x in below]


def kernel(R, C, L, Q, i_ref, a_ref, o_ref,
           a_all, az, i_all, i_t, acc, lay_buf, row_buf, col_buf,
           asend, arecv, xsend, xrecv, zsend, zrecv,
           osend, orecv, lsend, lrecv, rsend, rrecv, csend, crecv):
    r, c, l = lax.axis_index("row"), lax.axis_index("col"), lax.axis_index("layer")
    K, V_row, N = a_ref.shape
    V, M = i_ref.shape[1:]
    Kr = K // R
    kc = Kr // Q
    m = C // R
    w = kc * V
    rows = M // L
    stages = L.bit_length() - 1
    late = M // 2 // 128 * 128 if stages == 2 and M % 128 == 0 else 0
    early = M - late
    top = l >> (stages - 1)

    def remote(src, dst, ss, rs, **to):
        where = {"row": r, "col": c, "layer": l}
        where.update(to)
        return pltpu.make_async_remote_copy(src_ref=src, dst_ref=dst, send_sem=ss, recv_sem=rs,
                                            device_id=where, device_id_type=MESH)

    def ks(q):
        return pl.ds(q * kc, kc)

    def far_row(d):
        return lax.rem(r + d, R)

    def near(dc):
        return lax.rem(c + dc + C, C)

    order = sorted(range(1, C), key=lambda d: -min(d, C - d))

    def slice_for(d, q):
        return pl.ds(far_row(d) * Kr + q * kc, kc)

    def own_a(q):
        return pltpu.make_async_copy(a_ref.at[slice_for(0, q)], a_all.at[0, ks(q)], arecv.at[0, q])

    def own_i(q):
        return pltpu.make_async_copy(i_ref.at[slice_for(0, q)], i_all.at[0, ks(q)], xrecv.at[0, q])

    for q in range(Q):
        own_a(q).start()
        own_i(q).start()

    barrier = pltpu.get_barrier_semaphore()
    partners = [{"row": far_row(d), "col": near(dc)} for d in range(R) for dc in range(C) if d or dc]
    partners += [{"layer": l ^ (1 << t)} for t in range(stages)]
    for p in partners:
        where = {"row": r, "col": c, "layer": l}
        where.update(p)
        pl.semaphore_signal(barrier, inc=1, device_id=where, device_id_type=MESH)
    pl.semaphore_wait(barrier, len(partners))

    def row_a(d, q):
        return remote(a_ref.at[slice_for(d, q)], a_all.at[R - d, ks(q)], asend.at[d, q], arecv.at[R - d, q], row=far_row(d))

    parts = [(0, early, (1 - top) * late)] + ([(early, late, top * early)] if late else [])

    def row_i(d, q, p):
        at, size, start = parts[p]
        src = i_ref.at[slice_for(d, q), :, pl.ds(pl.multiple_of(start, 128), size)] if late else i_ref.at[slice_for(d, q)]
        return remote(src, i_all.at[R - d, ks(q), :, pl.ds(at, size)], xsend.at[p * R + d, q], xrecv.at[p * R + R - d, q],
                      row=far_row(d))

    def col_a(d, j, q):
        b = far_row(d) * m + j
        at = pl.ds(j * V, V)
        src = a_all.at[d, ks(q), at] if d else a_ref.at[slice_for(0, q), at]
        return b, remote(src, az.at[c, ks(q)], zsend.at[d, j, q], zrecv.at[c, q], col=b)

    def col_start(d, q):
        for j in range(m):
            b, cp = col_a(d, j, q)

            @pl.when(b != c)
            def _():
                cp.start()

    for q in range(Q):
        for d in range(1, R):
            row_a(d, q).start()
        col_start(0, q)
    for p in range(len(parts)):
        for q in range(Q):
            for d in range(1, R):
                row_i(d, q, p).start()

    whole = (0, M, 0)

    def turn(d, q, part):
        first, size = part[:2]
        for k in range(kc):
            at = (q * kc + k) * V
            i_t[d, first:first + size, at:at + V] = i_all[d, q * kc + k, :, first:first + size].T

    def add(d, block, x, q, part):
        first, size, start = part
        piece = lax.dot_general(i_t[d, first:first + size, q * w:(q + 1) * w], x, (((1,), (0,)), ((), ())),
                                preferred_element_type=jnp.float32)
        to = pl.ds(start if isinstance(start, int) else pl.multiple_of(start, 128), size)
        if q == 0:
            acc[d, block, to] = piece
        else:
            acc[d, block, to] += piece

    own_row = lax.rem(lax.div(c, m) - r + R, R)
    own_at = pl.ds(pl.multiple_of(lax.rem(c, m) * V, V), V)

    def own_block(d, q, part):
        add(d, c, a_all[own_row, ks(q), own_at].reshape(w, N), q, part)

    for q in range(Q):
        own_a(q).wait()
        for d in range(1, R):
            row_a(R - d, q).wait_recv()
            col_start(d, q)
        own_i(q).wait()
        turn(0, q, whole)
        own_block(0, q, whole)

    for q in range(Q):
        for dc in order[::-1]:
            s = near(dc)
            here = az.at[s, ks(q)]
            remote(here, here, zsend.at[0, 0, q], zrecv.at[s, q], col=s).wait_recv()
            add(0, s, az[s, ks(q)].reshape(w, N), q, whole)

    def block(t, hi, bit):
        return (hi << (t + 1)) | (bit << t) | (l & ((1 << t) - 1))

    def halving(d, t, i, col):
        n = L >> (t + 1)
        hi = (l >> (t + 1)) ^ hi_order(n)[i]
        bit = (l >> t) & 1
        slot = n - 1 + hi
        give, keep = block(t, hi, 1 - bit), block(t, hi, bit)
        give, keep = (pl.ds(pl.multiple_of(b * rows, 8), rows) for b in (give, keep))
        if d == 0:
            cp = remote(acc.at[0, :, give], lay_buf.at[0, slot], osend.at[slot], orecv.at[slot], layer=l ^ (1 << t))
        else:
            cp = remote(acc.at[d, col, give], lay_buf.at[d, slot, col], lsend.at[d, slot, col], lrecv.at[d, slot, col],
                        layer=l ^ (1 << t))
        return cp, keep, slot

    def own_stage(t):
        for i in range(L >> (t + 1)):
            cp, keep, slot = halving(0, t, i, None)
            cp.wait_recv()
            acc[0, :, keep] += lay_buf[0, slot]
            if t + 1 < stages and i < L >> (t + 2):
                halving(0, t + 1, i, None)[0].start()

    for i in range(L >> 1):
        halving(0, 0, i, None)[0].start()

    c_order = [near(dc) for dc in order] + [c]
    mine = pl.ds(pl.multiple_of(l * rows, 8), rows)

    def first_stage_start(i):
        for d in range(1, R):
            for col in c_order:
                halving(d, 0, i, col)[0].start()

    def stage_end(t, i):
        for d in range(1, R):
            for col in c_order:
                cp, keep, slot = halving(d, t, i, col)
                cp.wait_recv()
                acc[d, col, keep] += lay_buf[d, slot, col]
                if t + 1 == stages:
                    row_sum(d, col).start()
                elif i < L >> (t + 2):
                    halving(d, t + 1, i, col)[0].start()

    for p, part in enumerate(parts):
        for q in range(Q):
            for d in range(1, R):
                row_i(R - d, q, p).wait_recv()
                turn(d, q, part)
                own_block(d, q, part)
                for dc in order:
                    s = near(dc)
                    add(d, s, az[s, ks(q)].reshape(w, N), q, part)
            if p == 0 and q == 0:
                own_stage(0)
            if p == 1 and q == min(1, Q - 1):
                stage_end(0, 0)
        if late:
            first_stage_start(p)

    def row_sum(d, col):
        return remote(acc.at[d, col, mine], row_buf.at[R - d, c], rsend.at[d, col], rrecv.at[R - d, c],
                      row=far_row(d), col=col)

    def col_sum(dc):
        return remote(acc.at[0, near(dc), mine], col_buf.at[c], csend.at[dc], crecv.at[c], col=near(dc))

    if not late:
        for i in range(L >> 1):
            first_stage_start(i)
    for t in range(1, stages):
        own_stage(t)
    for dc in order:
        col_sum(dc).start()
    for t in range(stages):
        for i in range(L >> (t + 1)):
            if not (late and t == 0 and i == 0):
                stage_end(t, i)
    total = acc[0, c, mine]
    for dc in order[::-1]:
        s = near(dc)
        remote(col_buf.at[s], col_buf.at[s], csend.at[dc], crecv.at[s], col=s).wait_recv()
        total += col_buf[s]
    for col in c_order[::-1]:
        for d in range(1, R):
            here = row_buf.at[d, col]
            remote(here, here, rsend.at[d, col], rrecv.at[d, col], row=far_row(d), col=col).wait_recv()
            total += row_buf[d, col]
    o_ref[...] = total

    for q in range(Q):
        for d in range(R):
            if d:
                row_a(d, q).wait_send()
                for p in range(len(parts)):
                    row_i(d, q, p).wait_send()
            for j in range(m):
                b, cp = col_a(d, j, q)

                @pl.when(b != c)
                def _():
                    cp.wait_send()
    for t in range(stages):
        for i in range(L >> (t + 1)):
            halving(0, t, i, None)[0].wait_send()
            for d in range(1, R):
                for col in c_order:
                    halving(d, t, i, col)[0].wait_send()
    for col in c_order:
        for d in range(1, R):
            row_sum(d, col).wait_send()
    for dc in order:
        col_sum(dc).wait_send()


def general_call(R, C, L, integrals, amplitudes):
    K, V, M = integrals.shape
    V_row, N = amplitudes.shape[1:]
    rows = M // L
    Kr = K // R
    Q = Kr
    m = C // R
    slots = L - 1
    dma = pltpu.SemaphoreType.DMA
    vmem = pl.BlockSpec(memory_space=pltpu.VMEM)
    anyspace = pl.BlockSpec(memory_space=pl.ANY)
    return pl.pallas_call(
        functools.partial(kernel, R, C, L, Q),
        out_shape=jax.ShapeDtypeStruct((rows, N), jnp.float32),
        in_specs=[anyspace, anyspace],
        out_specs=vmem,
        scratch_shapes=[
            pltpu.VMEM((R, Kr, V_row, N), jnp.bfloat16),
            pltpu.VMEM((C, Kr, V, N), jnp.bfloat16),
            pltpu.VMEM((R, Kr, V, M), jnp.bfloat16),
            pltpu.VMEM((R, M, Kr * V), jnp.bfloat16),
            pltpu.VMEM((R, C, M, N), jnp.float32),
            pltpu.VMEM((R, slots, C, rows, N), jnp.float32),
            pltpu.VMEM((R, C, rows, N), jnp.float32),
            pltpu.VMEM((C, rows, N), jnp.float32),
            dma((R, Q)), dma((R, Q)),
            dma((2 * R, Q)), dma((2 * R, Q)),
            dma((R, m, Q)), dma((C, Q)),
            dma((slots,)), dma((slots,)),
            dma((R, slots, C)), dma((R, slots, C)),
            dma((R, C)), dma((R, C)),
            dma((C,)), dma((C,)),
        ],
        compiler_params=pltpu.CompilerParams(collective_id=0, has_side_effects=True),
    )(integrals, amplitudes)


def swift(R, C, L, T, lo, i_ref, a_ref, o_ref,
          a_x, az, i_in, i_s, i_t, acc, last, core_buf, x_buf, p_buf, z_buf, y_out, y_buf, last_buf, hi_buf,
          own, iown, asend, arecv, isend, irecv, zsend, zrecv,
          csend, crecv, xsend, xrecv, wsend, precv, wrecv, ysend, yrecv, lsend, lrecv, hsend, hrecv, there):
    r, c, l = lax.axis_index("row"), lax.axis_index("col"), lax.axis_index("layer")
    K, V, M = i_ref.shape
    N = a_ref.shape[2]
    Kr = K // R
    W = Kr * V
    m = C // R
    rows = M // L
    half_rows = 2 * rows
    o = 1 - r
    x, core = lax.div(l, 2), lax.rem(l, 2)
    side = lax.div(c, m)
    home = side == r
    away = jnp.logical_not(home)
    outer = (c == 0) | (c == C - 1)
    inner = jnp.logical_not(outer)

    def remote(src, dst, ss, rs, **to):
        where = {"row": r, "col": c, "layer": l}
        where.update(to)
        return pltpu.make_async_remote_copy(src_ref=src, dst_ref=dst, send_sem=ss, recv_sem=rs,
                                            device_id=where, device_id_type=MESH)

    def landed(ref, sem):
        pltpu.make_async_copy(ref, ref, sem).wait()

    def signal(sem, **to):
        where = {"row": r, "col": c, "layer": l}
        where.update(to)
        pl.semaphore_signal(sem, inc=1, device_id=where, device_id_type=MESH)

    def at(start, size, unit=16):
        return pl.ds(pl.multiple_of(start, unit), size)

    sib, opp = l ^ 1, l ^ 2

    barrier = pltpu.get_barrier_semaphore()
    signal(barrier, row=o)
    signal(barrier, layer=sib)
    signal(barrier, layer=opp)

    @pl.when(c > 0)
    def _():
        signal(barrier, col=c - 1)

    @pl.when(c < C - 1)
    def _():
        signal(barrier, col=c + 1)

    pl.semaphore_wait(barrier, 3 + (c > 0).astype(jnp.int32) + (c < C - 1).astype(jnp.int32))

    def row_a(q, j):
        span = pl.ds(j * V, V)
        return remote(a_ref.at[o * Kr + q, span], a_x.at[q, span], asend, arecv.at[q, j], row=o)

    for q in range(Kr):
        for j in range(m):
            row_a(q, j).start()

    def col_start(d, *qs, js=range(m)):
        for q in qs:
            for j in js:
                b = (o if d else r) * m + j
                span = pl.ds(j * V, V)
                src = a_x.at[q, span] if d else a_ref.at[r * Kr + q, span]

                @pl.when(b != c)
                def _():
                    remote(src, az.at[c, q], zsend, zrecv.at[c], col=b).start()

    ahead, hold, turnover = 3, 2, Kr - 2

    @pl.when(home)
    def _():
        col_start(0, *range(ahead))

    @pl.when(home & inner)
    def _():
        col_start(0, *range(ahead, Kr))

    for t in range(2, C):
        @pl.when((c >= 1) & (c + t - 1 < C))
        def _():
            signal(there.at[0, t - 2], col=c - 1)

        @pl.when((c + 1 < C) & (c - t + 1 >= 0))
        def _():
            signal(there.at[1, t - 2], col=c + 1)

        @pl.when(c + t < C)
        def _():
            pl.semaphore_wait(there.at[0, t - 2], 1)

        @pl.when(c - t >= 0)
        def _():
            pl.semaphore_wait(there.at[1, t - 2], 1)

    @pl.when(away)
    def _():
        col_start(0, *range(hold))

    @pl.when(away & outer)
    def _():
        col_start(0, *range(hold, Kr))

    here_v = at(lax.rem(c, m) * V, V, V)

    def own_a(q, src):
        pltpu.make_async_copy(src.at[q, here_v], az.at[c, q], own).start()

    per = 2

    def own_k(n):
        return (r if n * per >= Kr else o) * Kr + n * per % Kr

    for n in range(K // per):
        pltpu.make_async_copy(i_ref.at[pl.ds(own_k(n), per)], i_in.at[pl.ds(n * per, per)], iown.at[n]).start()

    @pl.when(home)
    def _():
        for q in range(Kr):
            pltpu.make_async_copy(a_ref.at[r * Kr + q, here_v], az.at[c, q], own).start()

    other = (1 - x) * half_rows
    mine = x * half_rows
    first, middle, final = (T, lo - T), (lo, rows - lo), (0, T)

    parts = (final, first, middle)
    order = [(i * rows + start, size) for start, size in parts for i in range(2)]
    place = {part: 2 * part[0] for part in parts}
    slabs = [(other, half_rows)] + [(mine + place[part], 2 * part[1]) for part in (first, middle, final)]

    def row_i(g):
        span = at(*slabs[g])
        return remote(i_s.at[span], i_t.at[1, span], isend, irecv.at[g], row=o)

    for q in range(Kr):
        for j in range(m):
            row_a(q, j).wait_recv()
            if hold <= q < turnover:
                @pl.when(outer | away)
                def _():
                    col_start(1, q, js=[j])
            else:
                col_start(1, q, js=[j])

        @pl.when(away)
        def _():
            own_a(q, a_x)

        if q == turnover:
            @pl.when(inner & home)
            def _():
                col_start(1, *range(hold, turnover))

            @pl.when(inner & away)
            def _():
                col_start(0, *range(hold, Kr))

            @pl.when(outer & home)
            def _():
                col_start(0, *range(ahead, Kr))

        if q < K // per:
            landed(i_in.at[pl.ds(q * per, per)], iown.at[q])
            for k in range(q * per, q * per + per):
                if k < Kr:
                    turned = i_in[k].T
                    for i in range(2):
                        half = turned[i * half_rows:(i + 1) * half_rows]

                        @pl.when(x == i)
                        def _():
                            i_s[i * half_rows:(i + 1) * half_rows, k * V:(k + 1) * V] = jnp.concatenate(
                                [half[start:start + size] for start, size in order], axis=0)

                        @pl.when(x != i)
                        def _():
                            i_s[i * half_rows:(i + 1) * half_rows, k * V:(k + 1) * V] = half
                else:
                    i_t[0, :, (k - Kr) * V:(k - Kr + 1) * V] = i_in[k].T
            if (q + 1) * per == Kr:
                for g in range(len(slabs)):
                    row_i(g).start()

    cols = [side * m, side * m + 1, (1 - side) * (C - 1), 2 - side]
    near, wide, late = (0, 2), (2, 1), (3, 1)
    early = (0, 3)

    def pick(u):
        return cols[u[0]:u[0] + u[1]]

    def wait_piece(s):
        @pl.when(s == c)
        def _():
            landed(az.at[c], own)

        @pl.when(s != c)
        def _():
            landed(az.at[s], zrecv.at[s])

    def product(d, u, start, size):
        right = [az[s].reshape(W, N) for s in pick(u)]
        right = right[0] if len(right) == 1 else jnp.concatenate(right, axis=1)
        return lax.dot_general(i_t[d, at(start, size)], right, (((1,), (0,)), ((), ())), preferred_element_type=jnp.float32)

    def fill(d, u, start, size):
        piece = product(d, u, start, size)
        for j, s in enumerate(pick(u)):
            acc[d, s, at(start, size)] = piece[:, j * N:(j + 1) * N]

    def fill_both(part):
        start, size = part
        for u in (near, (2, 2)):
            piece = product(1, u, mine + place[part], 2 * size)
            for j, s in enumerate(pick(u)):
                for i in range(2):
                    one = piece[i * size:(i + 1) * size, j * N:(j + 1) * N]
                    if part == final:
                        last[i, s] = one
                    else:
                        acc[1, s, at(mine + i * rows + start, size, 8)] = one

    def from_to(u):
        return pl.ds(cols[u[0]], u[1]), pl.ds(u[0], u[1])

    def core_span(d, keep):
        return first if d and keep == 1 else middle if keep == 2 else (0, rows)

    def core_start(d, us, keep):
        start, size = core_span(d, keep)
        give = 2 * (x if keep else 1 - x) + 1 - core
        for u in us:
            src, dst = from_to(u)
            remote(acc.at[d, src, at(give * rows + start, size, 8)], core_buf.at[d, min(keep, 1), dst, pl.ds(start, size)],
                   csend, crecv.at[d, us[0][0] // 3, keep], layer=sib).start()

    def core_end(d, us, keep):
        start, size = core_span(d, keep)
        have = 2 * (x if keep else 1 - x) + core
        slots = pl.ds(us[0][0], sum(u[1] for u in us))
        landed(core_buf.at[d, min(keep, 1), slots, pl.ds(start, size)], crecv.at[d, us[0][0] // 3, keep])
        for u in us:
            src, dst = from_to(u)
            acc[d, src, at(have * rows + start, size, 8)] += core_buf[d, min(keep, 1), dst, start:start + size]

    def x_start(d, us):
        for u in us:
            src, dst = from_to(u)
            remote(acc.at[d, src, at((2 * (1 - x) + core) * rows, rows)], x_buf.at[d, dst],
                   xsend, xrecv.at[d, us[0][0] // 3], layer=opp).start()

    def x_wait(d, us):
        landed(x_buf.at[d, pl.ds(us[0][0], sum(u[1] for u in us))], xrecv.at[d, us[0][0] // 3])

    def x_add(d, us, start, size, add=True):
        for u in us:
            src, dst = from_to(u)
            where = at(l * rows + start, size, 8)
            if add:
                acc[d, src, where] += x_buf[d, dst, start:start + size]
            else:
                acc[d, src, where] = x_buf[d, dst, start:start + size]

    def z_start(d, s):
        size, slot = lo if d else rows, (c ^ s) - 1
        sem = wrecv.at[d, jnp.where(slot == 0, 0, 1)]
        remote(acc.at[d, s, at(l * rows, size)], z_buf.at[d, slot, pl.ds(0, size)], wsend, sem, col=s).start()

    def lean(d, s, n):
        @pl.when(outer)
        def _():
            remote(acc.at[d, s, at(l * rows, rows)], p_buf.at[n], wsend, precv.at[n], col=c ^ 1).start()

    def across(d, s, n):
        @pl.when(inner)
        def _():
            landed(p_buf.at[n], precv.at[n])
            acc[d, s, at(l * rows, rows)] += p_buf[n]
            z_start(d, s)

    def hi_start(us):
        for u in us:
            for s in pick(u):
                remote(acc.at[1, s, at(l * rows + lo, rows - lo, 8)], hi_buf.at[c], hsend, hrecv, row=o, col=s).start()

    most = (near, wide)
    for i in range(3):
        wait_piece(cols[i])
    for u in most:
        fill(0, u, 0, M)
    core_start(0, most, 0)
    core_start(0, most, 1)
    core_end(0, most, 0)
    x_start(0, most)
    core_end(0, most, 1)

    row_i(0).wait_recv()
    for u in most:
        fill(1, u, other, half_rows)
    core_start(1, most, 0)
    x_wait(0, most)
    x_add(0, most, 0, rows)
    z_start(0, c ^ 1)
    lean(0, cols[2], 0)
    core_end(1, most, 0)
    x_start(1, most)

    wait_piece(cols[3])
    fill(0, late, other, half_rows)
    core_start(0, [late], 0)
    fill(1, late, other, half_rows)
    core_start(1, [late], 0)
    across(0, cols[2], 0)
    core_end(0, [late], 0)
    x_start(0, [late])
    core_end(1, [late], 0)
    x_start(1, [late])
    fill(0, late, mine, half_rows)
    core_start(0, [late], 1)

    row_i(1).wait_recv()
    fill_both(first)
    core_start(1, most, 1)
    core_start(1, [late], 1)
    core_end(0, [late], 1)
    x_wait(0, [late])
    x_add(0, [late], 0, rows)
    lean(0, cols[3], 1)
    x_wait(1, most)
    core_end(1, most, 1)
    x_add(1, most, 0, T, add=False)
    x_add(1, most, T, lo - T)
    z_start(1, cols[2])
    z_start(1, c ^ 1)
    core_end(1, [late], 1)
    x_wait(1, [late])
    x_add(1, [late], 0, T, add=False)
    x_add(1, [late], T, lo - T)
    z_start(1, cols[3])

    row_i(2).wait_recv()
    fill_both(middle)
    core_start(1, most, 2)
    core_start(1, [late], 2)
    def finish():
        row_i(3).wait_recv()
        fill_both(final)
        for dc in range(C):
            s = c ^ (C - 1 - dc)
            for i in range(2):
                remote(last.at[i, s], last_buf.at[core, c], lsend, lrecv, row=o, col=s, layer=2 * x + i).start()

    @pl.when(core == 1)
    def _():
        finish()

    core_end(1, most, 2)
    x_add(1, most, lo, rows - lo)
    hi_start(most)
    core_end(1, [late], 2)
    x_add(1, [late], lo, rows - lo)
    hi_start([late])

    @pl.when(core == 0)
    def _():
        finish()

    across(0, cols[3], 1)
    landed(z_buf.at[1, 0, pl.ds(0, lo)], wrecv.at[1, 0])
    y_sum = acc[1, c, at(l * rows, lo)] + z_buf[1, 0, :lo]
    landed(z_buf.at[1, pl.ds(1, 2), pl.ds(0, lo)], wrecv.at[1, 1])
    y_out[...] = y_sum + z_buf[1, 1, :lo] + z_buf[1, 2, :lo]

    remote(y_out, y_buf, ysend, yrecv, row=o).start()

    landed(a_x, asend)
    landed(az.at[pl.ds(0, m + 1)], zsend)
    landed(i_s, isend)
    landed(acc.at[0, :, pl.ds(0, M - T)], csend)
    landed(acc.at[0, :, pl.ds(0, half_rows)], xsend)

    landed(z_buf.at[0, 0], wrecv.at[0, 0])
    o_ref[...] = acc[0, c, at(l * rows, rows)] + z_buf[0, 0]

    landed(z_buf.at[0, 0], wrecv.at[0, 1])

    @pl.when(outer)
    def _():
        o_ref[...] += z_buf[0, 1]

    @pl.when(inner)
    def _():
        o_ref[...] += z_buf[0, 2]

    landed(hi_buf, hrecv)
    high = o_ref[lo:]
    for s in range(C):
        high += hi_buf[s]
    o_ref[lo:] = high
    landed(last_buf, lrecv)
    tail = o_ref[:T]
    for i in range(2):
        for s in range(C):
            tail += last_buf[i, s]
    o_ref[:T] = tail
    landed(y_buf, yrecv)
    o_ref[:lo] += y_buf[...]

    landed(acc.at[0, pl.ds(0, m), pl.ds(0, 3 * (rows + lo) // m)], wsend)
    landed(hi_buf, hsend)
    landed(last, lsend)
    landed(y_out, ysend)


def swift_call(R, C, L, integrals, amplitudes):
    K, V, M = integrals.shape
    V_row, N = amplitudes.shape[1:]
    rows = M // L
    Kr = K // R
    m = C // R
    T = 8
    lo = 72
    dma = pltpu.SemaphoreType.DMA
    f32, bf16 = jnp.float32, jnp.bfloat16
    anyspace = pl.BlockSpec(memory_space=pl.ANY)
    return pl.pallas_call(
        functools.partial(swift, R, C, L, T, lo),
        out_shape=pltpu.VMEM((rows, N), f32),
        in_specs=[anyspace, anyspace],
        out_specs=pl.BlockSpec(memory_space=pltpu.VMEM),
        scratch_shapes=[
            pltpu.VMEM((Kr, V_row, N), bf16),
            pltpu.VMEM((C, Kr, V, N), bf16),
            pltpu.VMEM((K, V, M), bf16),
            pltpu.VMEM((M, Kr * V), bf16),
            pltpu.VMEM((2, M, Kr * V), bf16),
            pltpu.VMEM((2, C, M, N), f32),
            pltpu.VMEM((2, C, T, N), f32),
            pltpu.VMEM((2, 2, C, rows, N), f32),
            pltpu.VMEM((2, C, rows, N), f32),
            pltpu.VMEM((2, rows, N), f32),
            pltpu.VMEM((2, C - 1, rows, N), f32),
            pltpu.VMEM((lo, N), f32),
            pltpu.VMEM((lo, N), f32),
            pltpu.VMEM((2, C, T, N), f32),
            pltpu.VMEM((C, rows - lo, N), f32),
            dma, dma((Kr,)),
            dma, dma((Kr, m)),
            dma, dma((4,)),
            dma, dma((C,)),
            dma, dma((2, 2, 3)),
            dma, dma((2, 2)),
            dma, dma((2,)), dma((2, 2)),
            dma, dma,
            dma, dma,
            dma, dma,
            pltpu.SemaphoreType.REGULAR((2, C - 2)),
        ],
        compiler_params=pltpu.CompilerParams(collective_id=0, has_side_effects=True),
    )(integrals, amplitudes)


def local(R, C, L, integrals, amplitudes, coulomb, row_gap, col_gap):
    swift_fits = R == 2 and C == 4 and L == 4 and integrals.shape[2] % (16 * L) == 0
    call = swift_call if swift_fits else general_call
    own_rows = call(R, C, L, integrals, amplitudes)
    gap_sum = row_gap[:, None] + col_gap[None, :]
    return (coulomb.astype(jnp.float32) + own_rows) / gap_sum


def solution(mesh):
    R, C, L = (mesh.shape[a] for a in ("row", "col", "layer"))
    placed = (
        P("layer", "col", "row"),
        P("layer", "row", "col"),
        P(("row", "layer"), "col"),
        P(("row", "layer")),
        P("col"),
    )
    return jax.shard_map(
        functools.partial(local, R, C, L), mesh=mesh, in_specs=placed, out_specs=P(("row", "layer"), "col"),
        check_vma=False,
    )
```

```python
import functools

import jax
import jax.numpy as jnp
from jax import lax
from jax.experimental import pallas as pl
from jax.experimental.pallas import tpu as pltpu
from jax.sharding import PartitionSpec as P

MESH = pl.DeviceIdType.MESH


def hi_order(n):
    if n == 1:
        return [0]
    below = hi_order(n // 2)
    return [2 * x + 1 for x in below] + [2 * x for x in below]


def kernel(R, C, L, Q, i_ref, a_ref, o_ref,
           a_all, az, i_all, i_t, acc, lay_buf, row_buf, col_buf,
           asend, arecv, xsend, xrecv, zsend, zrecv,
           osend, orecv, lsend, lrecv, rsend, rrecv, csend, crecv):
    r, c, l = lax.axis_index("row"), lax.axis_index("col"), lax.axis_index("layer")
    K, V_row, N = a_ref.shape
    V, M = i_ref.shape[1:]
    Kr = K // R
    kc = Kr // Q
    m = C // R
    w = kc * V
    rows = M // L
    stages = L.bit_length() - 1
    late = M // 2 // 128 * 128 if stages == 2 and M % 128 == 0 else 0
    early = M - late
    top = l >> (stages - 1)

    def remote(src, dst, ss, rs, **to):
        where = {"row": r, "col": c, "layer": l}
        where.update(to)
        return pltpu.make_async_remote_copy(src_ref=src, dst_ref=dst, send_sem=ss, recv_sem=rs,
                                            device_id=where, device_id_type=MESH)

    def ks(q):
        return pl.ds(q * kc, kc)

    def far_row(d):
        return lax.rem(r + d, R)

    def near(dc):
        return lax.rem(c + dc + C, C)

    order = sorted(range(1, C), key=lambda d: -min(d, C - d))

    def slice_for(d, q):
        return pl.ds(far_row(d) * Kr + q * kc, kc)

    def own_a(q):
        return pltpu.make_async_copy(a_ref.at[slice_for(0, q)], a_all.at[0, ks(q)], arecv.at[0, q])

    def own_i(q):
        return pltpu.make_async_copy(i_ref.at[slice_for(0, q)], i_all.at[0, ks(q)], xrecv.at[0, q])

    for q in range(Q):
        own_a(q).start()
        own_i(q).start()

    barrier = pltpu.get_barrier_semaphore()
    partners = [{"row": far_row(d), "col": near(dc)} for d in range(R) for dc in range(C) if d or dc]
    partners += [{"layer": l ^ (1 << t)} for t in range(stages)]
    for p in partners:
        where = {"row": r, "col": c, "layer": l}
        where.update(p)
        pl.semaphore_signal(barrier, inc=1, device_id=where, device_id_type=MESH)
    pl.semaphore_wait(barrier, len(partners))

    def row_a(d, q):
        return remote(a_ref.at[slice_for(d, q)], a_all.at[R - d, ks(q)], asend.at[d, q], arecv.at[R - d, q], row=far_row(d))

    parts = [(0, early, (1 - top) * late)] + ([(early, late, top * early)] if late else [])

    def row_i(d, q, p):
        at, size, start = parts[p]
        src = i_ref.at[slice_for(d, q), :, pl.ds(pl.multiple_of(start, 128), size)] if late else i_ref.at[slice_for(d, q)]
        return remote(src, i_all.at[R - d, ks(q), :, pl.ds(at, size)], xsend.at[p * R + d, q], xrecv.at[p * R + R - d, q],
                      row=far_row(d))

    def col_a(d, j, q):
        b = far_row(d) * m + j
        at = pl.ds(j * V, V)
        src = a_all.at[d, ks(q), at] if d else a_ref.at[slice_for(0, q), at]
        return b, remote(src, az.at[c, ks(q)], zsend.at[d, j, q], zrecv.at[c, q], col=b)

    def col_start(d, q):
        for j in range(m):
            b, cp = col_a(d, j, q)

            @pl.when(b != c)
            def _():
                cp.start()

    for q in range(Q):
        for d in range(1, R):
            row_a(d, q).start()
        col_start(0, q)
    for p in range(len(parts)):
        for q in range(Q):
            for d in range(1, R):
                row_i(d, q, p).start()

    whole = (0, M, 0)

    def turn(d, q, part):
        first, size = part[:2]
        for k in range(kc):
            at = (q * kc + k) * V
            i_t[d, first:first + size, at:at + V] = i_all[d, q * kc + k, :, first:first + size].T

    def add(d, block, x, q, part):
        first, size, start = part
        piece = lax.dot_general(i_t[d, first:first + size, q * w:(q + 1) * w], x, (((1,), (0,)), ((), ())),
                                preferred_element_type=jnp.float32)
        to = pl.ds(start if isinstance(start, int) else pl.multiple_of(start, 128), size)
        if q == 0:
            acc[d, block, to] = piece
        else:
            acc[d, block, to] += piece

    own_row = lax.rem(lax.div(c, m) - r + R, R)
    own_at = pl.ds(pl.multiple_of(lax.rem(c, m) * V, V), V)

    def own_block(d, q, part):
        add(d, c, a_all[own_row, ks(q), own_at].reshape(w, N), q, part)

    for q in range(Q):
        own_a(q).wait()
        for d in range(1, R):
            row_a(R - d, q).wait_recv()
            col_start(d, q)
        own_i(q).wait()
        turn(0, q, whole)
        own_block(0, q, whole)

    for q in range(Q):
        for dc in order[::-1]:
            s = near(dc)
            here = az.at[s, ks(q)]
            remote(here, here, zsend.at[0, 0, q], zrecv.at[s, q], col=s).wait_recv()
            add(0, s, az[s, ks(q)].reshape(w, N), q, whole)

    def block(t, hi, bit):
        return (hi << (t + 1)) | (bit << t) | (l & ((1 << t) - 1))

    def halving(d, t, i, col):
        n = L >> (t + 1)
        hi = (l >> (t + 1)) ^ hi_order(n)[i]
        bit = (l >> t) & 1
        slot = n - 1 + hi
        give, keep = block(t, hi, 1 - bit), block(t, hi, bit)
        give, keep = (pl.ds(pl.multiple_of(b * rows, 8), rows) for b in (give, keep))
        if d == 0:
            cp = remote(acc.at[0, :, give], lay_buf.at[0, slot], osend.at[slot], orecv.at[slot], layer=l ^ (1 << t))
        else:
            cp = remote(acc.at[d, col, give], lay_buf.at[d, slot, col], lsend.at[d, slot, col], lrecv.at[d, slot, col],
                        layer=l ^ (1 << t))
        return cp, keep, slot

    def own_stage(t):
        for i in range(L >> (t + 1)):
            cp, keep, slot = halving(0, t, i, None)
            cp.wait_recv()
            acc[0, :, keep] += lay_buf[0, slot]
            if t + 1 < stages and i < L >> (t + 2):
                halving(0, t + 1, i, None)[0].start()

    for i in range(L >> 1):
        halving(0, 0, i, None)[0].start()

    c_order = [near(dc) for dc in order] + [c]
    mine = pl.ds(pl.multiple_of(l * rows, 8), rows)

    def first_stage_start(i):
        for d in range(1, R):
            for col in c_order:
                halving(d, 0, i, col)[0].start()

    def stage_end(t, i):
        for d in range(1, R):
            for col in c_order:
                cp, keep, slot = halving(d, t, i, col)
                cp.wait_recv()
                acc[d, col, keep] += lay_buf[d, slot, col]
                if t + 1 == stages:
                    row_sum(d, col).start()
                elif i < L >> (t + 2):
                    halving(d, t + 1, i, col)[0].start()

    for p, part in enumerate(parts):
        for q in range(Q):
            for d in range(1, R):
                row_i(R - d, q, p).wait_recv()
                turn(d, q, part)
                own_block(d, q, part)
                for dc in order:
                    s = near(dc)
                    add(d, s, az[s, ks(q)].reshape(w, N), q, part)
            if p == 0 and q == 0:
                own_stage(0)
            if p == 1 and q == min(1, Q - 1):
                stage_end(0, 0)
        if late:
            first_stage_start(p)

    def row_sum(d, col):
        return remote(acc.at[d, col, mine], row_buf.at[R - d, c], rsend.at[d, col], rrecv.at[R - d, c],
                      row=far_row(d), col=col)

    def col_sum(dc):
        return remote(acc.at[0, near(dc), mine], col_buf.at[c], csend.at[dc], crecv.at[c], col=near(dc))

    if not late:
        for i in range(L >> 1):
            first_stage_start(i)
    for t in range(1, stages):
        own_stage(t)
    for dc in order:
        col_sum(dc).start()
    for t in range(stages):
        for i in range(L >> (t + 1)):
            if not (late and t == 0 and i == 0):
                stage_end(t, i)
    total = acc[0, c, mine]
    for dc in order[::-1]:
        s = near(dc)
        remote(col_buf.at[s], col_buf.at[s], csend.at[dc], crecv.at[s], col=s).wait_recv()
        total += col_buf[s]
    for col in c_order[::-1]:
        for d in range(1, R):
            here = row_buf.at[d, col]
            remote(here, here, rsend.at[d, col], rrecv.at[d, col], row=far_row(d), col=col).wait_recv()
            total += row_buf[d, col]
    o_ref[...] = total

    for q in range(Q):
        for d in range(R):
            if d:
                row_a(d, q).wait_send()
                for p in range(len(parts)):
                    row_i(d, q, p).wait_send()
            for j in range(m):
                b, cp = col_a(d, j, q)

                @pl.when(b != c)
                def _():
                    cp.wait_send()
    for t in range(stages):
        for i in range(L >> (t + 1)):
            halving(0, t, i, None)[0].wait_send()
            for d in range(1, R):
                for col in c_order:
                    halving(d, t, i, col)[0].wait_send()
    for col in c_order:
        for d in range(1, R):
            row_sum(d, col).wait_send()
    for dc in order:
        col_sum(dc).wait_send()


def general_call(R, C, L, integrals, amplitudes):
    K, V, M = integrals.shape
    V_row, N = amplitudes.shape[1:]
    rows = M // L
    Kr = K // R
    Q = Kr
    m = C // R
    slots = L - 1
    dma = pltpu.SemaphoreType.DMA
    vmem = pl.BlockSpec(memory_space=pltpu.VMEM)
    anyspace = pl.BlockSpec(memory_space=pl.ANY)
    return pl.pallas_call(
        functools.partial(kernel, R, C, L, Q),
        out_shape=jax.ShapeDtypeStruct((rows, N), jnp.float32),
        in_specs=[anyspace, anyspace],
        out_specs=vmem,
        scratch_shapes=[
            pltpu.VMEM((R, Kr, V_row, N), jnp.bfloat16),
            pltpu.VMEM((C, Kr, V, N), jnp.bfloat16),
            pltpu.VMEM((R, Kr, V, M), jnp.bfloat16),
            pltpu.VMEM((R, M, Kr * V), jnp.bfloat16),
            pltpu.VMEM((R, C, M, N), jnp.float32),
            pltpu.VMEM((R, slots, C, rows, N), jnp.float32),
            pltpu.VMEM((R, C, rows, N), jnp.float32),
            pltpu.VMEM((C, rows, N), jnp.float32),
            dma((R, Q)), dma((R, Q)),
            dma((2 * R, Q)), dma((2 * R, Q)),
            dma((R, m, Q)), dma((C, Q)),
            dma((slots,)), dma((slots,)),
            dma((R, slots, C)), dma((R, slots, C)),
            dma((R, C)), dma((R, C)),
            dma((C,)), dma((C,)),
        ],
        compiler_params=pltpu.CompilerParams(collective_id=0, has_side_effects=True),
    )(integrals, amplitudes)


def swift(R, C, L, T, lo, i_ref, a_ref, o_ref,
          a_x, az, i_in, i_s, i_t, acc, last, core_buf, x_buf, p_buf, z_buf, y_out, y_buf, last_buf, hi_buf,
          own, iown, asend, arecv, isend, irecv, zsend, zrecv,
          csend, crecv, xsend, xrecv, wsend, precv, wrecv, ysend, yrecv, lsend, lrecv, hsend, hrecv, there):
    r, c, l = lax.axis_index("row"), lax.axis_index("col"), lax.axis_index("layer")
    K, V, M = i_ref.shape
    N = a_ref.shape[2]
    Kr = K // R
    W = Kr * V
    m = C // R
    rows = M // L
    half_rows = 2 * rows
    o = 1 - r
    x, core = lax.div(l, 2), lax.rem(l, 2)
    side = lax.div(c, m)
    home = side == r
    away = jnp.logical_not(home)
    outer = (c == 0) | (c == C - 1)
    inner = jnp.logical_not(outer)

    def remote(src, dst, ss, rs, **to):
        where = {"row": r, "col": c, "layer": l}
        where.update(to)
        return pltpu.make_async_remote_copy(src_ref=src, dst_ref=dst, send_sem=ss, recv_sem=rs,
                                            device_id=where, device_id_type=MESH)

    def landed(ref, sem):
        pltpu.make_async_copy(ref, ref, sem).wait()

    def signal(sem, **to):
        where = {"row": r, "col": c, "layer": l}
        where.update(to)
        pl.semaphore_signal(sem, inc=1, device_id=where, device_id_type=MESH)

    def at(start, size, unit=16):
        return pl.ds(pl.multiple_of(start, unit), size)

    sib, opp = l ^ 1, l ^ 2

    barrier = pltpu.get_barrier_semaphore()
    signal(barrier, row=o)
    signal(barrier, layer=sib)
    signal(barrier, layer=opp)

    @pl.when(c > 0)
    def _():
        signal(barrier, col=c - 1)

    @pl.when(c < C - 1)
    def _():
        signal(barrier, col=c + 1)

    pl.semaphore_wait(barrier, 3 + (c > 0).astype(jnp.int32) + (c < C - 1).astype(jnp.int32))

    def row_a(q, j):
        span = pl.ds(j * V, V)
        return remote(a_ref.at[o * Kr + q, span], a_x.at[q, span], asend, arecv.at[j if q == 0 else q + m - 1], row=o)

    def row_start(*qs):
        for q in qs:
            for j in range(m):
                row_a(q, j).start()

    row_start(*range(2))

    @pl.when(core == 0)
    def _():
        row_start(*range(2, Kr))

    def col_start(d, *qs, js=range(m)):
        for q in qs:
            for j in js:
                b = (o if d else r) * m + j
                span = pl.ds(j * V, V)
                src = a_x.at[q, span] if d else a_ref.at[r * Kr + q, span]

                @pl.when(b != c)
                def _():
                    remote(src, az.at[c, q], zsend, zrecv.at[c], col=b).start()

    ahead, hold, turnover = 3, 2, Kr - 2

    @pl.when(home)
    def _():
        col_start(0, *range(ahead))

    @pl.when(home & inner)
    def _():
        col_start(0, *range(ahead, Kr))

    for t in range(2, C):
        @pl.when((c >= 1) & (c + t - 1 < C))
        def _():
            signal(there.at[0, t - 2], col=c - 1)

        @pl.when((c + 1 < C) & (c - t + 1 >= 0))
        def _():
            signal(there.at[1, t - 2], col=c + 1)

        @pl.when(c + t < C)
        def _():
            pl.semaphore_wait(there.at[0, t - 2], 1)

        @pl.when(c - t >= 0)
        def _():
            pl.semaphore_wait(there.at[1, t - 2], 1)

    @pl.when(core == 1)
    def _():
        row_start(*range(2, Kr))

    @pl.when(away)
    def _():
        col_start(0, *range(hold))

    @pl.when(away & outer)
    def _():
        col_start(0, *range(hold, Kr))

    here_v = at(lax.rem(c, m) * V, V, V)

    def own_a(q, src):
        pltpu.make_async_copy(src.at[q, here_v], az.at[c, q], own).start()

    per = 2

    def own_k(n):
        return (r if n * per >= Kr else o) * Kr + n * per % Kr

    for n in range(K // per):
        pltpu.make_async_copy(i_ref.at[pl.ds(own_k(n), per)], i_in.at[pl.ds(n * per, per)], iown.at[n]).start()

    @pl.when(home)
    def _():
        for q in range(Kr):
            pltpu.make_async_copy(a_ref.at[r * Kr + q, here_v], az.at[c, q], own).start()

    other = (1 - x) * half_rows
    mine = x * half_rows
    first, middle, final = (T, lo - T), (lo, rows - lo), (0, T)

    parts = (final, first, middle)
    order = [(i * rows + start, size) for start, size in parts for i in range(2)]
    place = {part: 2 * part[0] for part in parts}
    slabs = [(other, half_rows)] + [(mine + place[part], 2 * part[1]) for part in (first, middle, final)]

    def row_i(g):
        span = at(*slabs[g])
        return remote(i_s.at[span], i_t.at[1, span], isend, irecv.at[g], row=o)

    for q in range(Kr):
        for j in range(m):
            if q == 0:
                row_a(q, j).wait_recv()
            elif j == 0:
                landed(a_x.at[q], arecv.at[q + m - 1])
            if hold <= q < turnover:
                @pl.when(outer | away)
                def _():
                    col_start(1, q, js=[j])
            else:
                col_start(1, q, js=[j])

        @pl.when(away)
        def _():
            own_a(q, a_x)

        if q == turnover:
            @pl.when(inner & home)
            def _():
                col_start(1, *range(hold, turnover))

            @pl.when(inner & away)
            def _():
                col_start(0, *range(hold, Kr))

            @pl.when(outer & home)
            def _():
                col_start(0, *range(ahead, Kr))

        if q < K // per:
            landed(i_in.at[pl.ds(q * per, per)], iown.at[q])
            for k in range(q * per, q * per + per):
                if k < Kr:
                    turned = i_in[k].T
                    for i in range(2):
                        half = turned[i * half_rows:(i + 1) * half_rows]

                        @pl.when(x == i)
                        def _():
                            i_s[i * half_rows:(i + 1) * half_rows, k * V:(k + 1) * V] = jnp.concatenate(
                                [half[start:start + size] for start, size in order], axis=0)

                        @pl.when(x != i)
                        def _():
                            i_s[i * half_rows:(i + 1) * half_rows, k * V:(k + 1) * V] = half
                else:
                    i_t[0, :, (k - Kr) * V:(k - Kr + 1) * V] = i_in[k].T
            if (q + 1) * per == Kr:
                for g in range(len(slabs)):
                    row_i(g).start()

    cols = [side * m, side * m + 1, (1 - side) * (C - 1), 2 - side]
    near, wide, late = (0, 2), (2, 1), (3, 1)
    early = (0, 3)

    def pick(u):
        return cols[u[0]:u[0] + u[1]]

    def wait_piece(s):
        @pl.when(s == c)
        def _():
            landed(az.at[c], own)

        @pl.when(s != c)
        def _():
            landed(az.at[s], zrecv.at[s])

    def product(d, u, start, size):
        right = [az[s].reshape(W, N) for s in pick(u)]
        right = right[0] if len(right) == 1 else jnp.concatenate(right, axis=1)
        return lax.dot_general(i_t[d, at(start, size)], right, (((1,), (0,)), ((), ())), preferred_element_type=jnp.float32)

    def fill(d, u, start, size):
        piece = product(d, u, start, size)
        for j, s in enumerate(pick(u)):
            acc[d, s, at(start, size)] = piece[:, j * N:(j + 1) * N]

    def fill_both(part):
        start, size = part
        for u in (near, (2, 2)):
            piece = product(1, u, mine + place[part], 2 * size)
            for j, s in enumerate(pick(u)):
                for i in range(2):
                    one = piece[i * size:(i + 1) * size, j * N:(j + 1) * N]
                    if part == final:
                        last[i, s] = one
                    else:
                        acc[1, s, at(mine + i * rows + start, size, 8)] = one

    def from_to(u):
        return pl.ds(cols[u[0]], u[1]), pl.ds(u[0], u[1])

    def core_span(d, keep):
        return first if d and keep == 1 else middle if keep == 2 else (0, rows)

    def core_start(d, us, keep):
        start, size = core_span(d, keep)
        give = 2 * (x if keep else 1 - x) + 1 - core
        for u in us:
            src, dst = from_to(u)
            remote(acc.at[d, src, at(give * rows + start, size, 8)], core_buf.at[d, min(keep, 1), dst, pl.ds(start, size)],
                   csend, crecv.at[d, us[0][0] // 3, keep], layer=sib).start()

    def core_end(d, us, keep):
        start, size = core_span(d, keep)
        have = 2 * (x if keep else 1 - x) + core
        slots = pl.ds(us[0][0], sum(u[1] for u in us))
        landed(core_buf.at[d, min(keep, 1), slots, pl.ds(start, size)], crecv.at[d, us[0][0] // 3, keep])
        for u in us:
            src, dst = from_to(u)
            acc[d, src, at(have * rows + start, size, 8)] += core_buf[d, min(keep, 1), dst, start:start + size]

    def x_start(d, us):
        for u in us:
            src, dst = from_to(u)
            remote(acc.at[d, src, at((2 * (1 - x) + core) * rows, rows)], x_buf.at[d, dst],
                   xsend, xrecv.at[d, us[0][0] // 3], layer=opp).start()

    def x_wait(d, us):
        landed(x_buf.at[d, pl.ds(us[0][0], sum(u[1] for u in us))], xrecv.at[d, us[0][0] // 3])

    def x_add(d, us, start, size, add=True):
        for u in us:
            src, dst = from_to(u)
            where = at(l * rows + start, size, 8)
            if add:
                acc[d, src, where] += x_buf[d, dst, start:start + size]
            else:
                acc[d, src, where] = x_buf[d, dst, start:start + size]

    def z_start(d, s):
        size, slot = lo if d else rows, (c ^ s) - 1
        sem = wrecv.at[d, jnp.where(slot == 0, 0, 1)]
        remote(acc.at[d, s, at(l * rows, size)], z_buf.at[d, slot, pl.ds(0, size)], wsend, sem, col=s).start()

    def lean(d, s, n):
        @pl.when(outer)
        def _():
            remote(acc.at[d, s, at(l * rows, rows)], p_buf.at[n], wsend, precv.at[n], col=c ^ 1).start()

    def across(d, s, n):
        @pl.when(inner)
        def _():
            landed(p_buf.at[n], precv.at[n])
            acc[d, s, at(l * rows, rows)] += p_buf[n]
            z_start(d, s)

    def hi_start(us):
        for u in us:
            for s in pick(u):
                remote(acc.at[1, s, at(l * rows + lo, rows - lo, 8)], hi_buf.at[c], hsend, hrecv, row=o, col=s).start()

    most = (near, wide)
    for i in range(3):
        wait_piece(cols[i])
    for u in most:
        fill(0, u, 0, M)
    core_start(0, most, 0)
    core_start(0, most, 1)
    core_end(0, most, 0)
    x_start(0, most)
    core_end(0, most, 1)

    row_i(0).wait_recv()
    for u in most:
        fill(1, u, other, half_rows)
    core_start(1, most, 0)
    x_wait(0, most)
    x_add(0, most, 0, rows)
    z_start(0, c ^ 1)
    lean(0, cols[2], 0)
    core_end(1, most, 0)
    x_start(1, most)

    wait_piece(cols[3])
    fill(0, late, other, half_rows)
    core_start(0, [late], 0)
    fill(1, late, other, half_rows)
    core_start(1, [late], 0)
    across(0, cols[2], 0)
    core_end(0, [late], 0)
    x_start(0, [late])
    core_end(1, [late], 0)
    x_start(1, [late])
    fill(0, late, mine, half_rows)
    core_start(0, [late], 1)

    row_i(1).wait_recv()
    fill_both(first)
    core_start(1, most, 1)
    core_start(1, [late], 1)
    core_end(0, [late], 1)
    x_wait(0, [late])
    x_add(0, [late], 0, rows)
    lean(0, cols[3], 1)
    x_wait(1, most)
    core_end(1, most, 1)
    x_add(1, most, 0, T, add=False)
    x_add(1, most, T, lo - T)
    z_start(1, cols[2])
    z_start(1, c ^ 1)
    core_end(1, [late], 1)
    x_wait(1, [late])
    x_add(1, [late], 0, T, add=False)
    x_add(1, [late], T, lo - T)
    z_start(1, cols[3])

    row_i(2).wait_recv()
    fill_both(middle)
    core_start(1, most, 2)
    core_start(1, [late], 2)
    def finish():
        row_i(3).wait_recv()
        fill_both(final)
        for dc in range(C):
            s = c ^ (C - 1 - dc)
            for i in range(2):
                remote(last.at[i, s], last_buf.at[core, c], lsend, lrecv, row=o, col=s, layer=2 * x + i).start()

    @pl.when(core == 1)
    def _():
        finish()

    core_end(1, most, 2)
    x_add(1, most, lo, rows - lo)
    hi_start(most)
    core_end(1, [late], 2)
    x_add(1, [late], lo, rows - lo)
    hi_start([late])

    @pl.when(core == 0)
    def _():
        finish()

    across(0, cols[3], 1)
    landed(z_buf.at[1, 0, pl.ds(0, lo)], wrecv.at[1, 0])
    y_sum = acc[1, c, at(l * rows, lo)] + z_buf[1, 0, :lo]
    landed(z_buf.at[1, pl.ds(1, 2), pl.ds(0, lo)], wrecv.at[1, 1])
    y_out[...] = y_sum + z_buf[1, 1, :lo] + z_buf[1, 2, :lo]

    remote(y_out, y_buf, ysend, yrecv, row=o).start()

    landed(a_x, asend)
    landed(az.at[pl.ds(0, m + 1)], zsend)
    landed(i_s, isend)
    landed(acc.at[0, :, pl.ds(0, M - T)], csend)
    landed(acc.at[0, :, pl.ds(0, half_rows)], xsend)

    landed(z_buf.at[0, 0], wrecv.at[0, 0])
    o_ref[...] = acc[0, c, at(l * rows, rows)] + z_buf[0, 0]

    landed(z_buf.at[0, 0], wrecv.at[0, 1])

    @pl.when(outer)
    def _():
        o_ref[...] += z_buf[0, 1]

    @pl.when(inner)
    def _():
        o_ref[...] += z_buf[0, 2]

    landed(hi_buf, hrecv)
    high = o_ref[lo:]
    for s in range(C):
        high += hi_buf[s]
    o_ref[lo:] = high
    landed(last_buf, lrecv)
    tail = o_ref[:T]
    for i in range(2):
        for s in range(C):
            tail += last_buf[i, s]
    o_ref[:T] = tail
    landed(y_buf, yrecv)
    o_ref[:lo] += y_buf[...]

    landed(acc.at[0, pl.ds(0, m), pl.ds(0, 3 * (rows + lo) // m)], wsend)
    landed(hi_buf, hsend)
    landed(last, lsend)
    landed(y_out, ysend)


def swift_call(R, C, L, integrals, amplitudes):
    K, V, M = integrals.shape
    V_row, N = amplitudes.shape[1:]
    rows = M // L
    Kr = K // R
    m = C // R
    T = 8
    lo = rows * 3 // 4 // 8 * 8
    dma = pltpu.SemaphoreType.DMA
    f32, bf16 = jnp.float32, jnp.bfloat16
    anyspace = pl.BlockSpec(memory_space=pl.ANY)
    return pl.pallas_call(
        functools.partial(swift, R, C, L, T, lo),
        out_shape=pltpu.VMEM((rows, N), f32),
        in_specs=[anyspace, anyspace],
        out_specs=pl.BlockSpec(memory_space=pltpu.VMEM),
        scratch_shapes=[
            pltpu.VMEM((Kr, V_row, N), bf16),
            pltpu.VMEM((C, Kr, V, N), bf16),
            pltpu.VMEM((K, V, M), bf16),
            pltpu.VMEM((M, Kr * V), bf16),
            pltpu.VMEM((2, M, Kr * V), bf16),
            pltpu.VMEM((2, C, M, N), f32),
            pltpu.VMEM((2, C, T, N), f32),
            pltpu.VMEM((2, 2, C, rows, N), f32),
            pltpu.VMEM((2, C, rows, N), f32),
            pltpu.VMEM((2, rows, N), f32),
            pltpu.VMEM((2, C - 1, rows, N), f32),
            pltpu.VMEM((lo, N), f32),
            pltpu.VMEM((lo, N), f32),
            pltpu.VMEM((2, C, T, N), f32),
            pltpu.VMEM((C, rows - lo, N), f32),
            dma, dma((Kr,)),
            dma, dma((Kr + m - 1,)),
            dma, dma((4,)),
            dma, dma((C,)),
            dma, dma((2, 2, 3)),
            dma, dma((2, 2)),
            dma, dma((2,)), dma((2, 2)),
            dma, dma,
            dma, dma,
            dma, dma,
            pltpu.SemaphoreType.REGULAR((2, C - 2)),
        ],
        compiler_params=pltpu.CompilerParams(collective_id=0, has_side_effects=True),
    )(integrals, amplitudes)


def local(R, C, L, integrals, amplitudes, coulomb, row_gap, col_gap):
    K, V, M = integrals.shape
    N = amplitudes.shape[2]
    swift_fits = (R, C, L) == (2, 4, 4) and K % 16 == 0 and M % (16 * L) == 0 and V % 128 == 0 and N % 128 == 0
    call = swift_call if swift_fits else general_call
    own_rows = call(R, C, L, integrals, amplitudes)
    gap_sum = row_gap[:, None] + col_gap[None, :]
    return (coulomb.astype(jnp.float32) + own_rows) / gap_sum


def solution(mesh):
    R, C, L = (mesh.shape[a] for a in ("row", "col", "layer"))
    placed = (
        P("layer", "col", "row"),
        P("layer", "row", "col"),
        P(("row", "layer"), "col"),
        P(("row", "layer")),
        P("col"),
    )
    return jax.shard_map(
        functools.partial(local, R, C, L), mesh=mesh, in_specs=placed, out_specs=P(("row", "layer"), "col"),
        check_vma=False,
    )
```

```python
import functools

import jax
import jax.numpy as jnp
from jax import lax
from jax.experimental import pallas as pl
from jax.experimental.pallas import tpu as pltpu
from jax.sharding import PartitionSpec as P

MESH = pl.DeviceIdType.MESH


def hi_order(n):
    if n == 1:
        return [0]
    below = hi_order(n // 2)
    return [2 * x + 1 for x in below] + [2 * x for x in below]


def kernel(R, C, L, Q, i_ref, a_ref, o_ref,
           a_all, az, i_all, i_t, acc, lay_buf, row_buf, col_buf,
           asend, arecv, xsend, xrecv, zsend, zrecv,
           osend, orecv, lsend, lrecv, rsend, rrecv, csend, crecv):
    r, c, l = lax.axis_index("row"), lax.axis_index("col"), lax.axis_index("layer")
    K, V_row, N = a_ref.shape
    V, M = i_ref.shape[1:]
    Kr = K // R
    kc = Kr // Q
    m = C // R
    w = kc * V
    rows = M // L
    stages = L.bit_length() - 1
    late = M // 2 // 128 * 128 if stages == 2 and M % 128 == 0 else 0
    early = M - late
    top = l >> (stages - 1)

    def remote(src, dst, ss, rs, **to):
        where = {"row": r, "col": c, "layer": l}
        where.update(to)
        return pltpu.make_async_remote_copy(src_ref=src, dst_ref=dst, send_sem=ss, recv_sem=rs,
                                            device_id=where, device_id_type=MESH)

    def ks(q):
        return pl.ds(q * kc, kc)

    def far_row(d):
        return lax.rem(r + d, R)

    def near(dc):
        return lax.rem(c + dc + C, C)

    order = sorted(range(1, C), key=lambda d: -min(d, C - d))

    def slice_for(d, q):
        return pl.ds(far_row(d) * Kr + q * kc, kc)

    def own_a(q):
        return pltpu.make_async_copy(a_ref.at[slice_for(0, q)], a_all.at[0, ks(q)], arecv.at[0, q])

    def own_i(q):
        return pltpu.make_async_copy(i_ref.at[slice_for(0, q)], i_all.at[0, ks(q)], xrecv.at[0, q])

    for q in range(Q):
        own_a(q).start()
        own_i(q).start()

    barrier = pltpu.get_barrier_semaphore()
    partners = [{"row": far_row(d), "col": near(dc)} for d in range(R) for dc in range(C) if d or dc]
    partners += [{"layer": l ^ (1 << t)} for t in range(stages)]
    for p in partners:
        where = {"row": r, "col": c, "layer": l}
        where.update(p)
        pl.semaphore_signal(barrier, inc=1, device_id=where, device_id_type=MESH)
    pl.semaphore_wait(barrier, len(partners))

    def row_a(d, q):
        return remote(a_ref.at[slice_for(d, q)], a_all.at[R - d, ks(q)], asend.at[d, q], arecv.at[R - d, q], row=far_row(d))

    parts = [(0, early, (1 - top) * late)] + ([(early, late, top * early)] if late else [])

    def row_i(d, q, p):
        at, size, start = parts[p]
        src = i_ref.at[slice_for(d, q), :, pl.ds(pl.multiple_of(start, 128), size)] if late else i_ref.at[slice_for(d, q)]
        return remote(src, i_all.at[R - d, ks(q), :, pl.ds(at, size)], xsend.at[p * R + d, q], xrecv.at[p * R + R - d, q],
                      row=far_row(d))

    def col_a(d, j, q):
        b = far_row(d) * m + j
        at = pl.ds(j * V, V)
        src = a_all.at[d, ks(q), at] if d else a_ref.at[slice_for(0, q), at]
        return b, remote(src, az.at[c, ks(q)], zsend.at[d, j, q], zrecv.at[c, q], col=b)

    def col_start(d, q):
        for j in range(m):
            b, cp = col_a(d, j, q)

            @pl.when(b != c)
            def _():
                cp.start()

    for q in range(Q):
        for d in range(1, R):
            row_a(d, q).start()
        col_start(0, q)
    for p in range(len(parts)):
        for q in range(Q):
            for d in range(1, R):
                row_i(d, q, p).start()

    whole = (0, M, 0)

    def turn(d, q, part):
        first, size = part[:2]
        for k in range(kc):
            at = (q * kc + k) * V
            i_t[d, first:first + size, at:at + V] = i_all[d, q * kc + k, :, first:first + size].T

    def add(d, block, x, q, part):
        first, size, start = part
        piece = lax.dot_general(i_t[d, first:first + size, q * w:(q + 1) * w], x, (((1,), (0,)), ((), ())),
                                preferred_element_type=jnp.float32)
        to = pl.ds(start if isinstance(start, int) else pl.multiple_of(start, 128), size)
        if q == 0:
            acc[d, block, to] = piece
        else:
            acc[d, block, to] += piece

    own_row = lax.rem(lax.div(c, m) - r + R, R)
    own_at = pl.ds(pl.multiple_of(lax.rem(c, m) * V, V), V)

    def own_block(d, q, part):
        add(d, c, a_all[own_row, ks(q), own_at].reshape(w, N), q, part)

    for q in range(Q):
        own_a(q).wait()
        for d in range(1, R):
            row_a(R - d, q).wait_recv()
            col_start(d, q)
        own_i(q).wait()
        turn(0, q, whole)
        own_block(0, q, whole)

    for q in range(Q):
        for dc in order[::-1]:
            s = near(dc)
            here = az.at[s, ks(q)]
            remote(here, here, zsend.at[0, 0, q], zrecv.at[s, q], col=s).wait_recv()
            add(0, s, az[s, ks(q)].reshape(w, N), q, whole)

    def block(t, hi, bit):
        return (hi << (t + 1)) | (bit << t) | (l & ((1 << t) - 1))

    def halving(d, t, i, col):
        n = L >> (t + 1)
        hi = (l >> (t + 1)) ^ hi_order(n)[i]
        bit = (l >> t) & 1
        slot = n - 1 + hi
        give, keep = block(t, hi, 1 - bit), block(t, hi, bit)
        give, keep = (pl.ds(pl.multiple_of(b * rows, 8), rows) for b in (give, keep))
        if d == 0:
            cp = remote(acc.at[0, :, give], lay_buf.at[0, slot], osend.at[slot], orecv.at[slot], layer=l ^ (1 << t))
        else:
            cp = remote(acc.at[d, col, give], lay_buf.at[d, slot, col], lsend.at[d, slot, col], lrecv.at[d, slot, col],
                        layer=l ^ (1 << t))
        return cp, keep, slot

    def own_stage(t):
        for i in range(L >> (t + 1)):
            cp, keep, slot = halving(0, t, i, None)
            cp.wait_recv()
            acc[0, :, keep] += lay_buf[0, slot]
            if t + 1 < stages and i < L >> (t + 2):
                halving(0, t + 1, i, None)[0].start()

    for i in range(L >> 1):
        halving(0, 0, i, None)[0].start()

    c_order = [near(dc) for dc in order] + [c]
    mine = pl.ds(pl.multiple_of(l * rows, 8), rows)

    def first_stage_start(i):
        for d in range(1, R):
            for col in c_order:
                halving(d, 0, i, col)[0].start()

    def stage_end(t, i):
        for d in range(1, R):
            for col in c_order:
                cp, keep, slot = halving(d, t, i, col)
                cp.wait_recv()
                acc[d, col, keep] += lay_buf[d, slot, col]
                if t + 1 == stages:
                    row_sum(d, col).start()
                elif i < L >> (t + 2):
                    halving(d, t + 1, i, col)[0].start()

    for p, part in enumerate(parts):
        for q in range(Q):
            for d in range(1, R):
                row_i(R - d, q, p).wait_recv()
                turn(d, q, part)
                own_block(d, q, part)
                for dc in order:
                    s = near(dc)
                    add(d, s, az[s, ks(q)].reshape(w, N), q, part)
            if p == 0 and q == 0:
                own_stage(0)
            if p == 1 and q == min(1, Q - 1):
                stage_end(0, 0)
        if late:
            first_stage_start(p)

    def row_sum(d, col):
        return remote(acc.at[d, col, mine], row_buf.at[R - d, c], rsend.at[d, col], rrecv.at[R - d, c],
                      row=far_row(d), col=col)

    def col_sum(dc):
        return remote(acc.at[0, near(dc), mine], col_buf.at[c], csend.at[dc], crecv.at[c], col=near(dc))

    if not late:
        for i in range(L >> 1):
            first_stage_start(i)
    for t in range(1, stages):
        own_stage(t)
    for dc in order:
        col_sum(dc).start()
    for t in range(stages):
        for i in range(L >> (t + 1)):
            if not (late and t == 0 and i == 0):
                stage_end(t, i)
    total = acc[0, c, mine]
    for dc in order[::-1]:
        s = near(dc)
        remote(col_buf.at[s], col_buf.at[s], csend.at[dc], crecv.at[s], col=s).wait_recv()
        total += col_buf[s]
    for col in c_order[::-1]:
        for d in range(1, R):
            here = row_buf.at[d, col]
            remote(here, here, rsend.at[d, col], rrecv.at[d, col], row=far_row(d), col=col).wait_recv()
            total += row_buf[d, col]
    o_ref[...] = total

    for q in range(Q):
        for d in range(R):
            if d:
                row_a(d, q).wait_send()
                for p in range(len(parts)):
                    row_i(d, q, p).wait_send()
            for j in range(m):
                b, cp = col_a(d, j, q)

                @pl.when(b != c)
                def _():
                    cp.wait_send()
    for t in range(stages):
        for i in range(L >> (t + 1)):
            halving(0, t, i, None)[0].wait_send()
            for d in range(1, R):
                for col in c_order:
                    halving(d, t, i, col)[0].wait_send()
    for col in c_order:
        for d in range(1, R):
            row_sum(d, col).wait_send()
    for dc in order:
        col_sum(dc).wait_send()


def general_call(R, C, L, integrals, amplitudes):
    K, V, M = integrals.shape
    V_row, N = amplitudes.shape[1:]
    rows = M // L
    Kr = K // R
    Q = Kr
    m = C // R
    slots = L - 1
    dma = pltpu.SemaphoreType.DMA
    vmem = pl.BlockSpec(memory_space=pltpu.VMEM)
    anyspace = pl.BlockSpec(memory_space=pl.ANY)
    return pl.pallas_call(
        functools.partial(kernel, R, C, L, Q),
        out_shape=jax.ShapeDtypeStruct((rows, N), jnp.float32),
        in_specs=[anyspace, anyspace],
        out_specs=vmem,
        scratch_shapes=[
            pltpu.VMEM((R, Kr, V_row, N), jnp.bfloat16),
            pltpu.VMEM((C, Kr, V, N), jnp.bfloat16),
            pltpu.VMEM((R, Kr, V, M), jnp.bfloat16),
            pltpu.VMEM((R, M, Kr * V), jnp.bfloat16),
            pltpu.VMEM((R, C, M, N), jnp.float32),
            pltpu.VMEM((R, slots, C, rows, N), jnp.float32),
            pltpu.VMEM((R, C, rows, N), jnp.float32),
            pltpu.VMEM((C, rows, N), jnp.float32),
            dma((R, Q)), dma((R, Q)),
            dma((2 * R, Q)), dma((2 * R, Q)),
            dma((R, m, Q)), dma((C, Q)),
            dma((slots,)), dma((slots,)),
            dma((R, slots, C)), dma((R, slots, C)),
            dma((R, C)), dma((R, C)),
            dma((C,)), dma((C,)),
        ],
        compiler_params=pltpu.CompilerParams(collective_id=0, has_side_effects=True),
    )(integrals, amplitudes)


def swift(R, C, L, T, lo, i_ref, a_ref, b_ref, rg_ref, cg_ref, o_ref,
          bare, gap_r, gap_c, gap, gsem,
          a_x, az, i_in, i_s, i_t, acc, last, core_buf, x_buf, p_buf, z_buf, y_out, y_buf, last_buf, hi_buf,
          own, iown, asend, arecv, isend, irecv, zsend, zrecv,
          csend, crecv, xsend, xrecv, wsend, precv, wrecv, ysend, yrecv, lsend, lrecv, hsend, hrecv, there):
    r, c, l = lax.axis_index("row"), lax.axis_index("col"), lax.axis_index("layer")
    K, V, M = i_ref.shape
    N = a_ref.shape[2]
    Kr = K // R
    W = Kr * V
    m = C // R
    rows = M // L
    half_rows = 2 * rows
    o = 1 - r
    x, core = lax.div(l, 2), lax.rem(l, 2)
    side = lax.div(c, m)
    home = side == r
    away = jnp.logical_not(home)
    outer = (c == 0) | (c == C - 1)
    inner = jnp.logical_not(outer)

    def remote(src, dst, ss, rs, **to):
        where = {"row": r, "col": c, "layer": l}
        where.update(to)
        return pltpu.make_async_remote_copy(src_ref=src, dst_ref=dst, send_sem=ss, recv_sem=rs,
                                            device_id=where, device_id_type=MESH)

    def landed(ref, sem):
        pltpu.make_async_copy(ref, ref, sem).wait()

    def signal(sem, **to):
        where = {"row": r, "col": c, "layer": l}
        where.update(to)
        pl.semaphore_signal(sem, inc=1, device_id=where, device_id_type=MESH)

    def at(start, size, unit=16):
        return pl.ds(pl.multiple_of(start, unit), size)

    sib, opp = l ^ 1, l ^ 2

    barrier = pltpu.get_barrier_semaphore()
    signal(barrier, row=o)
    signal(barrier, layer=sib)
    signal(barrier, layer=opp)

    @pl.when(c > 0)
    def _():
        signal(barrier, col=c - 1)

    @pl.when(c < C - 1)
    def _():
        signal(barrier, col=c + 1)

    pl.semaphore_wait(barrier, 3 + (c > 0).astype(jnp.int32) + (c < C - 1).astype(jnp.int32))

    def row_a(q, j):
        span = pl.ds(j * V, V)
        return remote(a_ref.at[o * Kr + q, span], a_x.at[q, span], asend, arecv.at[j if q == 0 else q + m - 1], row=o)

    def row_start(*qs):
        for q in qs:
            for j in range(m):
                row_a(q, j).start()

    row_start(*range(2))

    @pl.when(core == 0)
    def _():
        row_start(*range(2, Kr))

    def col_start(d, *qs, js=range(m)):
        for q in qs:
            for j in js:
                b = (o if d else r) * m + j
                span = pl.ds(j * V, V)
                src = a_x.at[q, span] if d else a_ref.at[r * Kr + q, span]

                @pl.when(b != c)
                def _():
                    remote(src, az.at[c, q], zsend, zrecv.at[c], col=b).start()

    ahead, hold, turnover = 3, 2, Kr - 2

    @pl.when(home)
    def _():
        col_start(0, *range(ahead))

    @pl.when(home & inner)
    def _():
        col_start(0, *range(ahead, Kr))

    for t in range(2, C):
        @pl.when((c >= 1) & (c + t - 1 < C))
        def _():
            signal(there.at[0, t - 2], col=c - 1)

        @pl.when((c + 1 < C) & (c - t + 1 >= 0))
        def _():
            signal(there.at[1, t - 2], col=c + 1)

        @pl.when(c + t < C)
        def _():
            pl.semaphore_wait(there.at[0, t - 2], 1)

        @pl.when(c - t >= 0)
        def _():
            pl.semaphore_wait(there.at[1, t - 2], 1)

    @pl.when(core == 1)
    def _():
        row_start(*range(2, Kr))

    @pl.when(away)
    def _():
        col_start(0, *range(hold))

    @pl.when(away & outer)
    def _():
        col_start(0, *range(hold, Kr))

    here_v = at(lax.rem(c, m) * V, V, V)

    def own_a(q, src):
        pltpu.make_async_copy(src.at[q, here_v], az.at[c, q], own).start()

    per = 2

    def own_k(n):
        return (r if n * per >= Kr else o) * Kr + n * per % Kr

    for n, (src, dst) in enumerate(((b_ref, bare), (rg_ref, gap_r), (cg_ref, gap_c))):
        pltpu.make_async_copy(src, dst, gsem.at[n]).start()

    for n in range(K // per):
        pltpu.make_async_copy(i_ref.at[pl.ds(own_k(n), per)], i_in.at[pl.ds(n * per, per)], iown.at[n]).start()

    @pl.when(home)
    def _():
        for q in range(Kr):
            pltpu.make_async_copy(a_ref.at[r * Kr + q, here_v], az.at[c, q], own).start()

    other = (1 - x) * half_rows
    mine = x * half_rows
    first, middle, final = (T, lo - T), (lo, rows - lo), (0, T)

    parts = (final, first, middle)
    order = [(i * rows + start, size) for start, size in parts for i in range(2)]
    place = {part: 2 * part[0] for part in parts}
    slabs = [(other, half_rows)] + [(mine + place[part], 2 * part[1]) for part in (first, middle, final)]

    def row_i(g):
        span = at(*slabs[g])
        return remote(i_s.at[span], i_t.at[1, span], isend, irecv.at[g], row=o)

    for q in range(Kr):
        for j in range(m):
            if q == 0:
                row_a(q, j).wait_recv()
            elif j == 0:
                landed(a_x.at[q], arecv.at[q + m - 1])
            if hold <= q < turnover:
                @pl.when(outer | away)
                def _():
                    col_start(1, q, js=[j])
            else:
                col_start(1, q, js=[j])

        @pl.when(away)
        def _():
            own_a(q, a_x)

        if q == turnover:
            @pl.when(inner & home)
            def _():
                col_start(1, *range(hold, turnover))

            @pl.when(inner & away)
            def _():
                col_start(0, *range(hold, Kr))

            @pl.when(outer & home)
            def _():
                col_start(0, *range(ahead, Kr))

        if q < K // per:
            landed(i_in.at[pl.ds(q * per, per)], iown.at[q])
            for k in range(q * per, q * per + per):
                if k < Kr:
                    turned = i_in[k].T
                    for i in range(2):
                        half = turned[i * half_rows:(i + 1) * half_rows]

                        @pl.when(x == i)
                        def _():
                            i_s[i * half_rows:(i + 1) * half_rows, k * V:(k + 1) * V] = jnp.concatenate(
                                [half[start:start + size] for start, size in order], axis=0)

                        @pl.when(x != i)
                        def _():
                            i_s[i * half_rows:(i + 1) * half_rows, k * V:(k + 1) * V] = half
                else:
                    i_t[0, :, (k - Kr) * V:(k - Kr + 1) * V] = i_in[k].T
            if (q + 1) * per == Kr:
                for g in range(len(slabs)):
                    row_i(g).start()

    cols = [side * m, side * m + 1, (1 - side) * (C - 1), 2 - side]
    near, wide, late = (0, 2), (2, 1), (3, 1)
    early = (0, 3)

    def pick(u):
        return cols[u[0]:u[0] + u[1]]

    def wait_piece(s):
        @pl.when(s == c)
        def _():
            landed(az.at[c], own)

        @pl.when(s != c)
        def _():
            landed(az.at[s], zrecv.at[s])

    def product(d, u, start, size):
        right = [az[s].reshape(W, N) for s in pick(u)]
        right = right[0] if len(right) == 1 else jnp.concatenate(right, axis=1)
        return lax.dot_general(i_t[d, at(start, size)], right, (((1,), (0,)), ((), ())), preferred_element_type=jnp.float32)

    def fill(d, u, start, size):
        piece = product(d, u, start, size)
        for j, s in enumerate(pick(u)):
            acc[d, s, at(start, size)] = piece[:, j * N:(j + 1) * N]

    def fill_both(part):
        start, size = part
        for u in (near, (2, 2)):
            piece = product(1, u, mine + place[part], 2 * size)
            for j, s in enumerate(pick(u)):
                for i in range(2):
                    one = piece[i * size:(i + 1) * size, j * N:(j + 1) * N]
                    if part == final:
                        last[i, s] = one
                    else:
                        acc[1, s, at(mine + i * rows + start, size, 8)] = one

    def from_to(u):
        return pl.ds(cols[u[0]], u[1]), pl.ds(u[0], u[1])

    def core_span(d, keep):
        return first if d and keep == 1 else middle if keep == 2 else (0, rows)

    def core_start(d, us, keep):
        start, size = core_span(d, keep)
        give = 2 * (x if keep else 1 - x) + 1 - core
        for u in us:
            src, dst = from_to(u)
            remote(acc.at[d, src, at(give * rows + start, size, 8)], core_buf.at[d, min(keep, 1), dst, pl.ds(start, size)],
                   csend, crecv.at[d, us[0][0] // 3, keep], layer=sib).start()

    def core_end(d, us, keep):
        start, size = core_span(d, keep)
        have = 2 * (x if keep else 1 - x) + core
        slots = pl.ds(us[0][0], sum(u[1] for u in us))
        landed(core_buf.at[d, min(keep, 1), slots, pl.ds(start, size)], crecv.at[d, us[0][0] // 3, keep])
        for u in us:
            src, dst = from_to(u)
            acc[d, src, at(have * rows + start, size, 8)] += core_buf[d, min(keep, 1), dst, start:start + size]

    def x_start(d, us):
        for u in us:
            src, dst = from_to(u)
            remote(acc.at[d, src, at((2 * (1 - x) + core) * rows, rows)], x_buf.at[d, dst],
                   xsend, xrecv.at[d, us[0][0] // 3], layer=opp).start()

    def x_wait(d, us):
        landed(x_buf.at[d, pl.ds(us[0][0], sum(u[1] for u in us))], xrecv.at[d, us[0][0] // 3])

    def x_add(d, us, start, size, add=True):
        for u in us:
            src, dst = from_to(u)
            where = at(l * rows + start, size, 8)
            if add:
                acc[d, src, where] += x_buf[d, dst, start:start + size]
            else:
                acc[d, src, where] = x_buf[d, dst, start:start + size]

    def z_start(d, s):
        size, slot = lo if d else rows, (c ^ s) - 1
        sem = wrecv.at[d, jnp.where(slot == 0, 0, 1)]
        remote(acc.at[d, s, at(l * rows, size)], z_buf.at[d, slot, pl.ds(0, size)], wsend, sem, col=s).start()

    def lean(d, s, n):
        @pl.when(outer)
        def _():
            remote(acc.at[d, s, at(l * rows, rows)], p_buf.at[n], wsend, precv.at[n], col=c ^ 1).start()

    def across(d, s, n):
        @pl.when(inner)
        def _():
            landed(p_buf.at[n], precv.at[n])
            acc[d, s, at(l * rows, rows)] += p_buf[n]
            z_start(d, s)

    def hi_start(us):
        for u in us:
            for s in pick(u):
                remote(acc.at[1, s, at(l * rows + lo, rows - lo, 8)], hi_buf.at[c], hsend, hrecv, row=o, col=s).start()

    most = (near, wide)
    for i in range(3):
        wait_piece(cols[i])
    for u in most:
        fill(0, u, 0, M)
    core_start(0, most, 0)
    core_start(0, most, 1)
    core_end(0, most, 0)
    x_start(0, most)
    core_end(0, most, 1)

    row_i(0).wait_recv()
    for u in most:
        fill(1, u, other, half_rows)
    core_start(1, most, 0)
    x_wait(0, most)
    x_add(0, most, 0, rows)
    z_start(0, c ^ 1)
    lean(0, cols[2], 0)
    core_end(1, most, 0)
    x_start(1, most)

    wait_piece(cols[3])
    fill(0, late, other, half_rows)
    core_start(0, [late], 0)
    fill(1, late, other, half_rows)
    core_start(1, [late], 0)
    across(0, cols[2], 0)
    core_end(0, [late], 0)
    x_start(0, [late])
    core_end(1, [late], 0)
    x_start(1, [late])
    fill(0, late, mine, half_rows)
    core_start(0, [late], 1)

    row_i(1).wait_recv()
    fill_both(first)
    core_start(1, most, 1)
    core_start(1, [late], 1)
    core_end(0, [late], 1)
    x_wait(0, [late])
    x_add(0, [late], 0, rows)
    lean(0, cols[3], 1)
    x_wait(1, most)
    core_end(1, most, 1)
    x_add(1, most, 0, T, add=False)
    x_add(1, most, T, lo - T)
    z_start(1, cols[2])
    z_start(1, c ^ 1)
    core_end(1, [late], 1)
    x_wait(1, [late])
    x_add(1, [late], 0, T, add=False)
    x_add(1, [late], T, lo - T)
    z_start(1, cols[3])

    row_i(2).wait_recv()
    fill_both(middle)
    core_start(1, most, 2)
    core_start(1, [late], 2)
    def finish():
        row_i(3).wait_recv()
        fill_both(final)
        for dc in range(C):
            s = c ^ (C - 1 - dc)
            for i in range(2):
                remote(last.at[i, s], last_buf.at[core, c], lsend, lrecv, row=o, col=s, layer=2 * x + i).start()

    @pl.when(core == 1)
    def _():
        finish()

    core_end(1, most, 2)
    x_add(1, most, lo, rows - lo)
    hi_start(most)
    core_end(1, [late], 2)
    x_add(1, [late], lo, rows - lo)
    hi_start([late])

    @pl.when(core == 0)
    def _():
        finish()

    across(0, cols[3], 1)
    landed(z_buf.at[1, 0, pl.ds(0, lo)], wrecv.at[1, 0])
    y_sum = acc[1, c, at(l * rows, lo)] + z_buf[1, 0, :lo]
    landed(z_buf.at[1, pl.ds(1, 2), pl.ds(0, lo)], wrecv.at[1, 1])
    y_out[...] = y_sum + z_buf[1, 1, :lo] + z_buf[1, 2, :lo]

    remote(y_out, y_buf, ysend, yrecv, row=o).start()

    for n, (src, dst) in enumerate(((b_ref, bare), (rg_ref, gap_r), (cg_ref, gap_c))):
        pltpu.make_async_copy(src, dst, gsem.at[n]).wait()
    gap[...] = jnp.broadcast_to(gap_r[...], (N, rows)).T + gap_c[...]
    landed(a_x, asend)
    landed(az.at[pl.ds(0, m + 1)], zsend)
    landed(i_s, isend)
    landed(acc.at[0, :, pl.ds(0, M - T)], csend)
    landed(acc.at[0, :, pl.ds(0, half_rows)], xsend)

    landed(z_buf.at[0, 0], wrecv.at[0, 0])
    o_ref[...] = bare[...].astype(jnp.float32) + acc[0, c, at(l * rows, rows)] + z_buf[0, 0]

    landed(z_buf.at[0, 0], wrecv.at[0, 1])

    @pl.when(outer)
    def _():
        o_ref[...] += z_buf[0, 1]

    @pl.when(inner)
    def _():
        o_ref[...] += z_buf[0, 2]

    landed(hi_buf, hrecv)
    high = o_ref[lo:]
    for s in range(C):
        high += hi_buf[s]
    o_ref[lo:] = high
    landed(last_buf, lrecv)
    tail = o_ref[:T]
    for i in range(2):
        for s in range(C):
            tail += last_buf[i, s]
    o_ref[:T] = tail
    landed(y_buf, yrecv)
    o_ref[:lo] += y_buf[...]
    o_ref[...] = o_ref[...] / gap[...]

    landed(acc.at[0, pl.ds(0, m), pl.ds(0, 3 * (rows + lo) // m)], wsend)
    landed(hi_buf, hsend)
    landed(last, lsend)
    landed(y_out, ysend)


def swift_call(R, C, L, integrals, amplitudes, coulomb, row_gap, col_gap):
    K, V, M = integrals.shape
    V_row, N = amplitudes.shape[1:]
    rows = M // L
    Kr = K // R
    m = C // R
    T = 8
    lo = rows * 3 // 4 // 8 * 8
    dma = pltpu.SemaphoreType.DMA
    f32, bf16 = jnp.float32, jnp.bfloat16
    anyspace = pl.BlockSpec(memory_space=pl.ANY)
    return pl.pallas_call(
        functools.partial(swift, R, C, L, T, lo),
        out_shape=pltpu.VMEM((rows, N), f32),
        in_specs=[anyspace] * 5,
        out_specs=pl.BlockSpec(memory_space=pltpu.VMEM),
        scratch_shapes=[
            pltpu.VMEM((rows, N), bf16), pltpu.VMEM((1, rows), f32), pltpu.VMEM((1, N), f32), pltpu.VMEM((rows, N), f32), dma((3,)),
            pltpu.VMEM((Kr, V_row, N), bf16),
            pltpu.VMEM((C, Kr, V, N), bf16),
            pltpu.VMEM((K, V, M), bf16),
            pltpu.VMEM((M, Kr * V), bf16),
            pltpu.VMEM((2, M, Kr * V), bf16),
            pltpu.VMEM((2, C, M, N), f32),
            pltpu.VMEM((2, C, T, N), f32),
            pltpu.VMEM((2, 2, C, rows, N), f32),
            pltpu.VMEM((2, C, rows, N), f32),
            pltpu.VMEM((2, rows, N), f32),
            pltpu.VMEM((2, C - 1, rows, N), f32),
            pltpu.VMEM((lo, N), f32),
            pltpu.VMEM((lo, N), f32),
            pltpu.VMEM((2, C, T, N), f32),
            pltpu.VMEM((C, rows - lo, N), f32),
            dma, dma((Kr,)),
            dma, dma((Kr + m - 1,)),
            dma, dma((4,)),
            dma, dma((C,)),
            dma, dma((2, 2, 3)),
            dma, dma((2, 2)),
            dma, dma((2,)), dma((2, 2)),
            dma, dma,
            dma, dma,
            dma, dma,
            pltpu.SemaphoreType.REGULAR((2, C - 2)),
        ],
        compiler_params=pltpu.CompilerParams(collective_id=0, has_side_effects=True),
    )(integrals, amplitudes, coulomb, row_gap[None, :], col_gap[None, :])


def local(R, C, L, integrals, amplitudes, coulomb, row_gap, col_gap):
    K, V, M = integrals.shape
    N = amplitudes.shape[2]
    swift_fits = (R, C, L) == (2, 4, 4) and K % 16 == 0 and M % (16 * L) == 0 and V % 128 == 0 and N % 128 == 0
    if swift_fits:
        return swift_call(R, C, L, integrals, amplitudes, coulomb, row_gap, col_gap)
    own_rows = general_call(R, C, L, integrals, amplitudes)
    gap_sum = row_gap[:, None] + col_gap[None, :]
    return (coulomb.astype(jnp.float32) + own_rows) / gap_sum


def solution(mesh):
    R, C, L = (mesh.shape[a] for a in ("row", "col", "layer"))
    placed = (
        P("layer", "col", "row"),
        P("layer", "row", "col"),
        P(("row", "layer"), "col"),
        P(("row", "layer")),
        P("col"),
    )
    return jax.shard_map(
        functools.partial(local, R, C, L), mesh=mesh, in_specs=placed, out_specs=P(("row", "layer"), "col"),
        check_vma=False,
    )
```

```python
import functools

import jax
import jax.numpy as jnp
from jax import lax
from jax.experimental import pallas as pl
from jax.experimental.pallas import tpu as pltpu
from jax.sharding import PartitionSpec as P

MESH = pl.DeviceIdType.MESH


def hi_order(n):
    if n == 1:
        return [0]
    below = hi_order(n // 2)
    return [2 * x + 1 for x in below] + [2 * x for x in below]


def kernel(R, C, L, Q, i_ref, a_ref, o_ref,
           a_all, az, i_all, i_t, acc, lay_buf, row_buf, col_buf,
           asend, arecv, xsend, xrecv, zsend, zrecv,
           osend, orecv, lsend, lrecv, rsend, rrecv, csend, crecv):
    r, c, l = lax.axis_index("row"), lax.axis_index("col"), lax.axis_index("layer")
    K, V_row, N = a_ref.shape
    V, M = i_ref.shape[1:]
    Kr = K // R
    kc = Kr // Q
    m = C // R
    w = kc * V
    rows = M // L
    stages = L.bit_length() - 1
    late = M // 2 // 128 * 128 if stages == 2 and M % 128 == 0 else 0
    early = M - late
    top = l >> (stages - 1)

    def remote(src, dst, ss, rs, **to):
        where = {"row": r, "col": c, "layer": l}
        where.update(to)
        return pltpu.make_async_remote_copy(src_ref=src, dst_ref=dst, send_sem=ss, recv_sem=rs,
                                            device_id=where, device_id_type=MESH)

    def ks(q):
        return pl.ds(q * kc, kc)

    def far_row(d):
        return lax.rem(r + d, R)

    def near(dc):
        return lax.rem(c + dc + C, C)

    order = sorted(range(1, C), key=lambda d: -min(d, C - d))

    def slice_for(d, q):
        return pl.ds(far_row(d) * Kr + q * kc, kc)

    def own_a(q):
        return pltpu.make_async_copy(a_ref.at[slice_for(0, q)], a_all.at[0, ks(q)], arecv.at[0, q])

    def own_i(q):
        return pltpu.make_async_copy(i_ref.at[slice_for(0, q)], i_all.at[0, ks(q)], xrecv.at[0, q])

    for q in range(Q):
        own_a(q).start()
        own_i(q).start()

    barrier = pltpu.get_barrier_semaphore()
    partners = [{"row": far_row(d), "col": near(dc)} for d in range(R) for dc in range(C) if d or dc]
    partners += [{"layer": l ^ (1 << t)} for t in range(stages)]
    for p in partners:
        where = {"row": r, "col": c, "layer": l}
        where.update(p)
        pl.semaphore_signal(barrier, inc=1, device_id=where, device_id_type=MESH)
    pl.semaphore_wait(barrier, len(partners))

    def row_a(d, q):
        return remote(a_ref.at[slice_for(d, q)], a_all.at[R - d, ks(q)], asend.at[d, q], arecv.at[R - d, q], row=far_row(d))

    parts = [(0, early, (1 - top) * late)] + ([(early, late, top * early)] if late else [])

    def row_i(d, q, p):
        at, size, start = parts[p]
        src = i_ref.at[slice_for(d, q), :, pl.ds(pl.multiple_of(start, 128), size)] if late else i_ref.at[slice_for(d, q)]
        return remote(src, i_all.at[R - d, ks(q), :, pl.ds(at, size)], xsend.at[p * R + d, q], xrecv.at[p * R + R - d, q],
                      row=far_row(d))

    def col_a(d, j, q):
        b = far_row(d) * m + j
        at = pl.ds(j * V, V)
        src = a_all.at[d, ks(q), at] if d else a_ref.at[slice_for(0, q), at]
        return b, remote(src, az.at[c, ks(q)], zsend.at[d, j, q], zrecv.at[c, q], col=b)

    def col_start(d, q):
        for j in range(m):
            b, cp = col_a(d, j, q)

            @pl.when(b != c)
            def _():
                cp.start()

    for q in range(Q):
        for d in range(1, R):
            row_a(d, q).start()
        col_start(0, q)
    for p in range(len(parts)):
        for q in range(Q):
            for d in range(1, R):
                row_i(d, q, p).start()

    whole = (0, M, 0)

    def turn(d, q, part):
        first, size = part[:2]
        for k in range(kc):
            at = (q * kc + k) * V
            i_t[d, first:first + size, at:at + V] = i_all[d, q * kc + k, :, first:first + size].T

    def add(d, block, x, q, part):
        first, size, start = part
        piece = lax.dot_general(i_t[d, first:first + size, q * w:(q + 1) * w], x, (((1,), (0,)), ((), ())),
                                preferred_element_type=jnp.float32)
        to = pl.ds(start if isinstance(start, int) else pl.multiple_of(start, 128), size)
        if q == 0:
            acc[d, block, to] = piece
        else:
            acc[d, block, to] += piece

    own_row = lax.rem(lax.div(c, m) - r + R, R)
    own_at = pl.ds(pl.multiple_of(lax.rem(c, m) * V, V), V)

    def own_block(d, q, part):
        add(d, c, a_all[own_row, ks(q), own_at].reshape(w, N), q, part)

    for q in range(Q):
        own_a(q).wait()
        for d in range(1, R):
            row_a(R - d, q).wait_recv()
            col_start(d, q)
        own_i(q).wait()
        turn(0, q, whole)
        own_block(0, q, whole)

    for q in range(Q):
        for dc in order[::-1]:
            s = near(dc)
            here = az.at[s, ks(q)]
            remote(here, here, zsend.at[0, 0, q], zrecv.at[s, q], col=s).wait_recv()
            add(0, s, az[s, ks(q)].reshape(w, N), q, whole)

    def block(t, hi, bit):
        return (hi << (t + 1)) | (bit << t) | (l & ((1 << t) - 1))

    def halving(d, t, i, col):
        n = L >> (t + 1)
        hi = (l >> (t + 1)) ^ hi_order(n)[i]
        bit = (l >> t) & 1
        slot = n - 1 + hi
        give, keep = block(t, hi, 1 - bit), block(t, hi, bit)
        give, keep = (pl.ds(pl.multiple_of(b * rows, 8), rows) for b in (give, keep))
        if d == 0:
            cp = remote(acc.at[0, :, give], lay_buf.at[0, slot], osend.at[slot], orecv.at[slot], layer=l ^ (1 << t))
        else:
            cp = remote(acc.at[d, col, give], lay_buf.at[d, slot, col], lsend.at[d, slot, col], lrecv.at[d, slot, col],
                        layer=l ^ (1 << t))
        return cp, keep, slot

    def own_stage(t):
        for i in range(L >> (t + 1)):
            cp, keep, slot = halving(0, t, i, None)
            cp.wait_recv()
            acc[0, :, keep] += lay_buf[0, slot]
            if t + 1 < stages and i < L >> (t + 2):
                halving(0, t + 1, i, None)[0].start()

    for i in range(L >> 1):
        halving(0, 0, i, None)[0].start()

    c_order = [near(dc) for dc in order] + [c]
    mine = pl.ds(pl.multiple_of(l * rows, 8), rows)

    def first_stage_start(i):
        for d in range(1, R):
            for col in c_order:
                halving(d, 0, i, col)[0].start()

    def stage_end(t, i):
        for d in range(1, R):
            for col in c_order:
                cp, keep, slot = halving(d, t, i, col)
                cp.wait_recv()
                acc[d, col, keep] += lay_buf[d, slot, col]
                if t + 1 == stages:
                    row_sum(d, col).start()
                elif i < L >> (t + 2):
                    halving(d, t + 1, i, col)[0].start()

    for p, part in enumerate(parts):
        for q in range(Q):
            for d in range(1, R):
                row_i(R - d, q, p).wait_recv()
                turn(d, q, part)
                own_block(d, q, part)
                for dc in order:
                    s = near(dc)
                    add(d, s, az[s, ks(q)].reshape(w, N), q, part)
            if p == 0 and q == 0:
                own_stage(0)
            if p == 1 and q == min(1, Q - 1):
                stage_end(0, 0)
        if late:
            first_stage_start(p)

    def row_sum(d, col):
        return remote(acc.at[d, col, mine], row_buf.at[R - d, c], rsend.at[d, col], rrecv.at[R - d, c],
                      row=far_row(d), col=col)

    def col_sum(dc):
        return remote(acc.at[0, near(dc), mine], col_buf.at[c], csend.at[dc], crecv.at[c], col=near(dc))

    if not late:
        for i in range(L >> 1):
            first_stage_start(i)
    for t in range(1, stages):
        own_stage(t)
    for dc in order:
        col_sum(dc).start()
    for t in range(stages):
        for i in range(L >> (t + 1)):
            if not (late and t == 0 and i == 0):
                stage_end(t, i)
    total = acc[0, c, mine]
    for dc in order[::-1]:
        s = near(dc)
        remote(col_buf.at[s], col_buf.at[s], csend.at[dc], crecv.at[s], col=s).wait_recv()
        total += col_buf[s]
    for col in c_order[::-1]:
        for d in range(1, R):
            here = row_buf.at[d, col]
            remote(here, here, rsend.at[d, col], rrecv.at[d, col], row=far_row(d), col=col).wait_recv()
            total += row_buf[d, col]
    o_ref[...] = total

    for q in range(Q):
        for d in range(R):
            if d:
                row_a(d, q).wait_send()
                for p in range(len(parts)):
                    row_i(d, q, p).wait_send()
            for j in range(m):
                b, cp = col_a(d, j, q)

                @pl.when(b != c)
                def _():
                    cp.wait_send()
    for t in range(stages):
        for i in range(L >> (t + 1)):
            halving(0, t, i, None)[0].wait_send()
            for d in range(1, R):
                for col in c_order:
                    halving(d, t, i, col)[0].wait_send()
    for col in c_order:
        for d in range(1, R):
            row_sum(d, col).wait_send()
    for dc in order:
        col_sum(dc).wait_send()


def general_call(R, C, L, integrals, amplitudes):
    K, V, M = integrals.shape
    V_row, N = amplitudes.shape[1:]
    rows = M // L
    Kr = K // R
    Q = Kr
    m = C // R
    slots = L - 1
    dma = pltpu.SemaphoreType.DMA
    vmem = pl.BlockSpec(memory_space=pltpu.VMEM)
    anyspace = pl.BlockSpec(memory_space=pl.ANY)
    return pl.pallas_call(
        functools.partial(kernel, R, C, L, Q),
        out_shape=jax.ShapeDtypeStruct((rows, N), jnp.float32),
        in_specs=[anyspace, anyspace],
        out_specs=vmem,
        scratch_shapes=[
            pltpu.VMEM((R, Kr, V_row, N), jnp.bfloat16),
            pltpu.VMEM((C, Kr, V, N), jnp.bfloat16),
            pltpu.VMEM((R, Kr, V, M), jnp.bfloat16),
            pltpu.VMEM((R, M, Kr * V), jnp.bfloat16),
            pltpu.VMEM((R, C, M, N), jnp.float32),
            pltpu.VMEM((R, slots, C, rows, N), jnp.float32),
            pltpu.VMEM((R, C, rows, N), jnp.float32),
            pltpu.VMEM((C, rows, N), jnp.float32),
            dma((R, Q)), dma((R, Q)),
            dma((2 * R, Q)), dma((2 * R, Q)),
            dma((R, m, Q)), dma((C, Q)),
            dma((slots,)), dma((slots,)),
            dma((R, slots, C)), dma((R, slots, C)),
            dma((R, C)), dma((R, C)),
            dma((C,)), dma((C,)),
        ],
        compiler_params=pltpu.CompilerParams(collective_id=0, has_side_effects=True),
    )(integrals, amplitudes)


def swift(R, C, L, T, lo, i_ref, a_ref, b_ref, rg_ref, cg_ref, o_ref,
          bare, gap_r, gap_c, gap, gsem,
          a_x, az, i_in, i_s, i_t, acc, last, core_buf, x_buf, p_buf, z_buf, y_out, y_buf, last_buf, hi_buf,
          own, iown, asend, arecv, isend, irecv, zsend, zrecv,
          csend, crecv, xsend, xrecv, wsend, precv, wrecv, ysend, yrecv, lsend, lrecv, hsend, hrecv, there):
    r, c, l = lax.axis_index("row"), lax.axis_index("col"), lax.axis_index("layer")
    K, V, M = i_ref.shape
    N = a_ref.shape[2]
    Kr = K // R
    W = Kr * V
    m = C // R
    rows = M // L
    half_rows = 2 * rows
    o = 1 - r
    x, core = lax.div(l, 2), lax.rem(l, 2)
    side = lax.div(c, m)
    home = side == r
    away = jnp.logical_not(home)
    outer = (c == 0) | (c == C - 1)
    inner = jnp.logical_not(outer)

    def remote(src, dst, ss, rs, **to):
        where = {"row": r, "col": c, "layer": l}
        where.update(to)
        return pltpu.make_async_remote_copy(src_ref=src, dst_ref=dst, send_sem=ss, recv_sem=rs,
                                            device_id=where, device_id_type=MESH)

    def landed(ref, sem):
        pltpu.make_async_copy(ref, ref, sem).wait()

    def signal(sem, **to):
        where = {"row": r, "col": c, "layer": l}
        where.update(to)
        pl.semaphore_signal(sem, inc=1, device_id=where, device_id_type=MESH)

    def at(start, size, unit=16):
        return pl.ds(pl.multiple_of(start, unit), size)

    sib, opp = l ^ 1, l ^ 2

    barrier = pltpu.get_barrier_semaphore()
    signal(barrier, row=o)
    signal(barrier, layer=sib)
    signal(barrier, layer=opp)

    @pl.when(c > 0)
    def _():
        signal(barrier, col=c - 1)

    @pl.when(c < C - 1)
    def _():
        signal(barrier, col=c + 1)

    pl.semaphore_wait(barrier, 3 + (c > 0).astype(jnp.int32) + (c < C - 1).astype(jnp.int32))

    def row_a(q, j):
        span = pl.ds(j * V, V)
        return remote(a_ref.at[o * Kr + q, span], a_x.at[q, span], asend, arecv.at[j if q == 0 else q + m - 1], row=o)

    def row_start(*qs):
        for q in qs:
            for j in range(m):
                row_a(q, j).start()

    row_start(*range(2))

    @pl.when(core == 0)
    def _():
        row_start(*range(2, Kr))

    def col_start(d, *qs, js=range(m)):
        for q in qs:
            for j in js:
                b = (o if d else r) * m + j
                span = pl.ds(j * V, V)
                src = a_x.at[q, span] if d else a_ref.at[r * Kr + q, span]

                @pl.when(b != c)
                def _():
                    remote(src, az.at[c, q], zsend, zrecv.at[c], col=b).start()

    ahead, hold, turnover = 2, 3, Kr - 3

    @pl.when(home)
    def _():
        col_start(0, *range(ahead))

    @pl.when(home & inner)
    def _():
        col_start(0, *range(ahead, Kr))

    for t in range(2, C):
        @pl.when((c >= 1) & (c + t - 1 < C))
        def _():
            signal(there.at[0, t - 2], col=c - 1)

        @pl.when((c + 1 < C) & (c - t + 1 >= 0))
        def _():
            signal(there.at[1, t - 2], col=c + 1)

        @pl.when(c + t < C)
        def _():
            pl.semaphore_wait(there.at[0, t - 2], 1)

        @pl.when(c - t >= 0)
        def _():
            pl.semaphore_wait(there.at[1, t - 2], 1)

    @pl.when(core == 1)
    def _():
        row_start(*range(2, Kr))

    @pl.when(away)
    def _():
        col_start(0, *range(hold))

    @pl.when(away & outer)
    def _():
        col_start(0, *range(hold, Kr))

    here_v = at(lax.rem(c, m) * V, V, V)

    def own_a(q, src):
        pltpu.make_async_copy(src.at[q, here_v], az.at[c, q], own).start()

    per = 2

    def own_k(n):
        return (r if n * per >= Kr else o) * Kr + n * per % Kr

    for n, (src, dst) in enumerate(((b_ref, bare), (rg_ref, gap_r), (cg_ref, gap_c))):
        pltpu.make_async_copy(src, dst, gsem.at[n]).start()

    for n in range(K // per):
        pltpu.make_async_copy(i_ref.at[pl.ds(own_k(n), per)], i_in.at[pl.ds(n * per, per)], iown.at[n]).start()

    @pl.when(home)
    def _():
        for q in range(Kr):
            pltpu.make_async_copy(a_ref.at[r * Kr + q, here_v], az.at[c, q], own).start()

    other = (1 - x) * half_rows
    mine = x * half_rows
    first, middle, final = (T, lo - T), (lo, rows - lo), (0, T)

    parts = (final, first, middle)
    order = [(i * rows + start, size) for start, size in parts for i in range(2)]
    place = {part: 2 * part[0] for part in parts}
    slabs = [(other, half_rows)] + [(mine + place[part], 2 * part[1]) for part in (first, middle, final)]

    def row_i(g):
        span = at(*slabs[g])
        return remote(i_s.at[span], i_t.at[1, span], isend, irecv.at[g], row=o)

    for q in range(Kr):
        for j in range(m):
            if q == 0:
                row_a(q, j).wait_recv()
            elif j == 0:
                landed(a_x.at[q], arecv.at[q + m - 1])
            if hold <= q < turnover:
                @pl.when(outer | away)
                def _():
                    col_start(1, q, js=[j])
            else:
                col_start(1, q, js=[j])

        @pl.when(away)
        def _():
            own_a(q, a_x)

        if q == turnover:
            @pl.when(inner & home)
            def _():
                col_start(1, *range(hold, turnover))

            @pl.when(inner & away)
            def _():
                col_start(0, *range(hold, Kr))

            @pl.when(outer & home)
            def _():
                col_start(0, *range(ahead, Kr))

        if q < K // per:
            landed(i_in.at[pl.ds(q * per, per)], iown.at[q])
            for k in range(q * per, q * per + per):
                if k < Kr:
                    turned = i_in[k].T
                    for i in range(2):
                        half = turned[i * half_rows:(i + 1) * half_rows]

                        @pl.when(x == i)
                        def _():
                            i_s[i * half_rows:(i + 1) * half_rows, k * V:(k + 1) * V] = jnp.concatenate(
                                [half[start:start + size] for start, size in order], axis=0)

                        @pl.when(x != i)
                        def _():
                            i_s[i * half_rows:(i + 1) * half_rows, k * V:(k + 1) * V] = half
                else:
                    i_t[0, :, (k - Kr) * V:(k - Kr + 1) * V] = i_in[k].T
            if (q + 1) * per == Kr:
                for g in range(len(slabs)):
                    row_i(g).start()

    cols = [side * m, side * m + 1, (1 - side) * (C - 1), 2 - side]
    near, wide, late = (0, 2), (2, 1), (3, 1)
    early = (0, 3)

    def pick(u):
        return cols[u[0]:u[0] + u[1]]

    def wait_piece(s):
        @pl.when(s == c)
        def _():
            landed(az.at[c], own)

        @pl.when(s != c)
        def _():
            landed(az.at[s], zrecv.at[s])

    def product(d, u, start, size):
        right = [az[s].reshape(W, N) for s in pick(u)]
        right = right[0] if len(right) == 1 else jnp.concatenate(right, axis=1)
        return lax.dot_general(i_t[d, at(start, size)], right, (((1,), (0,)), ((), ())), preferred_element_type=jnp.float32)

    def fill(d, u, start, size):
        piece = product(d, u, start, size)
        for j, s in enumerate(pick(u)):
            acc[d, s, at(start, size)] = piece[:, j * N:(j + 1) * N]

    def fill_both(part):
        start, size = part
        for u in (near, (2, 2)):
            piece = product(1, u, mine + place[part], 2 * size)
            for j, s in enumerate(pick(u)):
                for i in range(2):
                    one = piece[i * size:(i + 1) * size, j * N:(j + 1) * N]
                    if part == final:
                        last[i, s] = one
                    else:
                        acc[1, s, at(mine + i * rows + start, size, 8)] = one

    def from_to(u):
        return pl.ds(cols[u[0]], u[1]), pl.ds(u[0], u[1])

    def core_span(d, keep):
        return first if d and keep == 1 else middle if keep == 2 else (0, rows)

    def core_start(d, us, keep):
        start, size = core_span(d, keep)
        give = 2 * (x if keep else 1 - x) + 1 - core
        for u in us:
            src, dst = from_to(u)
            remote(acc.at[d, src, at(give * rows + start, size, 8)], core_buf.at[d, min(keep, 1), dst, pl.ds(start, size)],
                   csend, crecv.at[d, us[0][0] // 3, keep], layer=sib).start()

    def core_end(d, us, keep):
        start, size = core_span(d, keep)
        have = 2 * (x if keep else 1 - x) + core
        slots = pl.ds(us[0][0], sum(u[1] for u in us))
        landed(core_buf.at[d, min(keep, 1), slots, pl.ds(start, size)], crecv.at[d, us[0][0] // 3, keep])
        for u in us:
            src, dst = from_to(u)
            acc[d, src, at(have * rows + start, size, 8)] += core_buf[d, min(keep, 1), dst, start:start + size]

    def x_start(d, us):
        for u in us:
            src, dst = from_to(u)
            remote(acc.at[d, src, at((2 * (1 - x) + core) * rows, rows)], x_buf.at[d, dst],
                   xsend, xrecv.at[d, us[0][0] // 3], layer=opp).start()

    def x_wait(d, us):
        landed(x_buf.at[d, pl.ds(us[0][0], sum(u[1] for u in us))], xrecv.at[d, us[0][0] // 3])

    def x_add(d, us, start, size, add=True):
        for u in us:
            src, dst = from_to(u)
            where = at(l * rows + start, size, 8)
            if add:
                acc[d, src, where] += x_buf[d, dst, start:start + size]
            else:
                acc[d, src, where] = x_buf[d, dst, start:start + size]

    def z_start(d, s):
        size, slot = lo if d else rows, (c ^ s) - 1
        sem = wrecv.at[d, jnp.where(slot == 0, 0, 1)]
        remote(acc.at[d, s, at(l * rows, size)], z_buf.at[d, slot, pl.ds(0, size)], wsend, sem, col=s).start()

    def lean(d, s, n):
        @pl.when(outer)
        def _():
            remote(acc.at[d, s, at(l * rows, rows)], p_buf.at[n], wsend, precv.at[n], col=c ^ 1).start()

    def across(d, s, n):
        @pl.when(inner)
        def _():
            landed(p_buf.at[n], precv.at[n])
            acc[d, s, at(l * rows, rows)] += p_buf[n]
            z_start(d, s)

    def hi_start(us):
        for u in us:
            for s in pick(u):
                remote(acc.at[1, s, at(l * rows + lo, rows - lo, 8)], hi_buf.at[c], hsend, hrecv, row=o, col=s).start()

    most = (near, wide)
    for i in range(3):
        wait_piece(cols[i])
    for u in most:
        fill(0, u, 0, M)
    core_start(0, most, 0)
    core_start(0, most, 1)
    core_end(0, most, 0)
    x_start(0, most)
    core_end(0, most, 1)

    row_i(0).wait_recv()
    for u in most:
        fill(1, u, other, half_rows)
    core_start(1, most, 0)
    x_wait(0, most)
    x_add(0, most, 0, rows)
    z_start(0, c ^ 1)
    lean(0, cols[2], 0)
    core_end(1, most, 0)
    x_start(1, most)

    wait_piece(cols[3])
    fill(0, late, other, half_rows)
    core_start(0, [late], 0)
    fill(1, late, other, half_rows)
    core_start(1, [late], 0)
    across(0, cols[2], 0)
    core_end(0, [late], 0)
    x_start(0, [late])
    core_end(1, [late], 0)
    x_start(1, [late])
    fill(0, late, mine, half_rows)
    core_start(0, [late], 1)

    row_i(1).wait_recv()
    fill_both(first)
    core_start(1, most, 1)
    core_start(1, [late], 1)
    core_end(0, [late], 1)
    x_wait(0, [late])
    x_add(0, [late], 0, rows)
    lean(0, cols[3], 1)
    x_wait(1, most)
    core_end(1, most, 1)
    x_add(1, most, 0, T, add=False)
    x_add(1, most, T, lo - T)
    z_start(1, cols[2])
    z_start(1, c ^ 1)
    core_end(1, [late], 1)
    x_wait(1, [late])
    x_add(1, [late], 0, T, add=False)
    x_add(1, [late], T, lo - T)
    z_start(1, cols[3])

    row_i(2).wait_recv()
    fill_both(middle)
    core_start(1, most, 2)
    core_start(1, [late], 2)
    def finish():
        row_i(3).wait_recv()
        fill_both(final)
        for dc in range(C):
            s = c ^ (C - 1 - dc)
            for i in range(2):
                remote(last.at[i, s], last_buf.at[core, c], lsend, lrecv, row=o, col=s, layer=2 * x + i).start()

    @pl.when(core == 1)
    def _():
        finish()

    core_end(1, most, 2)
    x_add(1, most, lo, rows - lo)
    hi_start(most)
    core_end(1, [late], 2)
    x_add(1, [late], lo, rows - lo)
    hi_start([late])

    @pl.when(core == 0)
    def _():
        finish()

    across(0, cols[3], 1)
    landed(z_buf.at[1, 0, pl.ds(0, lo)], wrecv.at[1, 0])
    y_sum = acc[1, c, at(l * rows, lo)] + z_buf[1, 0, :lo]
    landed(z_buf.at[1, pl.ds(1, 2), pl.ds(0, lo)], wrecv.at[1, 1])
    y_out[...] = y_sum + z_buf[1, 1, :lo] + z_buf[1, 2, :lo]

    remote(y_out, y_buf, ysend, yrecv, row=o).start()

    for n, (src, dst) in enumerate(((b_ref, bare), (rg_ref, gap_r), (cg_ref, gap_c))):
        pltpu.make_async_copy(src, dst, gsem.at[n]).wait()
    gap[...] = jnp.broadcast_to(gap_r[...], (N, rows)).T + gap_c[...]
    landed(a_x, asend)
    landed(az.at[pl.ds(0, m + 1)], zsend)
    landed(i_s, isend)
    landed(acc.at[0, :, pl.ds(0, M - T)], csend)
    landed(acc.at[0, :, pl.ds(0, half_rows)], xsend)

    landed(z_buf.at[0, 0], wrecv.at[0, 0])
    o_ref[...] = bare[...].astype(jnp.float32) + acc[0, c, at(l * rows, rows)] + z_buf[0, 0]

    landed(z_buf.at[0, 0], wrecv.at[0, 1])

    @pl.when(outer)
    def _():
        o_ref[...] += z_buf[0, 1]

    @pl.when(inner)
    def _():
        o_ref[...] += z_buf[0, 2]

    landed(hi_buf, hrecv)
    high = o_ref[lo:]
    for s in range(C):
        high += hi_buf[s]
    o_ref[lo:] = high
    landed(last_buf, lrecv)
    tail = o_ref[:T]
    for i in range(2):
        for s in range(C):
            tail += last_buf[i, s]
    o_ref[:T] = tail
    landed(y_buf, yrecv)
    o_ref[:lo] += y_buf[...]
    o_ref[...] = o_ref[...] / gap[...]

    landed(acc.at[0, pl.ds(0, m), pl.ds(0, 3 * (rows + lo) // m)], wsend)
    landed(hi_buf, hsend)
    landed(last, lsend)
    landed(y_out, ysend)


def swift_call(R, C, L, integrals, amplitudes, coulomb, row_gap, col_gap):
    K, V, M = integrals.shape
    V_row, N = amplitudes.shape[1:]
    rows = M // L
    Kr = K // R
    m = C // R
    T = 8
    lo = rows * 2 // 3 // 8 * 8
    dma = pltpu.SemaphoreType.DMA
    f32, bf16 = jnp.float32, jnp.bfloat16
    anyspace = pl.BlockSpec(memory_space=pl.ANY)
    return pl.pallas_call(
        functools.partial(swift, R, C, L, T, lo),
        out_shape=pltpu.VMEM((rows, N), f32),
        in_specs=[anyspace] * 5,
        out_specs=pl.BlockSpec(memory_space=pltpu.VMEM),
        scratch_shapes=[
            pltpu.VMEM((rows, N), bf16), pltpu.VMEM((1, rows), f32), pltpu.VMEM((1, N), f32), pltpu.VMEM((rows, N), f32), dma((3,)),
            pltpu.VMEM((Kr, V_row, N), bf16),
            pltpu.VMEM((C, Kr, V, N), bf16),
            pltpu.VMEM((K, V, M), bf16),
            pltpu.VMEM((M, Kr * V), bf16),
            pltpu.VMEM((2, M, Kr * V), bf16),
            pltpu.VMEM((2, C, M, N), f32),
            pltpu.VMEM((2, C, T, N), f32),
            pltpu.VMEM((2, 2, C, rows, N), f32),
            pltpu.VMEM((2, C, rows, N), f32),
            pltpu.VMEM((2, rows, N), f32),
            pltpu.VMEM((2, C - 1, rows, N), f32),
            pltpu.VMEM((lo, N), f32),
            pltpu.VMEM((lo, N), f32),
            pltpu.VMEM((2, C, T, N), f32),
            pltpu.VMEM((C, rows - lo, N), f32),
            dma, dma((Kr,)),
            dma, dma((Kr + m - 1,)),
            dma, dma((4,)),
            dma, dma((C,)),
            dma, dma((2, 2, 3)),
            dma, dma((2, 2)),
            dma, dma((2,)), dma((2, 2)),
            dma, dma,
            dma, dma,
            dma, dma,
            pltpu.SemaphoreType.REGULAR((2, C - 2)),
        ],
        compiler_params=pltpu.CompilerParams(collective_id=0, has_side_effects=True),
    )(integrals, amplitudes, coulomb, row_gap[None, :], col_gap[None, :])


def local(R, C, L, integrals, amplitudes, coulomb, row_gap, col_gap):
    K, V, M = integrals.shape
    N = amplitudes.shape[2]
    swift_fits = (R, C, L) == (2, 4, 4) and K % 16 == 0 and M % (16 * L) == 0 and V % 128 == 0 and N % 128 == 0
    if swift_fits:
        return swift_call(R, C, L, integrals, amplitudes, coulomb, row_gap, col_gap)
    own_rows = general_call(R, C, L, integrals, amplitudes)
    gap_sum = row_gap[:, None] + col_gap[None, :]
    return (coulomb.astype(jnp.float32) + own_rows) / gap_sum


def solution(mesh):
    R, C, L = (mesh.shape[a] for a in ("row", "col", "layer"))
    placed = (
        P("layer", "col", "row"),
        P("layer", "row", "col"),
        P(("row", "layer"), "col"),
        P(("row", "layer")),
        P("col"),
    )
    return jax.shard_map(
        functools.partial(local, R, C, L), mesh=mesh, in_specs=placed, out_specs=P(("row", "layer"), "col"),
        check_vma=False,
    )
```
